256 devices in a mesh: seq: 64 (over z, y, core), head: 4 (over x).
Axes of the slice: x: 4, y: 4, z: 8, core: 2. Of those that a mesh axis runs over, the one named last changes fastest.
Arguments:
- queries: bfloat16 [8192, 16, 128], P('seq', 'head'), may hold values from -6 to 6
- keys: bfloat16 [8192, 2, 16, 128], P('seq', None, 'head'), may hold values from -6 to 6
- values: bfloat16 [8192, 2, 16, 128], P('seq', None, 'head'), may hold values from -6 to 6
- betas: float32 [8192, 2, 16], P('seq', None, 'head'), may hold values from 0.5 to 2, as said below
- gain: float32 [128], replicated, may hold values from 0.1 to 1.9
- out_grad: bfloat16 [8192, 16, 128], P('seq', 'head'), may hold values from -6 to 6
Outputs:
- normed_out: bfloat16 [8192, 16, 128], P('seq', 'head')
- query_grad: bfloat16 [8192, 16, 128], P('seq', 'head')
- key_grad: bfloat16 [8192, 2, 16, 128], P('seq', None, 'head')
- value_grad: bfloat16 [8192, 2, 16, 128], P('seq', None, 'head')
- beta_grad: float32 [8192, 2, 16], P('seq', None, 'head')
- gain_grad: float32 [128], replicated
The draws below stay inside these ranges and needn't reach their ends.
Inputs may be any that keep to these rules, and one draw needn't show every extreme that they name: `betas`: every step size lies strictly between 0 and 2.
All inputs are finite; a program needn't handle non-finite values.
Results may differ from the reference program's by a relative error of at most 0.003.
Values sent between devices are 32-bit elements; how exact they have to be, the bound alone decides.
A program may use at most 128 MiB of HBM per device.

```python
import math
import jax
import jax.numpy as jnp
from jax import lax

HEADS = 16
DK = 128
DV = 128
STEPS = 2
TOKENS = 8192


def draw_betas(key, part):
    key_slow, key_rate, key_jitter, key_fast = jax.random.split(key, 4)
    slow_share = 0.5
    slow_heads = jax.random.uniform(key_slow, (HEADS,), jnp.float32) < slow_share
    slow_rates = jnp.exp(jax.random.uniform(key_rate, (HEADS,), jnp.float32, minval=math.log(0.05), maxval=0.0))
    jitter = jax.random.uniform(key_jitter, (TOKENS, STEPS, HEADS), jnp.float32, minval=0.5, maxval=1.5)
    slow_beta = 2.0 - slow_rates * jitter * (DK / (2.0 * TOKENS))
    fast_beta = jax.random.uniform(key_fast, (TOKENS, STEPS, HEADS), jnp.float32, minval=0.5, maxval=1.5)
    return jnp.where(slow_heads, slow_beta, fast_beta).astype(jnp.float32)


def shard_levels(own_key, shape, cuts, least, largest):
    def one(position, blocks):
        draws = jax.random.uniform(jax.random.fold_in(jax.random.fold_in(own_key, 6), position), (blocks,), jnp.float32, least / len(cuts), largest / len(cuts))
        return jnp.repeat(jnp.exp(draws), shape[position] // blocks).reshape((-1,) + (1,) * (len(shape) - position - 1))

    level = one(*cuts[0])
    for cut in cuts[1:]:
        level = level * one(*cut)
    return level


def gaussian(own_key, shape, deviation, reach, shards=(), held_as=jnp.bfloat16):
    result = jax.random.normal(own_key, shape, jnp.float32) * deviation
    if len(shards) > 0:
        result = shard_levels(own_key, shape, shards, -0.22, 0.18) * result
    return jnp.clip(result, min=-reach, max=reach).astype(held_as)


def setup_inputs(seed: int = 0) -> dict:
    arg_keys = jax.random.split(jax.random.key(seed), 7)
    queries = gaussian(arg_keys[0], (TOKENS, HEADS, DK), 1.0, 6.0, ((0, 64), (1, 4)))
    keys = gaussian(arg_keys[1], (TOKENS, STEPS, HEADS, DK), 1.0, 6.0, ((0, 64), (2, 4)))
    values = gaussian(arg_keys[2], (TOKENS, STEPS, HEADS, DV), 1.0, 6.0, ((0, 64), (2, 4)))
    betas = draw_betas(jax.random.fold_in(arg_keys[6], 71), 0)
    gain = jnp.clip(1.0 + 0.18 * jax.random.normal(arg_keys[4], (DV,), jnp.float32), 0.1, 1.9)
    out_grad = gaussian(arg_keys[5], (TOKENS, HEADS, DV), 1.0, 6.0, ((0, 64), (1, 4)))
    return {"queries": queries, "keys": keys, "values": values, "betas": betas, "gain": gain, "out_grad": out_grad}


EPS = 1e-06
HIGH_ACCURACY = lax.Precision.HIGHEST

def unit_rows(vectors):
    return vectors * lax.rsqrt(lax.optimization_barrier(jnp.sum(vectors * vectors, axis=-1, keepdims=True)) + EPS)

def recurrence(queries, keys, values, betas, gain):
    q_unit = unit_rows(queries)
    k_unit = unit_rows(keys)
    length = q_unit.shape[0]
    block_len = math.gcd(128, length)
    block_count = length // block_len
    q_blocks = q_unit.reshape(block_count, block_len, HEADS, DK)
    k_blocks = k_unit.reshape(block_count, block_len, STEPS, HEADS, DK)
    v_blocks = values.reshape(block_count, block_len, STEPS, HEADS, DV)
    b_blocks = betas.reshape(block_count, block_len, STEPS, HEADS)

    def token_step(memory_matrix, token_items):
        current_query, current_key, current_value, beta_now = token_items
        for reflection_step in range(STEPS):
            error_vector = current_value[reflection_step] - jnp.einsum('rdf,rd->rf', memory_matrix, current_key[reflection_step], precision=HIGH_ACCURACY)
            memory_matrix = memory_matrix + beta_now[reflection_step][:, None, None] * current_key[reflection_step][:, :, None] * error_vector[:, None, :]
        state_readout = jnp.einsum('rdf,rd->rf', memory_matrix, current_query, precision=HIGH_ACCURACY)
        return (memory_matrix, state_readout)

    def block_step(memory_matrix, block_items):
        return lax.scan(token_step, memory_matrix, block_items)
    block_step = jax.checkpoint(block_step)
    initial = jnp.zeros((HEADS, DK, DV), jnp.float32)
    _, readouts = lax.scan(block_step, initial, (q_blocks, k_blocks, v_blocks, b_blocks))
    readouts = readouts.reshape(length, HEADS, DV)
    inv_rms = lax.rsqrt(lax.optimization_barrier(jnp.mean(readouts * readouts, axis=-1, keepdims=True)) + EPS)
    return gain * (readouts * inv_rms)

def reference(queries, keys, values, betas, gain, out_grad):
    inputs = (queries.astype(jnp.float32), keys.astype(jnp.float32), values.astype(jnp.float32), betas, gain)
    normed, pullback = jax.vjp(recurrence, *inputs)
    gradients = pullback(out_grad.astype(jnp.float32))
    return (normed.astype(jnp.bfloat16), gradients[0].astype(jnp.bfloat16), gradients[1].astype(jnp.bfloat16), gradients[2].astype(jnp.bfloat16), gradients[3], gradients[4])
```

```python
import functools

import jax
import jax.numpy as jnp
from jax import lax
from jax.experimental import pallas as pl
from jax.experimental.pallas import tpu as pltpu
from jax.sharding import PartitionSpec as P

EPS = 1e-06
F32 = jnp.float32
BF16 = jnp.bfloat16
MESH = pl.DeviceIdType.MESH
NY = 4
NZ = 8
NC = 2


def split(x):
    hi = x.astype(BF16)
    lo = (x - hi.astype(F32)).astype(BF16)
    return hi, lo


def dot(a, b, dims):
    return lax.dot_general(a, b, (dims, ((), ())), preferred_element_type=F32)


def mm(a, b, ca=1, cb=0):
    ah, al = split(a)
    bh, bl = split(b)
    left = jnp.concatenate([ah, al, ah], axis=ca)
    right = jnp.concatenate([bh, bh, bl], axis=cb)
    return dot(left, right, ((ca,), (cb,)))


def iotas(rows, cols):
    return (
        lax.broadcasted_iota(jnp.int32, (rows, cols), 0),
        lax.broadcasted_iota(jnp.int32, (rows, cols), 1),
    )


def unit_pullback(d_unit, unit, inverse):
    return (d_unit - unit * jnp.sum(unit * d_unit, axis=-1, keepdims=True)) * inverse


def kernel(
    q_ref, k_ref, v_ref, b_ref, g_ref, do_ref,
    out_ref, dq_ref, dk_ref, dv_ref, db_ref, dg_ref,
    ku_s, qu_s, rk_s, rq_s, n_s, w_s, u_s, sc_s, r_s, ol_s, p_s, adj_s,
    ab_s, pair_s, comp_s, own_s, phi_s, beta_s, zab_s, za_s, sout_s, sin_s, s1_s,
    aown_s, phi0_s, theta_s, psi_s, c_s, cpair_s, cc_s, cown_s, crow_s, zc_s, gam_s, dsend_s, dout_s, d0_s,
    gpart_s, grow_s, gz_s, gx_s, gsum_s,
    send_sem, pair_sem, own_sem, zab_sem, za_sem, sin_sem, aown_sem, cpair_sem, cown_sem, zc_sem, dout_sem,
    gsend_sem, grow_sem, gz_sem, gx_sem,
):
    heads = q_ref.shape[1]
    tok = q_ref.shape[0]
    steps = k_ref.shape[0]
    dim = q_ref.shape[2]
    seq = lax.axis_index("seq")
    xpos = lax.axis_index("head")
    z = seq // (NY * NC)
    y = (seq // NC) % NY
    c = seq % NC

    def dev(zz, yy, cc):
        return {"seq": zz * (NY * NC) + yy * NC + cc}

    barrier = pltpu.get_barrier_semaphore()
    count = 0
    for dy in range(NY):
        for dc in range(NC):
            if dy or dc:
                pl.semaphore_signal(
                    barrier, inc=1, device_id=dev(z, (y + dy) % NY, (c + dc) % NC), device_id_type=MESH
                )
                count += 1
    for dz in range(1, NZ):
        for dc in range(NC):
            pl.semaphore_signal(
                barrier, inc=1, device_id=dev((z + dz) % NZ, y, (c + dc) % NC), device_id_type=MESH
            )
            count += 1
    for dx in range(1, 4):
        pl.semaphore_signal(
            barrier, inc=1, device_id={"head": (xpos + dx) % 4}, device_id_type=MESH
        )
        count += 1

    def remote(src, dst, ssem, rsem, target):
        return pltpu.make_async_remote_copy(
            src_ref=src, dst_ref=dst, send_sem=ssem, recv_sem=rsem, device_id=target, device_id_type=MESH
        )

    def arrived(dst, rsem):
        pltpu.make_async_copy(dst, dst, rsem).wait()

    row_i, col_i = iotas(steps, steps)
    tok_i, step_i = iotas(tok, steps)
    visible = step_i <= 2 * tok_i + 1
    eye = (row_i == col_i).astype(F32)
    eye_dim = eye[:dim, :dim]

    for dlt in range(1, NZ):
        @pl.when(z < dlt)
        def _():
            zab_s[dlt - 1] = jnp.zeros((2, dim, dim), F32)

        @pl.when(z + dlt >= NZ)
        def _():
            za_s[dlt - 1] = jnp.zeros((dim, dim), F32)
            zc_s[dlt - 1] = jnp.zeros((dim, dim), F32)

    for h in range(heads):
        q = q_ref[:, h, :].astype(F32)
        k = k_ref[:, h, :].astype(F32)
        v = v_ref[:, h, :].astype(F32)
        b = b_ref[:, h:h + 1]
        rq = lax.rsqrt(jnp.sum(q * q, axis=-1, keepdims=True) + EPS)
        rk = lax.rsqrt(jnp.sum(k * k, axis=-1, keepdims=True) + EPS)
        qu = q * rq
        ku = k * rk
        gram = mm(ku, ku, 1, 1)
        low = jnp.where(col_i < row_i, gram * b, 0.0)
        inv = eye - jnp.where(row_i // 2 == col_i // 2, low, 0.0)
        size = 2
        while size < steps:
            band = (row_i // (2 * size) == col_i // (2 * size)) & (row_i // size != col_i // size)
            inv = inv - mm(inv, mm(jnp.where(band, low, 0.0), inv))
            size *= 2
        wu = mm(inv, jnp.concatenate([b * ku, b * v], axis=1))
        ab = mm(ku, wu, 0, 0)
        ab_s[h, 0] = eye_dim - ab[:, :dim]
        ab_s[h, 1] = ab[:, dim:]
        sc = jnp.where(visible, mm(qu, ku, 1, 1), 0.0)
        ro = mm(sc, wu)
        ku_s[h] = ku
        qu_s[h] = qu
        rk_s[h] = rk
        rq_s[h] = rq
        n_s[h] = inv
        w_s[h] = wu[:, :dim]
        u_s[h] = wu[:, dim:]
        sc_s[h] = sc
        r_s[h] = qu - ro[:, :dim]
        ol_s[h] = ro[:, dim:]

    pl.semaphore_wait(barrier, count)

    other = 1 - c
    pair = dev(z, y, other)
    send = {}
    for j in range(2):
        send["pair", j] = remote(
            ab_s.at[2 * other + j], pair_s.at[j], send_sem.at[j], pair_sem.at[j], pair
        )
        send["pair", j].start()
    for j in range(2):
        arrived(pair_s.at[j], pair_sem.at[j])
        mine = ab_s[2 * c + j]
        theirs = pair_s[j]
        first = jnp.where(c == 0, mine, theirs)
        second = jnp.where(c == 0, theirs, mine)
        both = mm(second[0], jnp.concatenate([first[0], first[1]], axis=1))
        comp_s[j, 0] = both[:, :dim]
        comp_s[j, 1] = both[:, dim:] + second[1]
        head = 2 * c + j
        here = (c == 1) & (y == head)

        @pl.when(here)
        def _():
            pltpu.make_async_copy(comp_s.at[j], own_s.at[y], own_sem.at[y]).start()

        @pl.when(jnp.logical_not(here))
        def _():
            remote(comp_s.at[j], own_s.at[y], send_sem.at[2 + j], own_sem.at[y], dev(z, head, 1)).start()

    @pl.when(c == 1)
    def _():
        low_core = dev(z, y, 0)
        arrived(own_s.at[0], own_sem.at[0])
        x = jnp.concatenate([own_s[0, 0], own_s[0, 1]], axis=1)
        phi_s[0] = x[:, :dim]
        beta_s[0] = x[:, dim:]
        for i in range(1, NY):
            arrived(own_s.at[i], own_sem.at[i])
            x = mm(own_s[i, 0], x)
            x = jnp.concatenate([x[:, :dim], x[:, dim:] + own_s[i, 1]], axis=1)
            phi_s[i] = x[:, :dim]
            beta_s[i] = x[:, dim:]
        comp_row = own_s.at[0]
        comp_row[0] = x[:, :dim]
        comp_row[1] = x[:, dim:]
        for dlt in range(NZ - 1, 0, -1):
            @pl.when(z + dlt < NZ)
            def _():
                remote(
                    own_s.at[0], zab_s.at[dlt - 1], send_sem.at[4 + dlt], zab_sem.at[dlt - 1],
                    dev(z + dlt, y, 1),
                ).start()
        for dlt in range(1, NZ):
            @pl.when(z >= dlt)
            def _():
                remote(
                    phi_s.at[NY - 1], za_s.at[dlt - 1], send_sem.at[12 + dlt], za_sem.at[dlt - 1],
                    dev(z - dlt, y, 0),
                ).start()
        for i in range(1, NY):
            remote(own_s.at[i, 0], aown_s.at[i], send_sem.at[20 + i], aown_sem.at[i], low_core).start()
            remote(phi_s.at[i - 1], phi0_s.at[i], send_sem.at[24 + i], aown_sem.at[NY + i], low_core).start()
        state = jnp.zeros((dim, dim), F32)
        for dlt in range(NZ - 1, 0, -1):
            @pl.when(z >= dlt)
            def _():
                arrived(zab_s.at[dlt - 1], zab_sem.at[dlt - 1])

            if dlt == NZ - 1:
                state = zab_s[dlt - 1, 1]
            else:
                state = mm(zab_s[dlt - 1, 0], state) + zab_s[dlt - 1, 1]
        sout_s[0] = state
        later = mm(jnp.concatenate([phi_s[i] for i in range(NY - 1)], axis=0), state)
        for i in range(1, NY):
            sout_s[i] = later[(i - 1) * dim:i * dim] + beta_s[i - 1]
        for i in range(NY):
            remote(sout_s.at[i], sin_s.at[y], send_sem.at[28 + i], sin_sem.at[y], dev(z, i, 0)).start()
        for h in range(heads):
            arrived(sin_s.at[h], sin_sem.at[h])

    @pl.when(c == 0)
    def _():
        for i in range(1, NY):
            arrived(aown_s.at[i], aown_sem.at[i])
            arrived(phi0_s.at[i], aown_sem.at[NY + i])
        psi_s[NY - 2] = aown_s[NY - 1]
        for i in range(NY - 3, -1, -1):
            psi_s[i] = mm(psi_s[i + 1], aown_s[i + 1])
        theta_s[0] = eye_dim
        for dlt in range(1, NZ - 1):
            @pl.when(z + dlt < NZ)
            def _():
                arrived(za_s.at[dlt - 1], za_sem.at[dlt - 1])

            theta_s[dlt] = za_s[0] if dlt == 1 else mm(za_s[dlt - 1], theta_s[dlt - 1])

        @pl.when(z + NZ - 1 < NZ)
        def _():
            arrived(za_s.at[NZ - 2], za_sem.at[NZ - 2])

        for h in range(heads):
            arrived(sin_s.at[h], sin_sem.at[h])
            s1_s[h] = mm(ab_s[h, 0], sin_s[h]) + ab_s[h, 1]
            remote(s1_s.at[h], sin_s.at[h], send_sem.at[28 + h], sin_sem.at[h], pair).start()

    gain = g_ref[...]
    gain_part = jnp.zeros((1, dim), F32)
    for h in range(heads):
        state = sin_s[h]
        both = mm(jnp.concatenate([r_s[h], w_s[h]], axis=0), state)
        o = ol_s[h] + both[:tok]
        p_s[h] = u_s[h] - both[tok:]
        inv_rms = lax.rsqrt(jnp.mean(o * o, axis=-1, keepdims=True) + EPS)
        normal = o * inv_rms
        grad = do_ref[:, h, :].astype(F32)
        out_ref[:, h, :] = (gain * normal).astype(BF16)
        gain_part = gain_part + jnp.sum(grad * normal, axis=0, keepdims=True)
        scaled = grad * gain
        adj = inv_rms * (scaled - normal * jnp.mean(scaled * normal, axis=-1, keepdims=True))
        adj_s[h] = adj
        c_s[h] = mm(r_s[h], adj, 0, 0)

        @pl.when(c == 1)
        def _():
            remote(c_s.at[h], cpair_s.at[h], send_sem.at[32 + h], cpair_sem.at[h], pair).start()

    gpart_s[...] = jnp.broadcast_to(gain_part, (8, dim))
    me8 = y * NC + c
    n_g = 0
    gsends = []
    for d in range(1, NY * NC):
        to = (me8 + d) % (NY * NC)
        gsends.append(remote(
            gpart_s, grow_s.at[me8], gsend_sem.at[n_g], grow_sem.at[d - 1], dev(z, to // NC, to % NC)))
        gsends[-1].start()
        n_g += 1
    grow_s[me8] = gpart_s[...]

    @pl.when(c == 0)
    def _():
        for h in range(heads):
            arrived(cpair_s.at[h], cpair_sem.at[h])
            cc_s[h] = mm(ab_s[h, 0], cpair_s[h], 0, 0) + c_s[h]

            @pl.when(y == h)
            def _():
                pltpu.make_async_copy(cc_s.at[h], cown_s.at[h], cown_sem.at[h]).start()

            @pl.when(y != h)
            def _():
                remote(cc_s.at[h], cown_s.at[y], send_sem.at[32 + h], cown_sem.at[y], dev(z, h, 0)).start()
        for i in range(NY):
            arrived(cown_s.at[i], cown_sem.at[i])
        left = jnp.concatenate([phi0_s[i] for i in range(1, NY)], axis=0)
        right = jnp.concatenate([cown_s[i] for i in range(1, NY)], axis=0)
        crow_s[...] = cown_s[0] + mm(left, right, 0, 0)
        for dlt in range(NZ - 1, 0, -1):
            @pl.when(z >= dlt)
            def _():
                remote(
                    crow_s, zc_s.at[dlt - 1], send_sem.at[4 + dlt], zc_sem.at[dlt - 1], dev(z - dlt, y, 0)
                ).start()
        gam_s[NY - 2] = cown_s[NY - 1]
        for i in range(NY - 3, -1, -1):
            gam_s[i] = mm(aown_s[i + 1], gam_s[i + 1], 0, 0) + cown_s[i + 1]
        for dlt in range(NZ - 1, 0, -1):
            @pl.when(z + dlt < NZ)
            def _():
                arrived(zc_s.at[dlt - 1], zc_sem.at[dlt - 1])
        left = jnp.concatenate([theta_s[i] for i in range(1, NZ - 1)], axis=0)
        right = jnp.concatenate([zc_s[i] for i in range(1, NZ - 1)], axis=0)
        d_row = zc_s[0] + mm(left, right, 0, 0)
        dsend_s[NY - 1] = d_row
        for i in range(NY - 1):
            dsend_s[i] = mm(psi_s[i], d_row, 0, 0) + gam_s[i]
        for i in range(NY):
            remote(dsend_s.at[i], dout_s.at[y], send_sem.at[12 + i], dout_sem.at[y], dev(z, i, 1)).start()
        for h in range(heads):
            arrived(dout_s.at[h], dout_sem.at[h])

    @pl.when(c == 1)
    def _():
        for h in range(heads):
            arrived(dout_s.at[h], dout_sem.at[h])
            d0_s[h] = mm(ab_s[h, 0], dout_s[h], 0, 0) + c_s[h]
            remote(d0_s.at[h], dout_s.at[h], send_sem.at[36 + h], dout_sem.at[h], pair).start()

    for d in range(1, NY * NC):
        fr = (me8 + NY * NC - d) % (NY * NC)
        arrived(grow_s.at[fr], grow_sem.at[d - 1])
    gsum_s[0] = jnp.sum(grow_s[...], axis=0)
    for d in range(1, NZ):
        gsends.append(remote(
            gsum_s.at[0], gz_s.at[z], gsend_sem.at[n_g], gz_sem.at[d - 1], dev((z + d) % NZ, y, c)))
        gsends[-1].start()
        n_g += 1
    gz_s[z] = gsum_s[0]

    lane = lax.broadcasted_iota(jnp.int32, (steps, heads), 1)
    db_all = jnp.zeros((steps, heads), F32)
    for h in range(heads):
        ku = ku_s[h]
        qu = qu_s[h]
        p = p_s[h]
        adj = adj_s[h]
        b = b_ref[:, h:h + 1]
        state = sin_s[h]
        d_out = dout_s[h]
        m_do = jnp.where(visible, mm(adj, p, 1, 1), 0.0)
        dq = mm(adj, state, 1, 1) + mm(m_do, ku)
        dp = mm(sc_s[h], adj, 0, 0) + mm(ku, d_out)
        gm = mm(n_s[h], dp, 0, 0)
        dv = b * gm
        db = jnp.sum(gm * p, axis=-1, keepdims=True) / b
        hm = jnp.where(col_i < row_i, mm(dv, p, 1, 1), 0.0)
        dk = mm(m_do, qu, 0, 0) + mm(p, d_out, 1, 1) - mm(dv, state, 1, 1) - mm(hm, ku) - mm(hm, ku, 0, 0)
        dq_ref[:, h, :] = unit_pullback(dq, qu, rq_s[h]).astype(BF16)
        dk_ref[:, h, :] = unit_pullback(dk, ku, rk_s[h]).astype(BF16)
        dv_ref[:, h, :] = dv.astype(BF16)
        db_all = db_all + jnp.where(lane == h, db, 0.0)
    db_ref[...] = db_all

    for d in range(1, NZ):
        arrived(gz_s.at[(z + NZ - d) % NZ], gz_sem.at[d - 1])
    gsum_s[1] = jnp.sum(gz_s[...], axis=0)
    for d in range(1, 4):
        gsends.append(remote(
            gsum_s.at[1], gx_s.at[xpos], gsend_sem.at[n_g], gx_sem.at[d - 1], {"head": (xpos + d) % 4}))
        gsends[-1].start()
        n_g += 1
    gx_s[xpos] = gsum_s[1]
    for d in range(1, 4):
        arrived(gx_s.at[(xpos + 4 - d) % 4], gx_sem.at[d - 1])
    dg_ref[...] = jnp.sum(gx_s[...], axis=0)[0:1]

    for j in range(2):
        send["pair", j].wait_send()
        head = 2 * c + j

        @pl.when(jnp.logical_not((c == 1) & (y == head)))
        def _():
            remote(comp_s.at[j], own_s.at[y], send_sem.at[2 + j], own_sem.at[y], dev(z, head, 1)).wait_send()

    def left(src, sem):
        remote(src, src, sem, sem, pair).wait_send()

    @pl.when(c == 1)
    def _():
        for dlt in range(1, NZ):
            @pl.when(z + dlt < NZ)
            def _():
                left(own_s.at[0], send_sem.at[4 + dlt])

            @pl.when(z >= dlt)
            def _():
                left(phi_s.at[NY - 1], send_sem.at[12 + dlt])
        for i in range(1, NY):
            left(own_s.at[i, 0], send_sem.at[20 + i])
            left(phi_s.at[i - 1], send_sem.at[24 + i])
        for i in range(NY):
            left(sout_s.at[i], send_sem.at[28 + i])
            left(c_s.at[i], send_sem.at[32 + i])
            left(d0_s.at[i], send_sem.at[36 + i])

    @pl.when(c == 0)
    def _():
        for h in range(heads):
            left(s1_s.at[h], send_sem.at[28 + h])

            @pl.when(y != h)
            def _():
                left(cc_s.at[h], send_sem.at[32 + h])
        for dlt in range(1, NZ):
            @pl.when(z >= dlt)
            def _():
                left(crow_s, send_sem.at[4 + dlt])
        for i in range(NY):
            left(dsend_s.at[i], send_sem.at[12 + i])
    for copy in gsends:
        copy.wait_send()


def local(queries, keys, values, betas, gain, out_grad):
    tok, heads, dim = queries.shape
    steps = tok * keys.shape[1]
    f = lambda *s: pltpu.VMEM(s, F32)
    dma = pltpu.SemaphoreType.DMA
    vmem = pl.BlockSpec(memory_space=pltpu.VMEM)
    scratch = [
        f(heads, steps, dim), f(heads, tok, dim), f(heads, steps, 1), f(heads, tok, 1),
        f(heads, steps, steps), f(heads, steps, dim), f(heads, steps, dim), f(heads, tok, steps),
        f(heads, tok, dim), f(heads, tok, dim), f(heads, steps, dim), f(heads, tok, dim),
        f(heads, 2, dim, dim), f(2, 2, dim, dim), f(2, 2, dim, dim), f(NY, 2, dim, dim),
        f(NY, dim, dim), f(NY, dim, dim), f(NZ - 1, 2, dim, dim), f(NZ - 1, dim, dim),
        f(NY, dim, dim), f(heads, dim, dim), f(heads, dim, dim),
        f(NY, dim, dim), f(NY, dim, dim), f(NZ - 1, dim, dim), f(NY - 1, dim, dim), f(heads, dim, dim),
        f(heads, dim, dim), f(heads, dim, dim), f(NY, dim, dim), f(dim, dim), f(NZ - 1, dim, dim),
        f(NY - 1, dim, dim), f(NY, dim, dim), f(heads, dim, dim), f(heads, dim, dim),
        f(8, dim), f(NY * NC, 8, dim), f(NZ, 8, dim), f(4, 8, dim), f(2, 8, dim),
        dma((40,)), dma((2,)), dma((NY,)), dma((NZ - 1,)), dma((NZ - 1,)), dma((heads,)), dma((2 * NY,)),
        dma((heads,)), dma((NY,)), dma((NZ - 1,)), dma((heads,)),
        dma((24,)), dma((NY * NC - 1,)), dma((NZ - 1,)), dma((3,)),
    ]
    outs = pl.pallas_call(
        kernel,
        out_shape=(
            jax.ShapeDtypeStruct((tok, heads, dim), BF16),
            jax.ShapeDtypeStruct((tok, heads, dim), BF16),
            jax.ShapeDtypeStruct((steps, heads, dim), BF16),
            jax.ShapeDtypeStruct((steps, heads, dim), BF16),
            jax.ShapeDtypeStruct((steps, heads), F32),
            jax.ShapeDtypeStruct((1, dim), F32),
        ),
        in_specs=[vmem] * 6,
        out_specs=(vmem,) * 6,
        scratch_shapes=scratch,
        compiler_params=pltpu.CompilerParams(
            collective_id=0, has_side_effects=True, vmem_limit_bytes=60 * 1024 * 1024
        ),
        name="delta_product",
    )(
        queries,
        keys.reshape(steps, heads, dim),
        values.reshape(steps, heads, dim),
        betas.reshape(steps, heads),
        gain.reshape(1, dim),
        out_grad,
    )
    out, dq, dk, dv, db, dg = outs
    return (out, dq, dk.reshape(keys.shape), dv.reshape(values.shape), db.reshape(betas.shape), dg.reshape(dim))


def solution(mesh):
    return jax.shard_map(
        local,
        mesh=mesh,
        in_specs=(
            P("seq", "head", None),
            P("seq", None, "head", None),
            P("seq", None, "head", None),
            P("seq", None, "head"),
            P(),
            P("seq", "head", None),
        ),
        out_specs=(
            P("seq", "head", None),
            P("seq", "head", None),
            P("seq", None, "head", None),
            P("seq", None, "head", None),
            P("seq", None, "head"),
            P(),
        ),
        check_vma=False,
    )
```

```python
import functools

import jax
import jax.numpy as jnp
from jax import lax
from jax.experimental import pallas as pl
from jax.experimental.pallas import tpu as pltpu
from jax.sharding import PartitionSpec as P

EPS = 1e-06
F32 = jnp.float32
BF16 = jnp.bfloat16
MESH = pl.DeviceIdType.MESH
NY = 4
NZ = 8
NC = 2


def split(x):
    hi = x.astype(BF16)
    lo = (x - hi.astype(F32)).astype(BF16)
    return hi, lo


def dot(a, b, dims):
    return lax.dot_general(a, b, (dims, ((), ())), preferred_element_type=F32)


def mms(a, b, ca=1, cb=0):
    left = jnp.concatenate([a[0], a[1], a[0]], axis=ca)
    right = jnp.concatenate([b[0], b[0], b[1]], axis=cb)
    return dot(left, right, ((ca,), (cb,)))


def mm(a, b, ca=1, cb=0):
    return mms(split(a), split(b), ca, cb)


def iotas(rows, cols):
    return (
        lax.broadcasted_iota(jnp.int32, (rows, cols), 0),
        lax.broadcasted_iota(jnp.int32, (rows, cols), 1),
    )


def unit_pullback(d_unit, unit, inverse):
    return (d_unit - unit * jnp.sum(unit * d_unit, axis=-1, keepdims=True)) * inverse


def kernel(
    q_ref, k_ref, v_ref, b_ref, g_ref, do_ref,
    out_ref, dq_ref, dk_ref, dv_ref, db_ref, dg_ref,
    ku_s, qu_s, vf_s, dof_s, rk_s, rq_s, low_s, n_s, nt_s, nk_s, wu_s, sct_s, r_s, rt_s, ol_s, p_s, adj_s,
    g0_s, dk1_s, of_s, dq_s, dk_s, dvf_s,
    ab_s, pair_s, comp_s, own_s, phi_s, beta_s, zab_s, za_s, sout_s, sin_s, s1_s,
    aown_s, phi0_s, theta_s, psi_s, c_s, cpair_s, cc_s, cown_s, crow_s, zc_s, gam_s, dsend_s, dout_s, d0_s,
    gpart_s, grow_s, gz_s, gx_s, gsum_s,
    send_sem, pair_sem, own_sem, zab_sem, za_sem, sin_sem, aown_sem, cpair_sem, cown_sem, zc_sem, dout_sem,
    gsend_sem, grow_sem, gz_sem, gx_sem,
):
    steps, heads = b_ref.shape
    tok = q_ref.shape[0] // heads
    dim = q_ref.shape[1]
    seq = lax.axis_index("seq")
    xpos = lax.axis_index("head")
    z = seq // (NY * NC)
    y = (seq // NC) % NY
    c = seq % NC

    def dev(zz, yy, cc):
        return {"seq": zz * (NY * NC) + yy * NC + cc}

    barrier = pltpu.get_barrier_semaphore()
    count = 0
    for dy in range(NY):
        for dc in range(NC):
            if dy or dc:
                pl.semaphore_signal(
                    barrier, inc=1, device_id=dev(z, (y + dy) % NY, (c + dc) % NC), device_id_type=MESH
                )
                count += 1
    for dz in range(1, NZ):
        for dc in range(NC):
            pl.semaphore_signal(
                barrier, inc=1, device_id=dev((z + dz) % NZ, y, (c + dc) % NC), device_id_type=MESH
            )
            count += 1
    for dx in range(1, 4):
        pl.semaphore_signal(
            barrier, inc=1, device_id={"head": (xpos + dx) % 4}, device_id_type=MESH
        )
        count += 1

    def remote(src, dst, ssem, rsem, target):
        return pltpu.make_async_remote_copy(
            src_ref=src, dst_ref=dst, send_sem=ssem, recv_sem=rsem, device_id=target, device_id_type=MESH
        )

    def arrived(dst, rsem):
        pltpu.make_async_copy(dst, dst, rsem).wait()

    row_i, col_i = iotas(steps, steps)
    tok_i, step_i = iotas(tok, steps)
    visible = step_i <= 2 * tok_i + 1
    eye = (row_i == col_i).astype(F32)
    eye_dim = eye[:dim, :dim]

    for dlt in range(1, NZ):
        @pl.when(z < dlt)
        def _():
            zab_s[dlt - 1] = jnp.zeros((2, dim, dim), F32)

        @pl.when(z + dlt >= NZ)
        def _():
            za_s[dlt - 1] = jnp.zeros((dim, dim), F32)
            zc_s[dlt - 1] = jnp.zeros((dim, dim), F32)

    q = q_ref[...].astype(F32)
    k = k_ref[...].astype(F32)
    rq = lax.rsqrt(jnp.sum(q * q, axis=-1, keepdims=True) + EPS)
    rk = lax.rsqrt(jnp.sum(k * k, axis=-1, keepdims=True) + EPS)
    rq_s[...] = rq
    rk_s[...] = rk
    qu_s[...] = q * rq
    ku_s[...] = k * rk
    vf_s[...] = v_ref[...].astype(F32)
    dof_s[...] = do_ref[...].astype(F32)

    def of_head(ref, h, rows):
        return ref[pl.ds(h, rows, stride=heads), :]

    half = steps // 2
    base = 16
    blocks = half // base
    lane16 = lax.broadcasted_iota(jnp.int32, (base, half), 1) // base
    packed = []
    for h in range(heads):
        ku = of_head(ku_s, h, steps)
        b = b_ref[:, h:h + 1]
        low = jnp.where(col_i < row_i, mm(ku, ku, 1, 1) * b, 0.0)
        low_s[h] = low
        for part in range(2):
            tri = low[part * half:(part + 1) * half, part * half:(part + 1) * half]
            diag = jnp.zeros((base, half), F32)
            for i in range(blocks):
                diag = jnp.where(lane16 == i, tri[i * base:(i + 1) * base], diag)
            packed.append(diag)
    packed = jnp.concatenate(packed, axis=0)
    rows = packed.shape[0]
    lane = lax.broadcasted_iota(jnp.int32, (rows, half), 1)
    row = lax.broadcasted_iota(jnp.int32, (rows, half), 0)
    inv = jnp.where(row % base == lane % base, 1.0, 0.0)
    for step in range(base - 1):
        column = jnp.take_along_axis(packed, (lane // base) * base + step, axis=1)
        pivot = inv.reshape(rows // base, base, half)[:, step:step + 1, :]
        pivot = jnp.broadcast_to(pivot, (rows // base, base, half)).reshape(rows, half)
        inv = inv - column * pivot
    quads = [(h, part) for h in range(heads) for part in range(2)]
    for n, (h, part) in enumerate(quads):
        mine = inv[n * base:(n + 1) * base]
        n_s[h, part * half:(part + 1) * half, part * half:(part + 1) * half] = jnp.concatenate(
            [jnp.where(lane16 == i, mine, 0.0) for i in range(blocks)], axis=0
        )
        if part:
            n_s[h, 0:half, half:steps] = jnp.zeros((half, half), F32)
    sub_i, sub_j = row_i[:half, :half], col_i[:half, :half]
    size = base
    while size < half:
        band = (sub_i // (2 * size) == sub_j // (2 * size)) & (sub_i // size != sub_j // size)
        firsts = {}
        for h, part in quads:
            at = pl.ds(part * half, half)
            parts = split(n_s[h, at, at])
            firsts[h, part] = parts, mms(split(low_s[h, at, at]), parts)
        for h, part in quads:
            at = pl.ds(part * half, half)
            parts, first = firsts[h, part]
            n_s[h, at, at] = n_s[h, at, at] - jnp.where(band, mms(parts, split(first)), 0.0)
        size *= 2
    firsts = [mm(low_s[h, half:steps, 0:half], n_s[h, 0:half, 0:half]) for h in range(heads)]
    for h in range(heads):
        n_s[h, half:steps, 0:half] = -mm(n_s[h, half:steps, half:steps], firsts[h])
    for h in range(heads):
        ku = of_head(ku_s, h, steps)
        b = b_ref[:, h:h + 1]
        wu_s[h] = mm(n_s[h], jnp.concatenate([b * ku, b * of_head(vf_s, h, steps)], axis=1))
    for h in range(heads):
        ab = mm(of_head(ku_s, h, steps).T, wu_s[h])
        ab_s[h, 0] = eye_dim - ab[:, :dim]
        ab_s[h, 1] = ab[:, dim:]

    def fill_forward():
        for h in range(heads):
            ku = of_head(ku_s, h, steps)
            qu = of_head(qu_s, h, tok)
            sc = jnp.where(visible, mm(qu, ku, 1, 1), 0.0)
            ro = mm(sc, wu_s[h])
            r = qu - ro[:, :dim]
            r_s[h] = r
            rt_s[h] = r.T
            ol_s[h] = ro[:, dim:]
            sct_s[h] = sc.T
            nt = n_s[h].T
            nt_s[h] = nt
            nk_s[h] = mm(nt, ku)

    def fill_backward():
        for h in range(heads):
            ku = of_head(ku_s, h, steps)
            adj = adj_s[h]
            m_do = jnp.where(visible, mm(adj, p_s[h], 1, 1), 0.0)
            dq = mm(adj, sin_s[h], 1, 1) + mm(m_do, ku)
            dq_s[pl.ds(h, tok, stride=heads), :] = dq
            dk1_s[h] = mm(m_do.T, of_head(qu_s, h, tok))
            g0_s[h] = mm(nt_s[h], mm(sct_s[h], adj))

    pl.semaphore_wait(barrier, count)

    other = 1 - c
    pair = dev(z, y, other)
    send = {}
    for j in range(2):
        send["pair", j] = remote(
            ab_s.at[2 * other + j], pair_s.at[j], send_sem.at[j], pair_sem.at[j], pair
        )
        send["pair", j].start()
    for j in range(2):
        arrived(pair_s.at[j], pair_sem.at[j])
        mine = ab_s[2 * c + j]
        theirs = pair_s[j]
        first = jnp.where(c == 0, mine, theirs)
        second = jnp.where(c == 0, theirs, mine)
        both = mm(second[0], jnp.concatenate([first[0], first[1]], axis=1))
        comp_s[j, 0] = both[:, :dim]
        comp_s[j, 1] = both[:, dim:] + second[1]
        head = 2 * c + j
        here = (c == 1) & (y == head)

        @pl.when(here)
        def _():
            pltpu.make_async_copy(comp_s.at[j], own_s.at[y], own_sem.at[y]).start()

        @pl.when(jnp.logical_not(here))
        def _():
            remote(comp_s.at[j], own_s.at[y], send_sem.at[2 + j], own_sem.at[y], dev(z, head, 1)).start()

    @pl.when(c == 1)
    def _():
        low_core = dev(z, y, 0)
        arrived(own_s.at[0], own_sem.at[0])
        x = jnp.concatenate([own_s[0, 0], own_s[0, 1]], axis=1)
        phi_s[0] = x[:, :dim]
        beta_s[0] = x[:, dim:]
        for i in range(1, NY):
            arrived(own_s.at[i], own_sem.at[i])
            x = mm(own_s[i, 0], x)
            x = jnp.concatenate([x[:, :dim], x[:, dim:] + own_s[i, 1]], axis=1)
            phi_s[i] = x[:, :dim]
            beta_s[i] = x[:, dim:]
        comp_row = own_s.at[0]
        comp_row[0] = x[:, :dim]
        comp_row[1] = x[:, dim:]
        for dlt in range(NZ - 1, 0, -1):
            @pl.when(z + dlt < NZ)
            def _():
                remote(
                    own_s.at[0], zab_s.at[dlt - 1], send_sem.at[4 + dlt], zab_sem.at[dlt - 1],
                    dev(z + dlt, y, 1),
                ).start()
        for dlt in range(1, NZ):
            @pl.when(z >= dlt)
            def _():
                remote(
                    phi_s.at[NY - 1], za_s.at[dlt - 1], send_sem.at[12 + dlt], za_sem.at[dlt - 1],
                    dev(z - dlt, y, 0),
                ).start()
        for i in range(1, NY):
            remote(own_s.at[i, 0], aown_s.at[i], send_sem.at[20 + i], aown_sem.at[i], low_core).start()
            remote(phi_s.at[i - 1], phi0_s.at[i], send_sem.at[24 + i], aown_sem.at[NY + i], low_core).start()
        fill_forward()
        state = jnp.zeros((dim, dim), F32)
        for dlt in range(NZ - 1, 0, -1):
            @pl.when(z >= dlt)
            def _():
                arrived(zab_s.at[dlt - 1], zab_sem.at[dlt - 1])

            if dlt == NZ - 1:
                state = zab_s[dlt - 1, 1]
            else:
                state = mm(zab_s[dlt - 1, 0], state) + zab_s[dlt - 1, 1]
        sout_s[0] = state
        later = mm(jnp.concatenate([phi_s[i] for i in range(NY - 1)], axis=0), state)
        for i in range(1, NY):
            sout_s[i] = later[(i - 1) * dim:i * dim] + beta_s[i - 1]
        for i in range(NY):
            remote(sout_s.at[i], sin_s.at[y], send_sem.at[28 + i], sin_sem.at[y], dev(z, i, 0)).start()
        for h in range(heads):
            arrived(sin_s.at[h], sin_sem.at[h])

    @pl.when(c == 0)
    def _():
        fill_forward()
        for i in range(1, NY):
            arrived(aown_s.at[i], aown_sem.at[i])
            arrived(phi0_s.at[i], aown_sem.at[NY + i])
        psi_s[NY - 2] = aown_s[NY - 1]
        for i in range(NY - 3, -1, -1):
            psi_s[i] = mm(psi_s[i + 1], aown_s[i + 1])
        theta_s[0] = eye_dim
        for dlt in range(1, NZ - 1):
            @pl.when(z + dlt < NZ)
            def _():
                arrived(za_s.at[dlt - 1], za_sem.at[dlt - 1])

            theta_s[dlt] = za_s[0] if dlt == 1 else mm(za_s[dlt - 1], theta_s[dlt - 1])

        @pl.when(z + NZ - 1 < NZ)
        def _():
            arrived(za_s.at[NZ - 2], za_sem.at[NZ - 2])

        for h in range(heads):
            arrived(sin_s.at[h], sin_sem.at[h])
            s1_s[h] = mm(ab_s[h, 0], sin_s[h]) + ab_s[h, 1]
            remote(s1_s.at[h], sin_s.at[h], send_sem.at[28 + h], sin_sem.at[h], pair).start()

    gain = g_ref[...]
    gain_part = jnp.zeros((1, dim), F32)
    for h in range(heads):
        state = sin_s[h]
        both = mm(jnp.concatenate([r_s[h], wu_s[h, :, :dim]], axis=0), state)
        o = ol_s[h] + both[:tok]
        p_s[h] = wu_s[h, :, dim:] - both[tok:]
        inv_rms = lax.rsqrt(jnp.mean(o * o, axis=-1, keepdims=True) + EPS)
        normal = o * inv_rms
        grad = of_head(dof_s, h, tok)
        of_s[pl.ds(h, tok, stride=heads), :] = gain * normal
        gain_part = gain_part + jnp.sum(grad * normal, axis=0, keepdims=True)
        scaled = grad * gain
        adj = inv_rms * (scaled - normal * jnp.mean(scaled * normal, axis=-1, keepdims=True))
        adj_s[h] = adj
        c_s[h] = mm(rt_s[h], adj)

        @pl.when(c == 1)
        def _():
            remote(c_s.at[h], cpair_s.at[h], send_sem.at[32 + h], cpair_sem.at[h], pair).start()

    gpart_s[...] = jnp.broadcast_to(gain_part, (8, dim))
    me8 = y * NC + c
    n_g = 0
    gsends = []
    for d in range(1, NY * NC):
        to = (me8 + d) % (NY * NC)
        gsends.append(remote(
            gpart_s, grow_s.at[me8], gsend_sem.at[n_g], grow_sem.at[d - 1], dev(z, to // NC, to % NC)))
        gsends[-1].start()
        n_g += 1
    grow_s[me8] = gpart_s[...]

    def gain_along_z():
        for d in range(1, NY * NC):
            fr = (me8 + NY * NC - d) % (NY * NC)
            arrived(grow_s.at[fr], grow_sem.at[d - 1])
        gsum_s[0] = jnp.sum(grow_s[...], axis=0)
        for d in range(1, NZ):
            gz_copy(d).start()
        gz_s[z] = gsum_s[0]

    def gz_copy(d):
        return remote(
            gsum_s.at[0], gz_s.at[z], gsend_sem.at[6 + d], gz_sem.at[d - 1], dev((z + d) % NZ, y, c)
        )

    def gx_copy(d):
        return remote(
            gsum_s.at[1], gx_s.at[xpos], gsend_sem.at[13 + d], gx_sem.at[d - 1], {"head": (xpos + d) % 4}
        )

    @pl.when(c == 0)
    def _():
        for h in range(heads):
            arrived(cpair_s.at[h], cpair_sem.at[h])
            cc_s[h] = mm(ab_s[h, 0], cpair_s[h], 0, 0) + c_s[h]

            @pl.when(y == h)
            def _():
                pltpu.make_async_copy(cc_s.at[h], cown_s.at[h], cown_sem.at[h]).start()

            @pl.when(y != h)
            def _():
                remote(cc_s.at[h], cown_s.at[y], send_sem.at[32 + h], cown_sem.at[y], dev(z, h, 0)).start()
        for i in range(NY):
            arrived(cown_s.at[i], cown_sem.at[i])
        left = jnp.concatenate([phi0_s[i] for i in range(1, NY)], axis=0)
        right = jnp.concatenate([cown_s[i] for i in range(1, NY)], axis=0)
        crow_s[...] = cown_s[0] + mm(left, right, 0, 0)
        for dlt in range(NZ - 1, 0, -1):
            @pl.when(z >= dlt)
            def _():
                remote(
                    crow_s, zc_s.at[dlt - 1], send_sem.at[4 + dlt], zc_sem.at[dlt - 1], dev(z - dlt, y, 0)
                ).start()
        gam_s[NY - 2] = cown_s[NY - 1]
        for i in range(NY - 3, -1, -1):
            gam_s[i] = mm(aown_s[i + 1], gam_s[i + 1], 0, 0) + cown_s[i + 1]
        gain_along_z()
        fill_backward()
        for dlt in range(NZ - 1, 0, -1):
            @pl.when(z + dlt < NZ)
            def _():
                arrived(zc_s.at[dlt - 1], zc_sem.at[dlt - 1])
        left = jnp.concatenate([theta_s[i] for i in range(1, NZ - 1)], axis=0)
        right = jnp.concatenate([zc_s[i] for i in range(1, NZ - 1)], axis=0)
        d_row = zc_s[0] + mm(left, right, 0, 0)
        dsend_s[NY - 1] = d_row
        for i in range(NY - 1):
            dsend_s[i] = mm(psi_s[i], d_row, 0, 0) + gam_s[i]
        for i in range(NY):
            remote(dsend_s.at[i], dout_s.at[y], send_sem.at[12 + i], dout_sem.at[y], dev(z, i, 1)).start()
        for h in range(heads):
            arrived(dout_s.at[h], dout_sem.at[h])

    @pl.when(c == 1)
    def _():
        gain_along_z()
        fill_backward()
        for h in range(heads):
            arrived(dout_s.at[h], dout_sem.at[h])
            d0_s[h] = mm(ab_s[h, 0], dout_s[h], 0, 0) + c_s[h]
            remote(d0_s.at[h], dout_s.at[h], send_sem.at[36 + h], dout_sem.at[h], pair).start()

    for d in range(1, NZ):
        arrived(gz_s.at[(z + NZ - d) % NZ], gz_sem.at[d - 1])
    gsum_s[1] = jnp.sum(gz_s[...], axis=0)
    for d in range(1, 4):
        gx_copy(d).start()
    gx_s[xpos] = gsum_s[1]

    lane = lax.broadcasted_iota(jnp.int32, (steps, heads), 1)
    db_all = jnp.zeros((steps, heads), F32)
    for h in range(heads):
        p = p_s[h]
        b = b_ref[:, h:h + 1]
        d_out = dout_s[h]
        gm = g0_s[h] + mm(nk_s[h], d_out)
        dv = b * gm
        dvf_s[pl.ds(h, steps, stride=heads), :] = dv
        db = jnp.sum(gm * p, axis=-1, keepdims=True) / b
        db_all = db_all + jnp.where(lane == h, db, 0.0)
        hm = jnp.where(col_i < row_i, mm(dv, p, 1, 1), 0.0)
        dk = dk1_s[h] + mm(
            jnp.concatenate([p, dv], axis=1), jnp.concatenate([d_out, -sin_s[h]], axis=1), 1, 1
        ) - mm(hm + hm.T, of_head(ku_s, h, steps))
        dk_s[pl.ds(h, steps, stride=heads), :] = dk
    db_ref[...] = db_all
    out_ref[...] = of_s[...].astype(BF16)
    dq_ref[...] = unit_pullback(dq_s[...], qu_s[...], rq_s[...]).astype(BF16)
    dk_ref[...] = unit_pullback(dk_s[...], ku_s[...], rk_s[...]).astype(BF16)
    dv_ref[...] = dvf_s[...].astype(BF16)

    for d in range(1, 4):
        arrived(gx_s.at[(xpos + 4 - d) % 4], gx_sem.at[d - 1])
    dg_ref[...] = jnp.sum(gx_s[...], axis=0)[0:1]

    for j in range(2):
        send["pair", j].wait_send()
        head = 2 * c + j

        @pl.when(jnp.logical_not((c == 1) & (y == head)))
        def _():
            remote(comp_s.at[j], own_s.at[y], send_sem.at[2 + j], own_sem.at[y], dev(z, head, 1)).wait_send()

    def left(src, sem):
        remote(src, src, sem, sem, pair).wait_send()

    @pl.when(c == 1)
    def _():
        for dlt in range(1, NZ):
            @pl.when(z + dlt < NZ)
            def _():
                left(own_s.at[0], send_sem.at[4 + dlt])

            @pl.when(z >= dlt)
            def _():
                left(phi_s.at[NY - 1], send_sem.at[12 + dlt])
        for i in range(1, NY):
            left(own_s.at[i, 0], send_sem.at[20 + i])
            left(phi_s.at[i - 1], send_sem.at[24 + i])
        for i in range(NY):
            left(sout_s.at[i], send_sem.at[28 + i])
            left(c_s.at[i], send_sem.at[32 + i])
            left(d0_s.at[i], send_sem.at[36 + i])

    @pl.when(c == 0)
    def _():
        for h in range(heads):
            left(s1_s.at[h], send_sem.at[28 + h])

            @pl.when(y != h)
            def _():
                left(cc_s.at[h], send_sem.at[32 + h])
        for dlt in range(1, NZ):
            @pl.when(z >= dlt)
            def _():
                left(crow_s, send_sem.at[4 + dlt])
        for i in range(NY):
            left(dsend_s.at[i], send_sem.at[12 + i])
    for copy in gsends:
        copy.wait_send()
    for d in range(1, NZ):
        gz_copy(d).wait_send()
    for d in range(1, 4):
        gx_copy(d).wait_send()


def local(queries, keys, values, betas, gain, out_grad):
    tok, heads, dim = queries.shape
    steps = tok * keys.shape[1]
    f = lambda *s: pltpu.VMEM(s, F32)
    dma = pltpu.SemaphoreType.DMA
    vmem = pl.BlockSpec(memory_space=pltpu.VMEM)
    scratch = [
        f(steps * heads, dim), f(tok * heads, dim), f(steps * heads, dim), f(tok * heads, dim),
        f(steps * heads, 1), f(tok * heads, 1), f(heads, steps, steps), f(heads, steps, steps),
        f(heads, steps, steps), f(heads, steps, dim), f(heads, steps, 2 * dim), f(heads, steps, tok),
        f(heads, tok, dim), f(heads, dim, tok), f(heads, tok, dim), f(heads, steps, dim), f(heads, tok, dim),
        f(heads, steps, dim), f(heads, steps, dim), f(tok * heads, dim), f(tok * heads, dim),
        f(steps * heads, dim), f(steps * heads, dim),
        f(heads, 2, dim, dim), f(2, 2, dim, dim), f(2, 2, dim, dim), f(NY, 2, dim, dim),
        f(NY, dim, dim), f(NY, dim, dim), f(NZ - 1, 2, dim, dim), f(NZ - 1, dim, dim),
        f(NY, dim, dim), f(heads, dim, dim), f(heads, dim, dim),
        f(NY, dim, dim), f(NY, dim, dim), f(NZ - 1, dim, dim), f(NY - 1, dim, dim), f(heads, dim, dim),
        f(heads, dim, dim), f(heads, dim, dim), f(NY, dim, dim), f(dim, dim), f(NZ - 1, dim, dim),
        f(NY - 1, dim, dim), f(NY, dim, dim), f(heads, dim, dim), f(heads, dim, dim),
        f(8, dim), f(NY * NC, 8, dim), f(NZ, 8, dim), f(4, 8, dim), f(2, 8, dim),
        dma((40,)), dma((2,)), dma((NY,)), dma((NZ - 1,)), dma((NZ - 1,)), dma((heads,)), dma((2 * NY,)),
        dma((heads,)), dma((NY,)), dma((NZ - 1,)), dma((heads,)),
        dma((24,)), dma((NY * NC - 1,)), dma((NZ - 1,)), dma((3,)),
    ]
    outs = pl.pallas_call(
        kernel,
        out_shape=(
            jax.ShapeDtypeStruct((tok * heads, dim), BF16),
            jax.ShapeDtypeStruct((tok * heads, dim), BF16),
            jax.ShapeDtypeStruct((steps * heads, dim), BF16),
            jax.ShapeDtypeStruct((steps * heads, dim), BF16),
            jax.ShapeDtypeStruct((steps, heads), F32),
            jax.ShapeDtypeStruct((1, dim), F32),
        ),
        in_specs=[vmem] * 6,
        out_specs=(vmem,) * 6,
        scratch_shapes=scratch,
        compiler_params=pltpu.CompilerParams(
            collective_id=0, has_side_effects=True, vmem_limit_bytes=60 * 1024 * 1024
        ),
        name="delta_product",
    )(
        queries.reshape(tok * heads, dim),
        keys.reshape(steps * heads, dim),
        values.reshape(steps * heads, dim),
        betas.reshape(steps, heads),
        gain.reshape(1, dim),
        out_grad.reshape(tok * heads, dim),
    )
    out, dq, dk, dv, db, dg = outs
    return (
        out.reshape(queries.shape), dq.reshape(queries.shape), dk.reshape(keys.shape), dv.reshape(values.shape), db.reshape(betas.shape), dg.reshape(dim),
    )


def solution(mesh):
    return jax.shard_map(
        local,
        mesh=mesh,
        in_specs=(
            P("seq", "head", None),
            P("seq", None, "head", None),
            P("seq", None, "head", None),
            P("seq", None, "head"),
            P(),
            P("seq", "head", None),
        ),
        out_specs=(
            P("seq", "head", None),
            P("seq", "head", None),
            P("seq", None, "head", None),
            P("seq", None, "head", None),
            P("seq", None, "head"),
            P(),
        ),
        check_vma=False,
    )
```

```python
import functools

import jax
import jax.numpy as jnp
from jax import lax
from jax.experimental import pallas as pl
from jax.experimental.pallas import tpu as pltpu
from jax.sharding import PartitionSpec as P

EPS = 1e-06
F32 = jnp.float32
BF16 = jnp.bfloat16
MESH = pl.DeviceIdType.MESH
NY = 4
NZ = 8
NC = 2


def split(x):
    hi = x.astype(BF16)
    lo = (x - hi.astype(F32)).astype(BF16)
    return hi, lo


def dot(a, b, dims):
    return lax.dot_general(a, b, (dims, ((), ())), preferred_element_type=F32)


def mms(a, b, ca=1, cb=0):
    left = jnp.concatenate([a[0], a[1], a[0]], axis=ca)
    right = jnp.concatenate([b[0], b[0], b[1]], axis=cb)
    return dot(left, right, ((ca,), (cb,)))


def mm(a, b, ca=1, cb=0):
    return mms(split(a), split(b), ca, cb)


def iotas(rows, cols):
    return (
        lax.broadcasted_iota(jnp.int32, (rows, cols), 0),
        lax.broadcasted_iota(jnp.int32, (rows, cols), 1),
    )


def unit_pullback(d_unit, unit, inverse):
    return (d_unit - unit * jnp.sum(unit * d_unit, axis=-1, keepdims=True)) * inverse


def kernel(
    q_hbm, k_hbm, v_hbm, b_hbm, g_hbm, do_hbm,
    out_ref, dq_ref, dk_ref, dv_ref, db_ref, dg_ref,
    q_ref, k_ref, v_ref, bt_ref, g_ref, do_ref, b_ref, db_s, in_sem,
    ku_s, qu_s, vf_s, dof_s, rk_s, rq_s, low_s, n_s, nt_s, nk_s, wu_s, sct_s, r_s, rt_s, ol_s, p_s, adj_s,
    g0_s, dk1_s, of_s, dq_s, dk_s, dvf_s, dv_s,
    ab_s, pair_s, comp_s, own_s, phi_s, beta_s, zab_s, za_s, sout_s, sin_s, s1_s,
    aown_s, phi0_s, theta_s, psi_s, c_s, cpair_s, cc_s, cown_s, crow_s, zc_s, gam_s, dsend_s, dout_s, d0_s,
    gpart_s, grow_s, gz_s, gx_s, gsum_s,
    send_sem, pair_sem, own_sem, zab_sem, za_sem, sin_sem, aown_sem, cpair_sem, cown_sem, zc_sem, dout_sem,
    gsend_sem, grow_sem, gz_sem, gx_sem,
):
    steps, heads = b_ref.shape
    per = steps // (q_ref.shape[0] // heads)
    tok = q_ref.shape[0] // heads
    dim = q_ref.shape[1]
    seq = lax.axis_index("seq")
    xpos = lax.axis_index("head")
    z = seq // (NY * NC)
    y = (seq // NC) % NY
    c = seq % NC

    def dev(zz, yy, cc):
        return {"seq": zz * (NY * NC) + yy * NC + cc}

    barrier = pltpu.get_barrier_semaphore()
    count = 0
    for dy in range(NY):
        for dc in range(NC):
            if dy or dc:
                pl.semaphore_signal(
                    barrier, inc=1, device_id=dev(z, (y + dy) % NY, (c + dc) % NC), device_id_type=MESH
                )
                count += 1
    for dz in range(1, NZ):
        for dc in range(NC):
            pl.semaphore_signal(
                barrier, inc=1, device_id=dev((z + dz) % NZ, y, (c + dc) % NC), device_id_type=MESH
            )
            count += 1
    for dx in range(1, 4):
        pl.semaphore_signal(
            barrier, inc=1, device_id={"head": (xpos + dx) % 4}, device_id_type=MESH
        )
        count += 1

    loads = [
        pltpu.make_async_copy(src, dst, in_sem.at[n])
        for n, (src, dst) in enumerate([
            (k_hbm, k_ref), (b_hbm, bt_ref), (v_hbm, v_ref), (q_hbm, q_ref), (do_hbm, do_ref), (g_hbm, g_ref)
        ])
    ]
    for load in loads:
        load.start()

    def remote(src, dst, ssem, rsem, target):
        return pltpu.make_async_remote_copy(
            src_ref=src, dst_ref=dst, send_sem=ssem, recv_sem=rsem, device_id=target, device_id_type=MESH
        )

    def arrived(dst, rsem):
        pltpu.make_async_copy(dst, dst, rsem).wait()

    row_i, col_i = iotas(steps, steps)
    tok_i, step_i = iotas(tok, steps)
    visible = step_i <= 2 * tok_i + 1
    eye = (row_i == col_i).astype(F32)
    eye_dim = eye[:dim, :dim]

    for dlt in range(1, NZ):
        @pl.when(z < dlt)
        def _():
            zab_s[dlt - 1] = jnp.zeros((2, dim, dim), F32)

        @pl.when(z + dlt >= NZ)
        def _():
            za_s[dlt - 1] = jnp.zeros((dim, dim), F32)
            zc_s[dlt - 1] = jnp.zeros((dim, dim), F32)

    for load in loads:
        load.wait()
    turned = bt_ref[...].T
    for j in range(per):
        b_ref[pl.ds(j, tok, stride=per), :] = turned[:, j * heads:(j + 1) * heads]
    q = q_ref[...].astype(F32)
    k = k_ref[...].astype(F32)
    rq = lax.rsqrt(jnp.sum(q * q, axis=-1, keepdims=True) + EPS)
    rk = lax.rsqrt(jnp.sum(k * k, axis=-1, keepdims=True) + EPS)
    rq_s[...] = rq
    rk_s[...] = rk
    qu_s[...] = q * rq
    ku_s[...] = k * rk
    vf_s[...] = v_ref[...].astype(F32)
    dof_s[...] = do_ref[...].astype(F32)

    def of_head(ref, h, rows):
        return ref[pl.ds(h, rows, stride=heads), :]

    half = steps // 2
    base = 16
    blocks = half // base
    lane16 = lax.broadcasted_iota(jnp.int32, (base, half), 1) // base
    packed = []
    for h in range(heads):
        ku = of_head(ku_s, h, steps)
        b = b_ref[:, h:h + 1]
        low = jnp.where(col_i < row_i, mm(ku, ku, 1, 1) * b, 0.0)
        low_s[h] = low
        for part in range(2):
            tri = low[part * half:(part + 1) * half, part * half:(part + 1) * half]
            diag = jnp.zeros((base, half), F32)
            for i in range(blocks):
                diag = jnp.where(lane16 == i, tri[i * base:(i + 1) * base], diag)
            packed.append(diag)
    packed = jnp.concatenate(packed, axis=0)
    rows = packed.shape[0]
    lane = lax.broadcasted_iota(jnp.int32, (rows, half), 1)
    row = lax.broadcasted_iota(jnp.int32, (rows, half), 0)
    inv = jnp.where(row % base == lane % base, 1.0, 0.0)
    for step in range(base - 1):
        column = jnp.take_along_axis(packed, (lane // base) * base + step, axis=1)
        pivot = inv.reshape(rows // base, base, half)[:, step:step + 1, :]
        pivot = jnp.broadcast_to(pivot, (rows // base, base, half)).reshape(rows, half)
        inv = inv - column * pivot
    quads = [(h, part) for h in range(heads) for part in range(2)]
    for n, (h, part) in enumerate(quads):
        mine = inv[n * base:(n + 1) * base]
        n_s[h, part * half:(part + 1) * half, part * half:(part + 1) * half] = jnp.concatenate(
            [jnp.where(lane16 == i, mine, 0.0) for i in range(blocks)], axis=0
        )
        if part:
            n_s[h, 0:half, half:steps] = jnp.zeros((half, half), F32)
    sub_i, sub_j = row_i[:half, :half], col_i[:half, :half]
    size = base
    while size < half:
        band = (sub_i // (2 * size) == sub_j // (2 * size)) & (sub_i // size != sub_j // size)
        firsts = {}
        for h, part in quads:
            at = pl.ds(part * half, half)
            parts = split(n_s[h, at, at])
            firsts[h, part] = parts, mms(split(low_s[h, at, at]), parts)
        for h, part in quads:
            at = pl.ds(part * half, half)
            parts, first = firsts[h, part]
            n_s[h, at, at] = n_s[h, at, at] - jnp.where(band, mms(parts, split(first)), 0.0)
        size *= 2
    firsts = [mm(low_s[h, half:steps, 0:half], n_s[h, 0:half, 0:half]) for h in range(heads)]
    for h in range(heads):
        n_s[h, half:steps, 0:half] = -mm(n_s[h, half:steps, half:steps], firsts[h])
    for h in range(heads):
        ku = of_head(ku_s, h, steps)
        b = b_ref[:, h:h + 1]
        wu_s[h] = mm(n_s[h], jnp.concatenate([b * ku, b * of_head(vf_s, h, steps)], axis=1))
    for h in range(heads):
        ab = mm(of_head(ku_s, h, steps).T, wu_s[h])
        ab_s[h, 0] = eye_dim - ab[:, :dim]
        ab_s[h, 1] = ab[:, dim:]

    def fill_forward():
        for h in range(heads):
            ku = of_head(ku_s, h, steps)
            qu = of_head(qu_s, h, tok)
            sc = jnp.where(visible, mm(qu, ku, 1, 1), 0.0)
            ro = mm(sc, wu_s[h])
            r = qu - ro[:, :dim]
            r_s[h] = r
            rt_s[h] = r.T
            ol_s[h] = ro[:, dim:]
            sct_s[h] = sc.T
            nt = n_s[h].T
            nt_s[h] = nt
            nk_s[h] = mm(nt, ku)

    def fill_backward():
        for h in range(heads):
            ku = of_head(ku_s, h, steps)
            adj = adj_s[h]
            m_do = jnp.where(visible, mm(adj, p_s[h], 1, 1), 0.0)
            dq = mm(adj, sin_s[h], 1, 1) + mm(m_do, ku)
            dq_s[pl.ds(h, tok, stride=heads), :] = dq
            dk1_s[h] = mm(m_do.T, of_head(qu_s, h, tok))
            g0_s[h] = mm(nt_s[h], mm(sct_s[h], adj))

    pl.semaphore_wait(barrier, count)

    other = 1 - c
    pair = dev(z, y, other)
    send = {}
    for j in range(2):
        send["pair", j] = remote(
            ab_s.at[2 * other + j], pair_s.at[j], send_sem.at[j], pair_sem.at[j], pair
        )
        send["pair", j].start()
    for j in range(2):
        arrived(pair_s.at[j], pair_sem.at[j])
        mine = ab_s[2 * c + j]
        theirs = pair_s[j]
        first = jnp.where(c == 0, mine, theirs)
        second = jnp.where(c == 0, theirs, mine)
        both = mm(second[0], jnp.concatenate([first[0], first[1]], axis=1))
        comp_s[j, 0] = both[:, :dim]
        comp_s[j, 1] = both[:, dim:] + second[1]
        head = 2 * c + j
        here = (c == 1) & (y == head)

        @pl.when(here)
        def _():
            pltpu.make_async_copy(comp_s.at[j], own_s.at[y], own_sem.at[y]).start()

        @pl.when(jnp.logical_not(here))
        def _():
            remote(comp_s.at[j], own_s.at[y], send_sem.at[2 + j], own_sem.at[y], dev(z, head, 1)).start()

    @pl.when(c == 1)
    def _():
        low_core = dev(z, y, 0)
        arrived(own_s.at[0], own_sem.at[0])
        x = jnp.concatenate([own_s[0, 0], own_s[0, 1]], axis=1)
        phi_s[0] = x[:, :dim]
        beta_s[0] = x[:, dim:]
        for i in range(1, NY):
            arrived(own_s.at[i], own_sem.at[i])
            x = mm(own_s[i, 0], x)
            x = jnp.concatenate([x[:, :dim], x[:, dim:] + own_s[i, 1]], axis=1)
            phi_s[i] = x[:, :dim]
            beta_s[i] = x[:, dim:]
        comp_row = own_s.at[0]
        comp_row[0] = x[:, :dim]
        comp_row[1] = x[:, dim:]
        for dlt in range(NZ - 1, 0, -1):
            @pl.when(z + dlt < NZ)
            def _():
                remote(
                    own_s.at[0], zab_s.at[dlt - 1], send_sem.at[4 + dlt], zab_sem.at[dlt - 1],
                    dev(z + dlt, y, 1),
                ).start()
        for dlt in range(1, NZ):
            @pl.when(z >= dlt)
            def _():
                remote(
                    phi_s.at[NY - 1], za_s.at[dlt - 1], send_sem.at[12 + dlt], za_sem.at[dlt - 1],
                    dev(z - dlt, y, 0),
                ).start()
        for i in range(1, NY):
            remote(own_s.at[i, 0], aown_s.at[i], send_sem.at[20 + i], aown_sem.at[i], low_core).start()
            remote(phi_s.at[i - 1], phi0_s.at[i], send_sem.at[24 + i], aown_sem.at[NY + i], low_core).start()
        fill_forward()
        state = jnp.zeros((dim, dim), F32)
        for dlt in range(NZ - 1, 0, -1):
            @pl.when(z >= dlt)
            def _():
                arrived(zab_s.at[dlt - 1], zab_sem.at[dlt - 1])

            if dlt == NZ - 1:
                state = zab_s[dlt - 1, 1]
            else:
                state = mm(zab_s[dlt - 1, 0], state) + zab_s[dlt - 1, 1]
        sout_s[0] = state
        later = mm(jnp.concatenate([phi_s[i] for i in range(NY - 1)], axis=0), state)
        for i in range(1, NY):
            sout_s[i] = later[(i - 1) * dim:i * dim] + beta_s[i - 1]
        for i in range(NY):
            remote(sout_s.at[i], sin_s.at[y], send_sem.at[28 + i], sin_sem.at[y], dev(z, i, 0)).start()
        for h in range(heads):
            arrived(sin_s.at[h], sin_sem.at[h])

    @pl.when(c == 0)
    def _():
        fill_forward()
        for i in range(1, NY):
            arrived(aown_s.at[i], aown_sem.at[i])
            arrived(phi0_s.at[i], aown_sem.at[NY + i])
        psi_s[NY - 2] = aown_s[NY - 1]
        for i in range(NY - 3, -1, -1):
            psi_s[i] = mm(psi_s[i + 1], aown_s[i + 1])
        theta_s[0] = eye_dim
        for dlt in range(1, NZ - 1):
            @pl.when(z + dlt < NZ)
            def _():
                arrived(za_s.at[dlt - 1], za_sem.at[dlt - 1])

            theta_s[dlt] = za_s[0] if dlt == 1 else mm(za_s[dlt - 1], theta_s[dlt - 1])

        @pl.when(z + NZ - 1 < NZ)
        def _():
            arrived(za_s.at[NZ - 2], za_sem.at[NZ - 2])

        for h in range(heads):
            arrived(sin_s.at[h], sin_sem.at[h])
            s1_s[h] = mm(ab_s[h, 0], sin_s[h]) + ab_s[h, 1]
            remote(s1_s.at[h], sin_s.at[h], send_sem.at[28 + h], sin_sem.at[h], pair).start()

    gain = g_ref[...]
    gain_part = jnp.zeros((1, dim), F32)
    for h in range(heads):
        state = sin_s[h]
        both = mm(jnp.concatenate([r_s[h], wu_s[h, :, :dim]], axis=0), state)
        o = ol_s[h] + both[:tok]
        p_s[h] = wu_s[h, :, dim:] - both[tok:]
        inv_rms = lax.rsqrt(jnp.mean(o * o, axis=-1, keepdims=True) + EPS)
        normal = o * inv_rms
        grad = of_head(dof_s, h, tok)
        of_s[pl.ds(h, tok, stride=heads), :] = gain * normal
        gain_part = gain_part + jnp.sum(grad * normal, axis=0, keepdims=True)
        scaled = grad * gain
        adj = inv_rms * (scaled - normal * jnp.mean(scaled * normal, axis=-1, keepdims=True))
        adj_s[h] = adj
        c_s[h] = mm(rt_s[h], adj)

        @pl.when(c == 1)
        def _():
            remote(c_s.at[h], cpair_s.at[h], send_sem.at[32 + h], cpair_sem.at[h], pair).start()

    gpart_s[...] = jnp.broadcast_to(gain_part, (8, dim))
    me8 = y * NC + c
    n_g = 0
    gsends = []
    for d in range(1, NY * NC):
        to = (me8 + d) % (NY * NC)
        gsends.append(remote(
            gpart_s, grow_s.at[me8], gsend_sem.at[n_g], grow_sem.at[d - 1], dev(z, to // NC, to % NC)))
        gsends[-1].start()
        n_g += 1
    grow_s[me8] = gpart_s[...]

    def gain_along_z():
        for d in range(1, NY * NC):
            fr = (me8 + NY * NC - d) % (NY * NC)
            arrived(grow_s.at[fr], grow_sem.at[d - 1])
        gsum_s[0] = jnp.sum(grow_s[...], axis=0)
        for d in range(1, NZ):
            gz_copy(d).start()
        gz_s[z] = gsum_s[0]

    def gz_copy(d):
        return remote(
            gsum_s.at[0], gz_s.at[z], gsend_sem.at[6 + d], gz_sem.at[d - 1], dev((z + d) % NZ, y, c)
        )

    def gx_copy(d):
        return remote(
            gsum_s.at[1], gx_s.at[xpos], gsend_sem.at[13 + d], gx_sem.at[d - 1], {"head": (xpos + d) % 4}
        )

    @pl.when(c == 0)
    def _():
        for h in range(heads):
            arrived(cpair_s.at[h], cpair_sem.at[h])
            cc_s[h] = mm(ab_s[h, 0], cpair_s[h], 0, 0) + c_s[h]

            @pl.when(y == h)
            def _():
                pltpu.make_async_copy(cc_s.at[h], cown_s.at[h], cown_sem.at[h]).start()

            @pl.when(y != h)
            def _():
                remote(cc_s.at[h], cown_s.at[y], send_sem.at[32 + h], cown_sem.at[y], dev(z, h, 0)).start()
        for i in range(NY):
            arrived(cown_s.at[i], cown_sem.at[i])
        left = jnp.concatenate([phi0_s[i] for i in range(1, NY)], axis=0)
        right = jnp.concatenate([cown_s[i] for i in range(1, NY)], axis=0)
        crow_s[...] = cown_s[0] + mm(left, right, 0, 0)
        for dlt in range(NZ - 1, 0, -1):
            @pl.when(z >= dlt)
            def _():
                remote(
                    crow_s, zc_s.at[dlt - 1], send_sem.at[4 + dlt], zc_sem.at[dlt - 1], dev(z - dlt, y, 0)
                ).start()
        gam_s[NY - 2] = cown_s[NY - 1]
        for i in range(NY - 3, -1, -1):
            gam_s[i] = mm(aown_s[i + 1], gam_s[i + 1], 0, 0) + cown_s[i + 1]
        gain_along_z()
        fill_backward()
        for dlt in range(NZ - 1, 0, -1):
            @pl.when(z + dlt < NZ)
            def _():
                arrived(zc_s.at[dlt - 1], zc_sem.at[dlt - 1])
        left = jnp.concatenate([theta_s[i] for i in range(1, NZ - 1)], axis=0)
        right = jnp.concatenate([zc_s[i] for i in range(1, NZ - 1)], axis=0)
        d_row = zc_s[0] + mm(left, right, 0, 0)
        dsend_s[NY - 1] = d_row
        for i in range(NY - 1):
            dsend_s[i] = mm(psi_s[i], d_row, 0, 0) + gam_s[i]
        for i in range(NY):
            remote(dsend_s.at[i], dout_s.at[y], send_sem.at[12 + i], dout_sem.at[y], dev(z, i, 1)).start()
        for h in range(heads):
            arrived(dout_s.at[h], dout_sem.at[h])

    @pl.when(c == 1)
    def _():
        gain_along_z()
        fill_backward()
        for h in range(heads):
            arrived(dout_s.at[h], dout_sem.at[h])
            d0_s[h] = mm(ab_s[h, 0], dout_s[h], 0, 0) + c_s[h]
            remote(d0_s.at[h], dout_s.at[h], send_sem.at[36 + h], dout_sem.at[h], pair).start()

    for d in range(1, NZ):
        arrived(gz_s.at[(z + NZ - d) % NZ], gz_sem.at[d - 1])
    gsum_s[1] = jnp.sum(gz_s[...], axis=0)
    for d in range(1, 4):
        gx_copy(d).start()
    gx_s[xpos] = gsum_s[1]

    lane = lax.broadcasted_iota(jnp.int32, (steps, heads), 1)
    db_all = jnp.zeros((steps, heads), F32)
    for h in range(heads):
        gm = g0_s[h] + mm(nk_s[h], dout_s[h])
        b = b_ref[:, h:h + 1]
        dv = b * gm
        dv_s[h] = dv
        dvf_s[pl.ds(h, steps, stride=heads), :] = dv
        db = jnp.sum(gm * p_s[h], axis=-1, keepdims=True) / b
        db_all = db_all + jnp.where(lane == h, db, 0.0)
    db_s[...] = db_all
    for h in range(heads):
        hm = jnp.where(col_i < row_i, mm(dv_s[h], p_s[h], 1, 1), 0.0)
        low_s[h] = hm + hm.T
    for h in range(heads):
        dk = dk1_s[h] + mm(
            jnp.concatenate([p_s[h], dv_s[h]], axis=1), jnp.concatenate([dout_s[h], -sin_s[h]], axis=1), 1, 1
        ) - mm(low_s[h], of_head(ku_s, h, steps))
        dk_s[pl.ds(h, steps, stride=heads), :] = dk
    db_ref[...] = jnp.concatenate([db_s[pl.ds(j, tok, stride=per), :] for j in range(per)], axis=1).T
    out_ref[...] = of_s[...].astype(BF16)
    dq_ref[...] = unit_pullback(dq_s[...], qu_s[...], rq_s[...]).astype(BF16)
    dk_ref[...] = unit_pullback(dk_s[...], ku_s[...], rk_s[...]).astype(BF16)
    dv_ref[...] = dvf_s[...].astype(BF16)

    for d in range(1, 4):
        arrived(gx_s.at[(xpos + 4 - d) % 4], gx_sem.at[d - 1])
    dg_ref[...] = jnp.sum(gx_s[...], axis=0)[0:1]

    for j in range(2):
        send["pair", j].wait_send()
        head = 2 * c + j

        @pl.when(jnp.logical_not((c == 1) & (y == head)))
        def _():
            remote(comp_s.at[j], own_s.at[y], send_sem.at[2 + j], own_sem.at[y], dev(z, head, 1)).wait_send()

    def left(src, sem):
        remote(src, src, sem, sem, pair).wait_send()

    @pl.when(c == 1)
    def _():
        for dlt in range(1, NZ):
            @pl.when(z + dlt < NZ)
            def _():
                left(own_s.at[0], send_sem.at[4 + dlt])

            @pl.when(z >= dlt)
            def _():
                left(phi_s.at[NY - 1], send_sem.at[12 + dlt])
        for i in range(1, NY):
            left(own_s.at[i, 0], send_sem.at[20 + i])
            left(phi_s.at[i - 1], send_sem.at[24 + i])
        for i in range(NY):
            left(sout_s.at[i], send_sem.at[28 + i])
            left(c_s.at[i], send_sem.at[32 + i])
            left(d0_s.at[i], send_sem.at[36 + i])

    @pl.when(c == 0)
    def _():
        for h in range(heads):
            left(s1_s.at[h], send_sem.at[28 + h])

            @pl.when(y != h)
            def _():
                left(cc_s.at[h], send_sem.at[32 + h])
        for dlt in range(1, NZ):
            @pl.when(z >= dlt)
            def _():
                left(crow_s, send_sem.at[4 + dlt])
        for i in range(NY):
            left(dsend_s.at[i], send_sem.at[12 + i])
    for copy in gsends:
        copy.wait_send()
    for d in range(1, NZ):
        gz_copy(d).wait_send()
    for d in range(1, 4):
        gx_copy(d).wait_send()


def local(queries, keys, values, betas, gain, out_grad):
    tok, heads, dim = queries.shape
    per = keys.shape[1]
    steps = tok * per
    f = lambda *s: pltpu.VMEM(s, F32)
    dma = pltpu.SemaphoreType.DMA
    vmem = pl.BlockSpec(memory_space=pltpu.VMEM)
    b16 = lambda *sh: pltpu.VMEM(sh, BF16)
    scratch = [
        b16(tok * heads, dim), b16(steps * heads, dim), b16(steps * heads, dim), f(per * heads, tok), f(1, dim),
        b16(tok * heads, dim), f(steps, heads), f(steps, heads), dma((6,)),
        f(steps * heads, dim), f(tok * heads, dim), f(steps * heads, dim), f(tok * heads, dim),
        f(steps * heads, 1), f(tok * heads, 1), f(heads, steps, steps), f(heads, steps, steps),
        f(heads, steps, steps), f(heads, steps, dim), f(heads, steps, 2 * dim), f(heads, steps, tok),
        f(heads, tok, dim), f(heads, dim, tok), f(heads, tok, dim), f(heads, steps, dim), f(heads, tok, dim),
        f(heads, steps, dim), f(heads, steps, dim), f(tok * heads, dim), f(tok * heads, dim),
        f(steps * heads, dim), f(steps * heads, dim), f(heads, steps, dim),
        f(heads, 2, dim, dim), f(2, 2, dim, dim), f(2, 2, dim, dim), f(NY, 2, dim, dim),
        f(NY, dim, dim), f(NY, dim, dim), f(NZ - 1, 2, dim, dim), f(NZ - 1, dim, dim),
        f(NY, dim, dim), f(heads, dim, dim), f(heads, dim, dim),
        f(NY, dim, dim), f(NY, dim, dim), f(NZ - 1, dim, dim), f(NY - 1, dim, dim), f(heads, dim, dim),
        f(heads, dim, dim), f(heads, dim, dim), f(NY, dim, dim), f(dim, dim), f(NZ - 1, dim, dim),
        f(NY - 1, dim, dim), f(NY, dim, dim), f(heads, dim, dim), f(heads, dim, dim),
        f(8, dim), f(NY * NC, 8, dim), f(NZ, 8, dim), f(4, 8, dim), f(2, 8, dim),
        dma((40,)), dma((2,)), dma((NY,)), dma((NZ - 1,)), dma((NZ - 1,)), dma((heads,)), dma((2 * NY,)),
        dma((heads,)), dma((NY,)), dma((NZ - 1,)), dma((heads,)),
        dma((24,)), dma((NY * NC - 1,)), dma((NZ - 1,)), dma((3,)),
    ]
    outs = pl.pallas_call(
        kernel,
        out_shape=(
            jax.ShapeDtypeStruct((tok * heads, dim), BF16),
            jax.ShapeDtypeStruct((tok * heads, dim), BF16),
            jax.ShapeDtypeStruct((steps * heads, dim), BF16),
            jax.ShapeDtypeStruct((steps * heads, dim), BF16),
            jax.ShapeDtypeStruct((per * heads, tok), F32),
            jax.ShapeDtypeStruct((1, dim), F32),
        ),
        in_specs=[pl.BlockSpec(memory_space=pltpu.HBM)] * 6,
        out_specs=(vmem,) * 6,
        scratch_shapes=scratch,
        compiler_params=pltpu.CompilerParams(
            collective_id=0, has_side_effects=True, vmem_limit_bytes=32 * 1024 * 1024
        ),
        name="delta_product",
    )(
        queries.reshape(tok * heads, dim),
        keys.reshape(steps * heads, dim),
        values.reshape(steps * heads, dim),
        betas.transpose(1, 2, 0).reshape(per * heads, tok),
        gain.reshape(1, dim),
        out_grad.reshape(tok * heads, dim),
    )
    out, dq, dk, dv, db, dg = pl.pallas_call(
        store,
        out_shape=tuple(jax.ShapeDtypeStruct(a.shape, a.dtype) for a in outs),
        in_specs=[vmem] * 6,
        out_specs=(pl.BlockSpec(memory_space=pl.ANY),) * 6,
        scratch_shapes=[dma((6,))],
        compiler_params=pltpu.CompilerParams(vmem_limit_bytes=4 * 1024 * 1024),
        name="store",
    )(*outs)
    return (
        out.reshape(queries.shape), dq.reshape(queries.shape), dk.reshape(keys.shape), dv.reshape(values.shape),
        db.reshape(per, heads, tok).transpose(2, 0, 1), dg.reshape(dim),
    )


def store(*refs):
    sem = refs[-1]
    copies = [pltpu.make_async_copy(refs[n], refs[6 + n], sem.at[n]) for n in range(6)]
    for copy in copies:
        copy.start()
    for copy in copies:
        copy.wait()


def solution(mesh):
    return jax.shard_map(
        local,
        mesh=mesh,
        in_specs=(
            P("seq", "head", None),
            P("seq", None, "head", None),
            P("seq", None, "head", None),
            P("seq", None, "head"),
            P(),
            P("seq", "head", None),
        ),
        out_specs=(
            P("seq", "head", None),
            P("seq", "head", None),
            P("seq", None, "head", None),
            P("seq", None, "head", None),
            P("seq", None, "head"),
            P(),
        ),
        check_vma=False,
    )
```

```python
import functools

import jax
import jax.numpy as jnp
from jax import lax
from jax.experimental import pallas as pl
from jax.experimental.pallas import tpu as pltpu
from jax.sharding import PartitionSpec as P

EPS = 1e-06
F32 = jnp.float32
BF16 = jnp.bfloat16
MESH = pl.DeviceIdType.MESH
NY = 4
NZ = 8
NG = 4
NC = 2


def split(x):
    hi = x.astype(BF16)
    lo = (x - hi.astype(F32)).astype(BF16)
    return hi, lo


def dot(a, b, dims):
    return lax.dot_general(a, b, (dims, ((), ())), preferred_element_type=F32)


def mms(a, b, ca=1, cb=0):
    left = jnp.concatenate([a[0], a[1], a[0]], axis=ca)
    right = jnp.concatenate([b[0], b[0], b[1]], axis=cb)
    return dot(left, right, ((ca,), (cb,)))


def mm(a, b, ca=1, cb=0):
    return mms(split(a), split(b), ca, cb)


def iotas(rows, cols):
    return (
        lax.broadcasted_iota(jnp.int32, (rows, cols), 0),
        lax.broadcasted_iota(jnp.int32, (rows, cols), 1),
    )


def unit_pullback(d_unit, unit, inverse):
    return (d_unit - unit * jnp.sum(unit * d_unit, axis=-1, keepdims=True)) * inverse


def kernel(
    q_hbm, k_hbm, v_hbm, b_hbm, g_hbm, do_hbm,
    out_ref, dq_ref, dk_ref, dv_ref, db_ref, dg_ref,
    q_ref, k_ref, v_ref, bt_ref, g_ref, do_ref, b_ref, db_s, in_sem,
    ku_s, qu_s, vf_s, dof_s, rk_s, rq_s, low_s, n_s, nt_s, nk_s, wu_s, sct_s, r_s, rt_s, ol_s, p_s, adj_s,
    g0_s, dk1_s, of_s, dq_s, dk_s, dvf_s, dv_s,
    ab_s, pair_s, comp_s, own_s, phi_s, beta_s, zab_s, za_s, sout_s, sin_s, s1_s,
    aown_s, phi0_s, theta_s, psi_s, c_s, cpair_s, cc_s, cown_s, crow_s, zc_s, gam_s, dsend_s, dout_s, d0_s,
    gpart_s, grow_s, gz_s, gx_s, gsum_s, x_s, middle_s, mid_s, mid_sem,
    send_sem, pair_sem, own_sem, zab_sem, za_sem, sin_sem, aown_sem, cpair_sem, cown_sem, zc_sem, dout_sem,
    gsend_sem, grow_sem, gz_sem, gx_sem,
):
    steps, heads = b_ref.shape
    per = steps // (q_ref.shape[0] // heads)
    tok = q_ref.shape[0] // heads
    dim = q_ref.shape[1]
    seq = lax.axis_index("seq")
    xpos = lax.axis_index("head")
    z = seq // (NY * NC)
    y = (seq // NC) % NY
    c = seq % NC

    def dev(zz, yy, cc):
        return {"seq": zz * (NY * NC) + yy * NC + cc}

    barrier = pltpu.get_barrier_semaphore()
    count = 0
    for dy in range(NY):
        for dc in range(NC):
            if dy or dc:
                pl.semaphore_signal(
                    barrier, inc=1, device_id=dev(z, (y + dy) % NY, (c + dc) % NC), device_id_type=MESH
                )
                count += 1
    for dz in range(1, NZ):
        for dc in range(NC):
            pl.semaphore_signal(
                barrier, inc=1, device_id=dev((z + dz) % NZ, y, (c + dc) % NC), device_id_type=MESH
            )
            count += 1
    for dx in range(1, 4):
        pl.semaphore_signal(
            barrier, inc=1, device_id={"head": (xpos + dx) % 4}, device_id_type=MESH
        )
        count += 1

    loads = [
        pltpu.make_async_copy(src, dst, in_sem.at[n])
        for n, (src, dst) in enumerate([
            (k_hbm, k_ref), (b_hbm, bt_ref), (v_hbm, v_ref), (q_hbm, q_ref), (do_hbm, do_ref), (g_hbm, g_ref)
        ])
    ]
    for load in loads:
        load.start()

    def remote(src, dst, ssem, rsem, target):
        return pltpu.make_async_remote_copy(
            src_ref=src, dst_ref=dst, send_sem=ssem, recv_sem=rsem, device_id=target, device_id_type=MESH
        )

    def arrived(dst, rsem):
        pltpu.make_async_copy(dst, dst, rsem).wait()

    group = z // NG
    rank = z % NG

    def zab_copy(dlt):
        return remote(
            own_s.at[0], zab_s.at[rank], send_sem.at[4 + dlt], zab_sem.at[rank], dev(z + dlt, y, 1)
        )

    def zback_copy():
        return remote(own_s.at[0], zab_s.at[rank], send_sem.at[8], zab_sem.at[rank], dev(0, y, 1))

    def middle_copy(n):
        to = jnp.where(rank == 0, NZ - 1 - n, NG + n)
        return remote(middle_s, mid_s, send_sem.at[9 + n], mid_sem, dev(to, y, 1))

    row_i, col_i = iotas(steps, steps)
    tok_i, step_i = iotas(tok, steps)
    visible = step_i <= 2 * tok_i + 1
    eye = (row_i == col_i).astype(F32)
    eye_dim = eye[:dim, :dim]

    for dlt in range(1, NZ):
        @pl.when(z + dlt >= NZ)
        def _():
            za_s[dlt - 1] = jnp.zeros((dim, dim), F32)
            zc_s[dlt - 1] = jnp.zeros((dim, dim), F32)

    for load in loads:
        load.wait()
    turned = bt_ref[...].T
    for j in range(per):
        b_ref[pl.ds(j, tok, stride=per), :] = turned[:, j * heads:(j + 1) * heads]
    q = q_ref[...].astype(F32)
    k = k_ref[...].astype(F32)
    rq = lax.rsqrt(jnp.sum(q * q, axis=-1, keepdims=True) + EPS)
    rk = lax.rsqrt(jnp.sum(k * k, axis=-1, keepdims=True) + EPS)
    rq_s[...] = rq
    rk_s[...] = rk
    qu_s[...] = q * rq
    ku_s[...] = k * rk
    vf_s[...] = v_ref[...].astype(F32)
    dof_s[...] = do_ref[...].astype(F32)

    def of_head(ref, h, rows):
        return ref[pl.ds(h, rows, stride=heads), :]

    half = steps // 2
    base = 16
    blocks = half // base
    lane16 = lax.broadcasted_iota(jnp.int32, (base, half), 1) // base
    packed = []
    for h in range(heads):
        ku = of_head(ku_s, h, steps)
        b = b_ref[:, h:h + 1]
        low = jnp.where(col_i < row_i, mm(ku, ku, 1, 1) * b, 0.0)
        low_s[h] = low
        for part in range(2):
            tri = low[part * half:(part + 1) * half, part * half:(part + 1) * half]
            diag = jnp.zeros((base, half), F32)
            for i in range(blocks):
                diag = jnp.where(lane16 == i, tri[i * base:(i + 1) * base], diag)
            packed.append(diag)
    packed = jnp.concatenate(packed, axis=0)
    rows = packed.shape[0]
    lane = lax.broadcasted_iota(jnp.int32, (rows, half), 1)
    row = lax.broadcasted_iota(jnp.int32, (rows, half), 0)
    inv = jnp.where(row % base == lane % base, 1.0, 0.0)
    for step in range(base - 1):
        column = jnp.take_along_axis(packed, (lane // base) * base + step, axis=1)
        pivot = inv.reshape(rows // base, base, half)[:, step:step + 1, :]
        pivot = jnp.broadcast_to(pivot, (rows // base, base, half)).reshape(rows, half)
        inv = inv - column * pivot
    quads = [(h, part) for h in range(heads) for part in range(2)]
    for n, (h, part) in enumerate(quads):
        mine = inv[n * base:(n + 1) * base]
        n_s[h, part * half:(part + 1) * half, part * half:(part + 1) * half] = jnp.concatenate(
            [jnp.where(lane16 == i, mine, 0.0) for i in range(blocks)], axis=0
        )
        if part:
            n_s[h, 0:half, half:steps] = jnp.zeros((half, half), F32)
    sub_i, sub_j = row_i[:half, :half], col_i[:half, :half]
    size = base
    while size < half:
        band = (sub_i // (2 * size) == sub_j // (2 * size)) & (sub_i // size != sub_j // size)
        firsts = {}
        for h, part in quads:
            at = pl.ds(part * half, half)
            parts = split(n_s[h, at, at])
            firsts[h, part] = parts, mms(split(low_s[h, at, at]), parts)
        for h, part in quads:
            at = pl.ds(part * half, half)
            parts, first = firsts[h, part]
            n_s[h, at, at] = n_s[h, at, at] - jnp.where(band, mms(parts, split(first)), 0.0)
        size *= 2
    firsts = [mm(low_s[h, half:steps, 0:half], n_s[h, 0:half, 0:half]) for h in range(heads)]
    for h in range(heads):
        n_s[h, half:steps, 0:half] = -mm(n_s[h, half:steps, half:steps], firsts[h])
    for h in range(heads):
        ku = of_head(ku_s, h, steps)
        b = b_ref[:, h:h + 1]
        wu_s[h] = mm(n_s[h], jnp.concatenate([b * ku, b * of_head(vf_s, h, steps)], axis=1))
    for h in range(heads):
        ab = mm(of_head(ku_s, h, steps).T, wu_s[h])
        ab_s[h, 0] = eye_dim - ab[:, :dim]
        ab_s[h, 1] = ab[:, dim:]

    def fill_forward():
        for h in range(heads):
            ku = of_head(ku_s, h, steps)
            qu = of_head(qu_s, h, tok)
            sc = jnp.where(visible, mm(qu, ku, 1, 1), 0.0)
            ro = mm(sc, wu_s[h])
            r = qu - ro[:, :dim]
            r_s[h] = r
            rt_s[h] = r.T
            ol_s[h] = ro[:, dim:]
            sct_s[h] = sc.T
            nt = n_s[h].T
            nt_s[h] = nt
            nk_s[h] = mm(nt, ku)

    def fill_backward():
        for h in range(heads):
            ku = of_head(ku_s, h, steps)
            adj = adj_s[h]
            m_do = jnp.where(visible, mm(adj, p_s[h], 1, 1), 0.0)
            dq = mm(adj, sin_s[h], 1, 1) + mm(m_do, ku)
            dq_s[pl.ds(h, tok, stride=heads), :] = dq
            dk1_s[h] = mm(m_do.T, of_head(qu_s, h, tok))
            g0_s[h] = mm(nt_s[h], mm(sct_s[h], adj))
        out_ref[...] = of_s[...].astype(BF16)
        dq_ref[...] = unit_pullback(dq_s[...], qu_s[...], rq_s[...]).astype(BF16)

    pl.semaphore_wait(barrier, count)

    other = 1 - c
    pair = dev(z, y, other)
    send = {}
    for j in range(2):
        send["pair", j] = remote(
            ab_s.at[2 * other + j], pair_s.at[j], send_sem.at[j], pair_sem.at[j], pair
        )
        send["pair", j].start()
    for j in range(2):
        arrived(pair_s.at[j], pair_sem.at[j])
        mine = ab_s[2 * c + j]
        theirs = pair_s[j]
        first = jnp.where(c == 0, mine, theirs)
        second = jnp.where(c == 0, theirs, mine)
        both = mm(second[0], jnp.concatenate([first[0], first[1]], axis=1))
        comp_s[j, 0] = both[:, :dim]
        comp_s[j, 1] = both[:, dim:] + second[1]
        head = 2 * c + j
        here = (c == 1) & (y == head)

        @pl.when(here)
        def _():
            pltpu.make_async_copy(comp_s.at[j], own_s.at[y], own_sem.at[y]).start()

        @pl.when(jnp.logical_not(here))
        def _():
            remote(comp_s.at[j], own_s.at[y], send_sem.at[2 + j], own_sem.at[y], dev(z, head, 1)).start()

    @pl.when(c == 1)
    def _():
        low_core = dev(z, y, 0)
        arrived(own_s.at[0], own_sem.at[0])
        x = jnp.concatenate([own_s[0, 0], own_s[0, 1]], axis=1)
        phi_s[0] = x[:, :dim]
        beta_s[0] = x[:, dim:]
        for i in range(1, NY):
            arrived(own_s.at[i], own_sem.at[i])
            x = mm(own_s[i, 0], x)
            x = jnp.concatenate([x[:, :dim], x[:, dim:] + own_s[i, 1]], axis=1)
            phi_s[i] = x[:, :dim]
            beta_s[i] = x[:, dim:]
        comp_row = own_s.at[0]
        comp_row[0] = x[:, :dim]
        comp_row[1] = x[:, dim:]
        for dlt in range(NG - 1, 0, -1):
            @pl.when(rank + dlt < NG)
            def _():
                zab_copy(dlt).start()

        @pl.when((group == 0) & (rank > 0))
        def _():
            zback_copy().start()

        for i in range(1, NY):
            remote(own_s.at[i, 0], aown_s.at[i], send_sem.at[20 + i], aown_sem.at[i], low_core).start()
            remote(phi_s.at[i - 1], phi0_s.at[i], send_sem.at[24 + i], aown_sem.at[NY + i], low_core).start()
        fill_forward()

        @pl.when(rank == 0)
        def _():
            x_s[:, :dim] = eye_dim
            x_s[:, dim:] = jnp.zeros((dim, dim), F32)

        for i in range(NG - 1):
            @pl.when(rank > i)
            def _():
                arrived(zab_s.at[i], zab_sem.at[i])
                if i == 0:
                    x_s[:, :dim] = zab_s[0, 0]
                    x_s[:, dim:] = zab_s[0, 1]
                else:
                    nxt = mm(zab_s[i, 0], x_s[...])
                    x_s[:, :dim] = nxt[:, :dim]
                    x_s[:, dim:] = nxt[:, dim:] + zab_s[i, 1]

        @pl.when((group == 0) & (rank == NG - 1))
        def _():
            middle_s[...] = mm(own_s[0, 0], x_s[:, dim:]) + own_s[0, 1]
            for n in range(2):
                middle_copy(n).start()

        @pl.when((group == 0) & (rank == 0))
        def _():
            state = own_s[0, 1]
            for i in range(1, NG):
                arrived(zab_s.at[i], zab_sem.at[i])
                state = mm(zab_s[i, 0], state) + zab_s[i, 1]
            middle_s[...] = state
            for n in range(2):
                middle_copy(n).start()

        sout_s[0] = x_s[:, dim:]
        later = mm(jnp.concatenate([phi_s[i] for i in range(NY - 1)], axis=0), x_s[...])
        for i in range(1, NY):
            sout_s[i] = later[(i - 1) * dim:i * dim, dim:] + beta_s[i - 1]

        @pl.when(group == 1)
        def _():
            arrived(mid_s, mid_sem)
            stack = jnp.concatenate([x_s[:, :dim], later[:, :dim]], axis=0)
            more = mm(stack, mid_s[...])
            for i in range(NY):
                sout_s[i] = sout_s[i] + more[i * dim:(i + 1) * dim]

        for i in range(NY):
            remote(sout_s.at[i], sin_s.at[y], send_sem.at[28 + i], sin_sem.at[y], dev(z, i, 0)).start()
        for dlt in range(1, NZ):
            @pl.when(z >= dlt)
            def _():
                remote(
                    phi_s.at[NY - 1], za_s.at[dlt - 1], send_sem.at[12 + dlt], za_sem.at[dlt - 1],
                    dev(z - dlt, y, 0),
                ).start()
        for h in range(heads):
            arrived(sin_s.at[h], sin_sem.at[h])

    @pl.when(c == 0)
    def _():
        fill_forward()
        for i in range(1, NY):
            arrived(aown_s.at[i], aown_sem.at[i])
            arrived(phi0_s.at[i], aown_sem.at[NY + i])
        psi_s[NY - 2] = aown_s[NY - 1]
        for i in range(NY - 3, -1, -1):
            psi_s[i] = mm(psi_s[i + 1], aown_s[i + 1])
        for h in range(heads):
            arrived(sin_s.at[h], sin_sem.at[h])
            s1_s[h] = mm(ab_s[h, 0], sin_s[h]) + ab_s[h, 1]
            remote(s1_s.at[h], sin_s.at[h], send_sem.at[28 + h], sin_sem.at[h], pair).start()

    gain = g_ref[...]
    gain_part = jnp.zeros((1, dim), F32)
    for h in range(heads):
        both = mm(jnp.concatenate([r_s[h], wu_s[h, :, :dim]], axis=0), sin_s[h])
        ol_s[h] = ol_s[h] + both[:tok]
        p_s[h] = wu_s[h, :, dim:] - both[tok:]
    for h in range(heads):
        o = ol_s[h]
        inv_rms = lax.rsqrt(jnp.mean(o * o, axis=-1, keepdims=True) + EPS)
        normal = o * inv_rms
        grad = of_head(dof_s, h, tok)
        of_s[pl.ds(h, tok, stride=heads), :] = gain * normal
        gain_part = gain_part + jnp.sum(grad * normal, axis=0, keepdims=True)
        scaled = grad * gain
        adj_s[h] = inv_rms * (scaled - normal * jnp.mean(scaled * normal, axis=-1, keepdims=True))
    for h in range(heads):
        c_s[h] = mm(rt_s[h], adj_s[h])

        @pl.when(c == 1)
        def _():
            remote(c_s.at[h], cpair_s.at[h], send_sem.at[32 + h], cpair_sem.at[h], pair).start()

    gpart_s[...] = jnp.broadcast_to(gain_part, (8, dim))
    me8 = y * NC + c
    n_g = 0
    gsends = []
    for d in range(1, NY * NC):
        to = (me8 + d) % (NY * NC)
        gsends.append(remote(
            gpart_s, grow_s.at[me8], gsend_sem.at[n_g], grow_sem.at[d - 1], dev(z, to // NC, to % NC)))
        gsends[-1].start()
        n_g += 1
    grow_s[me8] = gpart_s[...]

    def gain_along_z():
        for d in range(1, NY * NC):
            fr = (me8 + NY * NC - d) % (NY * NC)
            arrived(grow_s.at[fr], grow_sem.at[d - 1])
        gsum_s[0] = jnp.sum(grow_s[...], axis=0)
        for d in range(1, NZ):
            gz_copy(d).start()
        gz_s[z] = gsum_s[0]

    def gz_copy(d):
        return remote(
            gsum_s.at[0], gz_s.at[z], gsend_sem.at[6 + d], gz_sem.at[d - 1], dev((z + d) % NZ, y, c)
        )

    def gx_copy(d):
        return remote(
            gsum_s.at[1], gx_s.at[xpos], gsend_sem.at[13 + d], gx_sem.at[d - 1], {"head": (xpos + d) % 4}
        )

    @pl.when(c == 0)
    def _():
        for h in range(heads):
            arrived(cpair_s.at[h], cpair_sem.at[h])
            cc_s[h] = mm(ab_s[h, 0], cpair_s[h], 0, 0) + c_s[h]

            @pl.when(y == h)
            def _():
                pltpu.make_async_copy(cc_s.at[h], cown_s.at[h], cown_sem.at[h]).start()

            @pl.when(y != h)
            def _():
                remote(cc_s.at[h], cown_s.at[y], send_sem.at[32 + h], cown_sem.at[y], dev(z, h, 0)).start()
        for i in range(NY):
            arrived(cown_s.at[i], cown_sem.at[i])
        left = jnp.concatenate([phi0_s[i] for i in range(1, NY)], axis=0)
        right = jnp.concatenate([cown_s[i] for i in range(1, NY)], axis=0)
        crow_s[...] = cown_s[0] + mm(left, right, 0, 0)
        for dlt in range(NZ - 1, 0, -1):
            @pl.when(z >= dlt)
            def _():
                remote(
                    crow_s, zc_s.at[dlt - 1], send_sem.at[4 + dlt], zc_sem.at[dlt - 1], dev(z - dlt, y, 0)
                ).start()
        gam_s[NY - 2] = cown_s[NY - 1]
        for i in range(NY - 3, -1, -1):
            gam_s[i] = mm(aown_s[i + 1], gam_s[i + 1], 0, 0) + cown_s[i + 1]
        gain_along_z()
        fill_backward()
        for dlt in range(1, NZ - 1):
            @pl.when(z + dlt < NZ)
            def _():
                arrived(za_s.at[dlt - 1], za_sem.at[dlt - 1])

            theta_s[dlt] = za_s[0] if dlt == 1 else mm(za_s[dlt - 1], theta_s[dlt - 1])

        @pl.when(z + NZ - 1 < NZ)
        def _():
            arrived(za_s.at[NZ - 2], za_sem.at[NZ - 2])

        for dlt in range(NZ - 1, 0, -1):
            @pl.when(z + dlt < NZ)
            def _():
                arrived(zc_s.at[dlt - 1], zc_sem.at[dlt - 1])
        left = jnp.concatenate([theta_s[i] for i in range(1, NZ - 1)], axis=0)
        right = jnp.concatenate([zc_s[i] for i in range(1, NZ - 1)], axis=0)
        d_row = zc_s[0] + mm(left, right, 0, 0)
        dsend_s[NY - 1] = d_row
        for i in range(NY - 1):
            dsend_s[i] = mm(psi_s[i], d_row, 0, 0) + gam_s[i]
        for i in range(NY):
            remote(dsend_s.at[i], dout_s.at[y], send_sem.at[12 + i], dout_sem.at[y], dev(z, i, 1)).start()
        for h in range(heads):
            arrived(dout_s.at[h], dout_sem.at[h])

    @pl.when(c == 1)
    def _():
        gain_along_z()
        fill_backward()
        for h in range(heads):
            arrived(dout_s.at[h], dout_sem.at[h])
            d0_s[h] = mm(ab_s[h, 0], dout_s[h], 0, 0) + c_s[h]
            remote(d0_s.at[h], dout_s.at[h], send_sem.at[36 + h], dout_sem.at[h], pair).start()

    for d in range(1, NZ):
        arrived(gz_s.at[(z + NZ - d) % NZ], gz_sem.at[d - 1])
    gsum_s[1] = jnp.sum(gz_s[...], axis=0)
    for d in range(1, 4):
        gx_copy(d).start()
    gx_s[xpos] = gsum_s[1]

    lane = lax.broadcasted_iota(jnp.int32, (steps, heads), 1)
    db_all = jnp.zeros((steps, heads), F32)
    for h in range(heads):
        gm = g0_s[h] + mm(nk_s[h], dout_s[h])
        b = b_ref[:, h:h + 1]
        dv = b * gm
        dv_s[h] = dv
        dvf_s[pl.ds(h, steps, stride=heads), :] = dv
        db = jnp.sum(gm * p_s[h], axis=-1, keepdims=True) / b
        db_all = db_all + jnp.where(lane == h, db, 0.0)
    db_s[...] = db_all
    for h in range(heads):
        hm = jnp.where(col_i < row_i, mm(dv_s[h], p_s[h], 1, 1), 0.0)
        low_s[h] = hm + hm.T
    for h in range(heads):
        dk = dk1_s[h] + mm(
            jnp.concatenate([p_s[h], dv_s[h]], axis=1), jnp.concatenate([dout_s[h], -sin_s[h]], axis=1), 1, 1
        ) - mm(low_s[h], of_head(ku_s, h, steps))
        dk_s[pl.ds(h, steps, stride=heads), :] = dk
    db_ref[...] = jnp.concatenate([db_s[pl.ds(j, tok, stride=per), :] for j in range(per)], axis=1).T
    dk_ref[...] = unit_pullback(dk_s[...], ku_s[...], rk_s[...]).astype(BF16)
    dv_ref[...] = dvf_s[...].astype(BF16)

    for d in range(1, 4):
        arrived(gx_s.at[(xpos + 4 - d) % 4], gx_sem.at[d - 1])
    dg_ref[...] = jnp.sum(gx_s[...], axis=0)[0:1]

    for j in range(2):
        send["pair", j].wait_send()
        head = 2 * c + j

        @pl.when(jnp.logical_not((c == 1) & (y == head)))
        def _():
            remote(comp_s.at[j], own_s.at[y], send_sem.at[2 + j], own_sem.at[y], dev(z, head, 1)).wait_send()

    def left(src, sem):
        remote(src, src, sem, sem, pair).wait_send()

    @pl.when(c == 1)
    def _():
        for dlt in range(1, NG):
            @pl.when(rank + dlt < NG)
            def _():
                zab_copy(dlt).wait_send()

        @pl.when((group == 0) & (rank > 0))
        def _():
            zback_copy().wait_send()

        @pl.when((z == 0) | (z == NG - 1))
        def _():
            for n in range(2):
                middle_copy(n).wait_send()

        for dlt in range(1, NZ):
            @pl.when(z >= dlt)
            def _():
                left(phi_s.at[NY - 1], send_sem.at[12 + dlt])
        for i in range(1, NY):
            left(own_s.at[i, 0], send_sem.at[20 + i])
            left(phi_s.at[i - 1], send_sem.at[24 + i])
        for i in range(NY):
            left(sout_s.at[i], send_sem.at[28 + i])
            left(c_s.at[i], send_sem.at[32 + i])
            left(d0_s.at[i], send_sem.at[36 + i])

    @pl.when(c == 0)
    def _():
        for h in range(heads):
            left(s1_s.at[h], send_sem.at[28 + h])

            @pl.when(y != h)
            def _():
                left(cc_s.at[h], send_sem.at[32 + h])
        for dlt in range(1, NZ):
            @pl.when(z >= dlt)
            def _():
                left(crow_s, send_sem.at[4 + dlt])
        for i in range(NY):
            left(dsend_s.at[i], send_sem.at[12 + i])
    for copy in gsends:
        copy.wait_send()
    for d in range(1, NZ):
        gz_copy(d).wait_send()
    for d in range(1, 4):
        gx_copy(d).wait_send()


def local(queries, keys, values, betas, gain, out_grad):
    tok, heads, dim = queries.shape
    per = keys.shape[1]
    steps = tok * per
    f = lambda *s: pltpu.VMEM(s, F32)
    dma = pltpu.SemaphoreType.DMA
    vmem = pl.BlockSpec(memory_space=pltpu.VMEM)
    b16 = lambda *sh: pltpu.VMEM(sh, BF16)
    scratch = [
        b16(tok * heads, dim), b16(steps * heads, dim), b16(steps * heads, dim), f(per * heads, tok), f(1, dim),
        b16(tok * heads, dim), f(steps, heads), f(steps, heads), dma((6,)),
        f(steps * heads, dim), f(tok * heads, dim), f(steps * heads, dim), f(tok * heads, dim),
        f(steps * heads, 1), f(tok * heads, 1), f(heads, steps, steps), f(heads, steps, steps),
        f(heads, steps, steps), f(heads, steps, dim), f(heads, steps, 2 * dim), f(heads, steps, tok),
        f(heads, tok, dim), f(heads, dim, tok), f(heads, tok, dim), f(heads, steps, dim), f(heads, tok, dim),
        f(heads, steps, dim), f(heads, steps, dim), f(tok * heads, dim), f(tok * heads, dim),
        f(steps * heads, dim), f(steps * heads, dim), f(heads, steps, dim),
        f(heads, 2, dim, dim), f(2, 2, dim, dim), f(2, 2, dim, dim), f(NY, 2, dim, dim),
        f(NY, dim, dim), f(NY, dim, dim), f(NG, 2, dim, dim), f(NZ - 1, dim, dim),
        f(NY, dim, dim), f(heads, dim, dim), f(heads, dim, dim),
        f(NY, dim, dim), f(NY, dim, dim), f(NZ - 1, dim, dim), f(NY - 1, dim, dim), f(heads, dim, dim),
        f(heads, dim, dim), f(heads, dim, dim), f(NY, dim, dim), f(dim, dim), f(NZ - 1, dim, dim),
        f(NY - 1, dim, dim), f(NY, dim, dim), f(heads, dim, dim), f(heads, dim, dim),
        f(8, dim), f(NY * NC, 8, dim), f(NZ, 8, dim), f(4, 8, dim), f(2, 8, dim),
        f(dim, 2 * dim), f(dim, dim), f(dim, dim), dma,
        dma((40,)), dma((2,)), dma((NY,)), dma((NG,)), dma((NZ - 1,)), dma((heads,)), dma((2 * NY,)),
        dma((heads,)), dma((NY,)), dma((NZ - 1,)), dma((heads,)),
        dma((24,)), dma((NY * NC - 1,)), dma((NZ - 1,)), dma((3,)),
    ]
    outs = pl.pallas_call(
        kernel,
        out_shape=(
            jax.ShapeDtypeStruct((tok * heads, dim), BF16),
            jax.ShapeDtypeStruct((tok * heads, dim), BF16),
            jax.ShapeDtypeStruct((steps * heads, dim), BF16),
            jax.ShapeDtypeStruct((steps * heads, dim), BF16),
            jax.ShapeDtypeStruct((per * heads, tok), F32),
            jax.ShapeDtypeStruct((1, dim), F32),
        ),
        in_specs=[pl.BlockSpec(memory_space=pltpu.HBM)] * 6,
        out_specs=(vmem,) * 6,
        scratch_shapes=scratch,
        compiler_params=pltpu.CompilerParams(
            collective_id=0, has_side_effects=True, vmem_limit_bytes=32 * 1024 * 1024
        ),
        name="delta_product",
    )(*[
        pltpu.with_memory_space_constraint(a, pltpu.HBM)
        for a in (
            queries.reshape(tok * heads, dim),
            keys.reshape(steps * heads, dim),
            values.reshape(steps * heads, dim),
            betas.transpose(1, 2, 0).reshape(per * heads, tok),
            gain.reshape(1, dim),
            out_grad.reshape(tok * heads, dim),
        )
    ])
    out, dq, dk, dv, db, dg = pl.pallas_call(
        store,
        out_shape=tuple(jax.ShapeDtypeStruct(a.shape, a.dtype) for a in outs),
        in_specs=[vmem] * 6,
        out_specs=(pl.BlockSpec(memory_space=pl.ANY),) * 6,
        scratch_shapes=[dma((6,))],
        compiler_params=pltpu.CompilerParams(vmem_limit_bytes=4 * 1024 * 1024),
        name="store",
    )(*outs)
    return (
        out.reshape(queries.shape), dq.reshape(queries.shape), dk.reshape(keys.shape), dv.reshape(values.shape),
        db.reshape(per, heads, tok).transpose(2, 0, 1), dg.reshape(dim),
    )


def store(*refs):
    sem = refs[-1]
    copies = [pltpu.make_async_copy(refs[n], refs[6 + n], sem.at[n]) for n in range(6)]
    for copy in copies:
        copy.start()
    for copy in copies:
        copy.wait()


def solution(mesh):
    return jax.shard_map(
        local,
        mesh=mesh,
        in_specs=(
            P("seq", "head", None),
            P("seq", None, "head", None),
            P("seq", None, "head", None),
            P("seq", None, "head"),
            P(),
            P("seq", "head", None),
        ),
        out_specs=(
            P("seq", "head", None),
            P("seq", "head", None),
            P("seq", None, "head", None),
            P("seq", None, "head", None),
            P("seq", None, "head"),
            P(),
        ),
        check_vma=False,
    )
```

```python
import functools

import jax
import jax.numpy as jnp
from jax import lax
from jax.experimental import pallas as pl
from jax.experimental.pallas import tpu as pltpu
from jax.sharding import PartitionSpec as P

EPS = 1e-06
F32 = jnp.float32
BF16 = jnp.bfloat16
MESH = pl.DeviceIdType.MESH
NY = 4
NZ = 8
NG = 4
NC = 2


def split(x):
    hi = x.astype(BF16)
    lo = (x - hi.astype(F32)).astype(BF16)
    return hi, lo


def dot(a, b, dims):
    return lax.dot_general(a, b, (dims, ((), ())), preferred_element_type=F32)


def mms(a, b, ca=1, cb=0):
    left = jnp.concatenate([a[0], a[1], a[0]], axis=ca)
    right = jnp.concatenate([b[0], b[0], b[1]], axis=cb)
    return dot(left, right, ((ca,), (cb,)))


def mm(a, b, ca=1, cb=0):
    return mms(split(a), split(b), ca, cb)


def iotas(rows, cols):
    return (
        lax.broadcasted_iota(jnp.int32, (rows, cols), 0),
        lax.broadcasted_iota(jnp.int32, (rows, cols), 1),
    )


def unit_pullback(d_unit, unit, inverse):
    return (d_unit - unit * jnp.sum(unit * d_unit, axis=-1, keepdims=True)) * inverse


def kernel(
    q_hbm, k_hbm, v_hbm, b_hbm, g_hbm, do_hbm,
    out_ref, dq_ref, dk_ref, dv_ref, db_ref, dg_ref,
    q_ref, k_ref, v_ref, bt_ref, g_ref, do_ref, b_ref, db_s, in_sem,
    ku_s, qu_s, vf_s, dof_s, rk_s, rq_s, low_s, n_s, nt_s, nk_s, wu_s, sct_s, r_s, rt_s, ol_s, p_s, adj_s,
    g0_s, dk1_s, of_s, dq_s, dk_s, dvf_s, dv_s,
    ab_s, pair_s, comp_s, own_s, phi_s, beta_s, zab_s, za_s, sout_s, sin_s, s1_s,
    aown_s, phi0_s, theta_s, psi_s, c_s, cpair_s, cc_s, cown_s, crow_s, zc_s, gam_s, dsend_s, dout_s, d0_s,
    gpart_s, grow_s, gz_s, gx_s, gsum_s, xa_s, xb_s, middle_s, mid_s, mid_sem,
    send_sem, pair_sem, own_sem, zab_sem, za_sem, sin_sem, aown_sem, cpair_sem, cown_sem, zc_sem, dout_sem,
    gsend_sem, grow_sem, gz_sem, gx_sem,
):
    steps, heads = b_ref.shape
    per = steps // (q_ref.shape[0] // heads)
    tok = q_ref.shape[0] // heads
    dim = q_ref.shape[1]
    seq = lax.axis_index("seq")
    xpos = lax.axis_index("head")
    z = seq // (NY * NC)
    y = (seq // NC) % NY
    c = seq % NC

    def dev(zz, yy, cc):
        return {"seq": zz * (NY * NC) + yy * NC + cc}

    barrier = pltpu.get_barrier_semaphore()
    count = 0
    for dy in range(NY):
        for dc in range(NC):
            if dy or dc:
                pl.semaphore_signal(
                    barrier, inc=1, device_id=dev(z, (y + dy) % NY, (c + dc) % NC), device_id_type=MESH
                )
                count += 1
    for dz in range(1, NZ):
        for dc in range(NC):
            pl.semaphore_signal(
                barrier, inc=1, device_id=dev((z + dz) % NZ, y, (c + dc) % NC), device_id_type=MESH
            )
            count += 1
    for dx in range(1, 4):
        pl.semaphore_signal(
            barrier, inc=1, device_id={"head": (xpos + dx) % 4}, device_id_type=MESH
        )
        count += 1

    loads = [
        pltpu.make_async_copy(src, dst, in_sem.at[n])
        for n, (src, dst) in enumerate([
            (k_hbm, k_ref), (b_hbm, bt_ref), (v_hbm, v_ref), (q_hbm, q_ref), (do_hbm, do_ref), (g_hbm, g_ref)
        ])
    ]
    for load in loads:
        load.start()

    def remote(src, dst, ssem, rsem, target):
        return pltpu.make_async_remote_copy(
            src_ref=src, dst_ref=dst, send_sem=ssem, recv_sem=rsem, device_id=target, device_id_type=MESH
        )

    def arrived(dst, rsem):
        pltpu.make_async_copy(dst, dst, rsem).wait()

    group = z // NG
    rank = z % NG

    near_first = [(y + d) % NY for d in (0, 1, 3, 2)]

    def own_copy(j, part):
        head = 2 * c + j
        return remote(
            comp_s.at[j, part], own_s.at[y, part], send_sem.at[2 + j if part == 0 else 45 + j],
            own_sem.at[part * NY + y], dev(z, head, 1),
        )

    def own_here(j):
        return (c == 1) & (y == 2 * c + j)

    def own_start(j, part):
        @pl.when(own_here(j))
        def _():
            pltpu.make_async_copy(
                comp_s.at[j, part], own_s.at[y, part], own_sem.at[part * NY + y]
            ).start()

        @pl.when(jnp.logical_not(own_here(j)))
        def _():
            own_copy(j, part).start()

    def zab_copy(dlt, part, back=False):
        src = (beta_s if part else phi_s).at[NY - 1]
        to = 0 if back else z + dlt
        sem = (8, 44)[part] if back else (4, 40)[part] + dlt
        return remote(
            src, zab_s.at[rank, part], send_sem.at[sem], zab_sem.at[part * NG + rank], dev(to, y, 1)
        )

    def zab_each(part, act):
        for dlt in range(NG - 1, 0, -1):
            @pl.when((rank + dlt < NG) & ((z > 0) | (part == 1)))
            def _():
                act(zab_copy(dlt, part))

        @pl.when((group == 0) & (rank > 0))
        def _():
            act(zab_copy(0, part, True))

    def middle_copy(n):
        to = jnp.where(rank == 0, NZ - 1 - n, NG + n)
        return remote(middle_s, mid_s, send_sem.at[9 + n], mid_sem, dev(to, y, 1))

    row_i, col_i = iotas(steps, steps)
    tok_i, step_i = iotas(tok, steps)
    visible = step_i <= 2 * tok_i + 1
    eye = (row_i == col_i).astype(F32)
    eye_dim = eye[:dim, :dim]

    for dlt in range(1, NZ):
        @pl.when(z + dlt >= NZ)
        def _():
            za_s[dlt - 1] = jnp.zeros((dim, dim), F32)
            zc_s[dlt - 1] = jnp.zeros((dim, dim), F32)

    for load in loads:
        load.wait()
    turned = bt_ref[...].T
    for j in range(per):
        b_ref[pl.ds(j, tok, stride=per), :] = turned[:, j * heads:(j + 1) * heads]
    q = q_ref[...].astype(F32)
    k = k_ref[...].astype(F32)
    rq = lax.rsqrt(jnp.sum(q * q, axis=-1, keepdims=True) + EPS)
    rk = lax.rsqrt(jnp.sum(k * k, axis=-1, keepdims=True) + EPS)
    rq_s[...] = rq
    rk_s[...] = rk
    qu_s[...] = q * rq
    ku_s[...] = k * rk
    vf_s[...] = v_ref[...].astype(F32)
    dof_s[...] = do_ref[...].astype(F32)

    def of_head(ref, h, rows):
        return ref[pl.ds(h, rows, stride=heads), :]

    half = steps // 2
    base = 16
    blocks = half // base
    lane16 = lax.broadcasted_iota(jnp.int32, (base, half), 1) // base
    packed = []
    for h in range(heads):
        ku = of_head(ku_s, h, steps)
        b = b_ref[:, h:h + 1]
        low = jnp.where(col_i < row_i, mm(ku, ku, 1, 1) * b, 0.0)
        low_s[h] = low
        for part in range(2):
            tri = low[part * half:(part + 1) * half, part * half:(part + 1) * half]
            diag = jnp.zeros((base, half), F32)
            for i in range(blocks):
                diag = jnp.where(lane16 == i, tri[i * base:(i + 1) * base], diag)
            packed.append(diag)
    packed = jnp.concatenate(packed, axis=0)
    rows = packed.shape[0]
    lane = lax.broadcasted_iota(jnp.int32, (rows, half), 1)
    row = lax.broadcasted_iota(jnp.int32, (rows, half), 0)
    inv = jnp.where(row % base == lane % base, 1.0, 0.0)
    for step in range(base - 1):
        column = jnp.take_along_axis(packed, (lane // base) * base + step, axis=1)
        pivot = inv.reshape(rows // base, base, half)[:, step:step + 1, :]
        pivot = jnp.broadcast_to(pivot, (rows // base, base, half)).reshape(rows, half)
        inv = inv - column * pivot
    quads = [(h, part) for h in range(heads) for part in range(2)]
    for n, (h, part) in enumerate(quads):
        mine = inv[n * base:(n + 1) * base]
        n_s[h, part * half:(part + 1) * half, part * half:(part + 1) * half] = jnp.concatenate(
            [jnp.where(lane16 == i, mine, 0.0) for i in range(blocks)], axis=0
        )
        if part:
            n_s[h, 0:half, half:steps] = jnp.zeros((half, half), F32)
    sub_i, sub_j = row_i[:half, :half], col_i[:half, :half]
    size = base
    while size < half:
        band = (sub_i // (2 * size) == sub_j // (2 * size)) & (sub_i // size != sub_j // size)
        firsts = {}
        for h, part in quads:
            at = pl.ds(part * half, half)
            parts = split(n_s[h, at, at])
            firsts[h, part] = parts, mms(split(low_s[h, at, at]), parts)
        for h, part in quads:
            at = pl.ds(part * half, half)
            parts, first = firsts[h, part]
            n_s[h, at, at] = n_s[h, at, at] - jnp.where(band, mms(parts, split(first)), 0.0)
        size *= 2
    firsts = [mm(low_s[h, half:steps, 0:half], n_s[h, 0:half, 0:half]) for h in range(heads)]
    for h in range(heads):
        n_s[h, half:steps, 0:half] = -mm(n_s[h, half:steps, half:steps], firsts[h])
    for h in range(heads):
        ku = of_head(ku_s, h, steps)
        b = b_ref[:, h:h + 1]
        wu_s[h] = mm(n_s[h], jnp.concatenate([b * ku, b * of_head(vf_s, h, steps)], axis=1))
    for h in range(heads):
        ab = mm(of_head(ku_s, h, steps).T, wu_s[h])
        ab_s[h, 0] = eye_dim - ab[:, :dim]
        ab_s[h, 1] = ab[:, dim:]

    def fill_forward():
        for h in range(heads):
            ku = of_head(ku_s, h, steps)
            qu = of_head(qu_s, h, tok)
            sc = jnp.where(visible, mm(qu, ku, 1, 1), 0.0)
            ro = mm(sc, wu_s[h])
            r = qu - ro[:, :dim]
            r_s[h] = r
            rt_s[h] = r.T
            ol_s[h] = ro[:, dim:]
            sct_s[h] = sc.T
            nt = n_s[h].T
            nt_s[h] = nt
            nk_s[h] = mm(nt, ku)

    def fill_backward():
        for h in range(heads):
            ku = of_head(ku_s, h, steps)
            adj = adj_s[h]
            m_do = jnp.where(visible, mm(adj, p_s[h], 1, 1), 0.0)
            dq = mm(adj, sin_s[h], 1, 1) + mm(m_do, ku)
            dq_s[pl.ds(h, tok, stride=heads), :] = dq
            dk1_s[h] = mm(m_do.T, of_head(qu_s, h, tok))
            g0_s[h] = mm(nt_s[h], mm(sct_s[h], adj))
        out_ref[...] = of_s[...].astype(BF16)
        dq_ref[...] = unit_pullback(dq_s[...], qu_s[...], rq_s[...]).astype(BF16)

    pl.semaphore_wait(barrier, count)

    other = 1 - c
    pair = dev(z, y, other)
    send = {}
    for j in range(2):
        send["pair", j] = remote(
            ab_s.at[2 * other + j], pair_s.at[j], send_sem.at[j], pair_sem.at[j], pair
        )
        send["pair", j].start()
    for j in range(2):
        arrived(pair_s.at[j], pair_sem.at[j])
        mine = ab_s[2 * c + j]
        theirs = pair_s[j]
        first = jnp.where(c == 0, mine, theirs)
        second = jnp.where(c == 0, theirs, mine)
        both = mm(second[0], jnp.concatenate([first[0], first[1]], axis=1))
        comp_s[j, 0] = both[:, :dim]
        comp_s[j, 1] = both[:, dim:] + second[1]
        own_start(j, 0)
    for j in range(2):
        own_start(j, 1)

    @pl.when(c == 1)
    def _():
        low_core = dev(z, y, 0)
        for i in range(NY):
            arrived(own_s.at[i, 0], own_sem.at[i])
            phi_s[i] = mm(own_s[i, 0], phi_s[i - 1]) if i else own_s[0, 0]
        zab_each(0, lambda copy: copy.start())
        for i in range(NY):
            arrived(own_s.at[i, 1], own_sem.at[NY + i])
            beta_s[i] = mm(own_s[i, 0], beta_s[i - 1]) + own_s[i, 1] if i else own_s[0, 1]
        zab_each(1, lambda copy: copy.start())

        for i in range(1, NY):
            remote(own_s.at[i, 0], aown_s.at[i], send_sem.at[20 + i], aown_sem.at[i], low_core).start()
            remote(phi_s.at[i - 1], phi0_s.at[i], send_sem.at[24 + i], aown_sem.at[NY + i], low_core).start()
        fill_forward()

        phis = jnp.concatenate([phi_s[i] for i in range(NY - 1)], axis=0)

        @pl.when(group == 1)
        def _():
            @pl.when(rank == 0)
            def _():
                xa_s[0:dim] = eye_dim

            for i in range(NG - 1):
                @pl.when(rank > i)
                def _():
                    arrived(zab_s.at[i, 0], zab_sem.at[i])
                    xa_s[0:dim] = mm(zab_s[i, 0], xa_s[0:dim]) if i else zab_s[0, 0]
            xa_s[dim:] = mm(phis, xa_s[0:dim])

        @pl.when(group == 0)
        def _():
            for i in range(1, NG):
                @pl.when((rank > i) | (rank == 0))
                def _():
                    arrived(zab_s.at[i, 0], zab_sem.at[i])

        @pl.when(rank == 0)
        def _():
            xb_s[...] = jnp.zeros((dim, dim), F32)

        for i in range(NG - 1):
            @pl.when(rank > i)
            def _():
                arrived(zab_s.at[i, 1], zab_sem.at[NG + i])
                xb_s[...] = mm(zab_s[i, 0], xb_s[...]) + zab_s[i, 1] if i else zab_s[0, 1]

        @pl.when((group == 0) & (rank == NG - 1))
        def _():
            middle_s[...] = mm(phi_s[NY - 1], xb_s[...]) + beta_s[NY - 1]
            for n in range(2):
                middle_copy(n).start()

        @pl.when((group == 0) & (rank == 0))
        def _():
            state = beta_s[NY - 1]
            for i in range(1, NG):
                arrived(zab_s.at[i, 1], zab_sem.at[NG + i])
                state = mm(zab_s[i, 0], state) + zab_s[i, 1]
            middle_s[...] = state
            for n in range(2):
                middle_copy(n).start()

        sout_s[0] = xb_s[...]
        later = mm(phis, xb_s[...])
        for i in range(1, NY):
            sout_s[i] = later[(i - 1) * dim:i * dim] + beta_s[i - 1]

        @pl.when(group == 1)
        def _():
            arrived(mid_s, mid_sem)
            more = mm(xa_s[...], mid_s[...])
            for i in range(NY):
                sout_s[i] = sout_s[i] + more[i * dim:(i + 1) * dim]

        for i in near_first[::-1]:
            remote(sout_s.at[i], sin_s.at[y], send_sem.at[28 + i], sin_sem.at[y], dev(z, i, 0)).start()
        for dlt in range(1, NZ):
            @pl.when(z >= dlt)
            def _():
                remote(
                    phi_s.at[NY - 1], za_s.at[dlt - 1], send_sem.at[12 + dlt], za_sem.at[dlt - 1],
                    dev(z - dlt, y, 0),
                ).start()
        for h in range(heads):
            arrived(sin_s.at[h], sin_sem.at[h])

    @pl.when(c == 0)
    def _():
        fill_forward()
        for i in range(1, NY):
            arrived(aown_s.at[i], aown_sem.at[i])
            arrived(phi0_s.at[i], aown_sem.at[NY + i])
        psi_s[NY - 2] = aown_s[NY - 1]
        for i in range(NY - 3, -1, -1):
            psi_s[i] = mm(psi_s[i + 1], aown_s[i + 1])
        for h in near_first:
            arrived(sin_s.at[h], sin_sem.at[h])
            s1_s[h] = mm(ab_s[h, 0], sin_s[h]) + ab_s[h, 1]
            remote(s1_s.at[h], sin_s.at[h], send_sem.at[28 + h], sin_sem.at[h], pair).start()

    gain = g_ref[...]
    gain_part = jnp.zeros((1, dim), F32)
    for h in range(heads):
        both = mm(jnp.concatenate([r_s[h], wu_s[h, :, :dim]], axis=0), sin_s[h])
        ol_s[h] = ol_s[h] + both[:tok]
        p_s[h] = wu_s[h, :, dim:] - both[tok:]
    for h in range(heads):
        o = ol_s[h]
        inv_rms = lax.rsqrt(jnp.mean(o * o, axis=-1, keepdims=True) + EPS)
        normal = o * inv_rms
        grad = of_head(dof_s, h, tok)
        of_s[pl.ds(h, tok, stride=heads), :] = gain * normal
        gain_part = gain_part + jnp.sum(grad * normal, axis=0, keepdims=True)
        scaled = grad * gain
        adj_s[h] = inv_rms * (scaled - normal * jnp.mean(scaled * normal, axis=-1, keepdims=True))
    for h in range(heads):
        c_s[h] = mm(rt_s[h], adj_s[h])

    @pl.when(c == 1)
    def _():
        for h in near_first[::-1]:
            remote(c_s.at[h], cpair_s.at[h], send_sem.at[32 + h], cpair_sem.at[h], pair).start()

    gpart_s[...] = jnp.broadcast_to(gain_part, (8, dim))
    me8 = y * NC + c
    n_g = 0
    gsends = []
    for d in range(1, NY * NC):
        to = (me8 + d) % (NY * NC)
        gsends.append(remote(
            gpart_s, grow_s.at[me8], gsend_sem.at[n_g], grow_sem.at[d - 1], dev(z, to // NC, to % NC)))
        gsends[-1].start()
        n_g += 1
    grow_s[me8] = gpart_s[...]

    def gain_along_z():
        for d in range(1, NY * NC):
            fr = (me8 + NY * NC - d) % (NY * NC)
            arrived(grow_s.at[fr], grow_sem.at[d - 1])
        gsum_s[0] = jnp.sum(grow_s[...], axis=0)
        for d in range(1, NZ):
            gz_copy(d).start()
        gz_s[z] = gsum_s[0]

    def gain_along_x():
        for d in range(1, NZ):
            arrived(gz_s.at[(z + NZ - d) % NZ], gz_sem.at[d - 1])
        gsum_s[1] = jnp.sum(gz_s[...], axis=0)
        for d in range(1, 4):
            gx_copy(d).start()
        gx_s[xpos] = gsum_s[1]

    def gz_copy(d):
        return remote(
            gsum_s.at[0], gz_s.at[z], gsend_sem.at[6 + d], gz_sem.at[d - 1], dev((z + d) % NZ, y, c)
        )

    def gx_copy(d):
        return remote(
            gsum_s.at[1], gx_s.at[xpos], gsend_sem.at[13 + d], gx_sem.at[d - 1], {"head": (xpos + d) % 4}
        )

    @pl.when(c == 0)
    def _():
        for h in near_first[::-1]:
            arrived(cpair_s.at[h], cpair_sem.at[h])
            cc_s[h] = mm(ab_s[h, 0], cpair_s[h], 0, 0) + c_s[h]
            if h is near_first[0]:
                pltpu.make_async_copy(cc_s.at[h], cown_s.at[h], cown_sem.at[h]).start()
            else:
                remote(cc_s.at[h], cown_s.at[y], send_sem.at[32 + h], cown_sem.at[y], dev(z, h, 0)).start()
        for i in range(NY):
            arrived(cown_s.at[i], cown_sem.at[i])
        left = jnp.concatenate([phi0_s[i] for i in range(1, NY)], axis=0)
        right = jnp.concatenate([cown_s[i] for i in range(1, NY)], axis=0)
        crow_s[...] = cown_s[0] + mm(left, right, 0, 0)
        for dlt in range(NZ - 1, 0, -1):
            @pl.when(z >= dlt)
            def _():
                remote(
                    crow_s, zc_s.at[dlt - 1], send_sem.at[4 + dlt], zc_sem.at[dlt - 1], dev(z - dlt, y, 0)
                ).start()
        gam_s[NY - 2] = cown_s[NY - 1]
        for i in range(NY - 3, -1, -1):
            gam_s[i] = mm(aown_s[i + 1], gam_s[i + 1], 0, 0) + cown_s[i + 1]
        gain_along_z()
        fill_backward()
        for dlt in range(1, NZ - 1):
            @pl.when(z + dlt < NZ)
            def _():
                arrived(za_s.at[dlt - 1], za_sem.at[dlt - 1])

            theta_s[dlt] = za_s[0] if dlt == 1 else mm(za_s[dlt - 1], theta_s[dlt - 1])

        @pl.when(z + NZ - 1 < NZ)
        def _():
            arrived(za_s.at[NZ - 2], za_sem.at[NZ - 2])

        gain_along_x()
        for dlt in range(NZ - 1, 0, -1):
            @pl.when(z + dlt < NZ)
            def _():
                arrived(zc_s.at[dlt - 1], zc_sem.at[dlt - 1])
        left = jnp.concatenate([theta_s[i] for i in range(1, NZ - 1)], axis=0)
        right = jnp.concatenate([zc_s[i] for i in range(1, NZ - 1)], axis=0)
        d_row = zc_s[0] + mm(left, right, 0, 0)
        dsend_s[NY - 1] = d_row
        for i in range(NY - 1):
            dsend_s[i] = mm(psi_s[i], d_row, 0, 0) + gam_s[i]
        for i in near_first[::-1]:
            remote(dsend_s.at[i], dout_s.at[y], send_sem.at[12 + i], dout_sem.at[y], dev(z, i, 1)).start()
        for h in range(heads):
            arrived(dout_s.at[h], dout_sem.at[h])

    @pl.when(c == 1)
    def _():
        gain_along_z()
        fill_backward()
        gain_along_x()
        for h in near_first:
            arrived(dout_s.at[h], dout_sem.at[h])
            d0_s[h] = mm(ab_s[h, 0], dout_s[h], 0, 0) + c_s[h]
            remote(d0_s.at[h], dout_s.at[h], send_sem.at[36 + h], dout_sem.at[h], pair).start()

    lane = lax.broadcasted_iota(jnp.int32, (steps, heads), 1)
    db_all = jnp.zeros((steps, heads), F32)
    for h in range(heads):
        gm = g0_s[h] + mm(nk_s[h], dout_s[h])
        b = b_ref[:, h:h + 1]
        dv = b * gm
        dv_s[h] = dv
        dvf_s[pl.ds(h, steps, stride=heads), :] = dv
        db = jnp.sum(gm * p_s[h], axis=-1, keepdims=True) / b
        db_all = db_all + jnp.where(lane == h, db, 0.0)
    db_s[...] = db_all
    for h in range(heads):
        hm = jnp.where(col_i < row_i, mm(dv_s[h], p_s[h], 1, 1), 0.0)
        low_s[h] = hm + hm.T
    for h in range(heads):
        dk = dk1_s[h] + mm(
            jnp.concatenate([p_s[h], dv_s[h]], axis=1), jnp.concatenate([dout_s[h], -sin_s[h]], axis=1), 1, 1
        ) - mm(low_s[h], of_head(ku_s, h, steps))
        dk_s[pl.ds(h, steps, stride=heads), :] = dk
    db_ref[...] = jnp.concatenate([db_s[pl.ds(j, tok, stride=per), :] for j in range(per)], axis=1).T
    dk_ref[...] = unit_pullback(dk_s[...], ku_s[...], rk_s[...]).astype(BF16)
    dv_ref[...] = dvf_s[...].astype(BF16)

    for d in range(1, 4):
        arrived(gx_s.at[(xpos + 4 - d) % 4], gx_sem.at[d - 1])
    dg_ref[...] = jnp.sum(gx_s[...], axis=0)[0:1]

    for j in range(2):
        send["pair", j].wait_send()

        @pl.when(jnp.logical_not(own_here(j)))
        def _():
            own_copy(j, 0).wait_send()
            own_copy(j, 1).wait_send()

    def left(src, sem):
        remote(src, src, sem, sem, pair).wait_send()

    @pl.when(c == 1)
    def _():
        for part in range(2):
            zab_each(part, lambda copy: copy.wait_send())

        @pl.when((z == 0) | (z == NG - 1))
        def _():
            for n in range(2):
                middle_copy(n).wait_send()

        for dlt in range(1, NZ):
            @pl.when(z >= dlt)
            def _():
                left(phi_s.at[NY - 1], send_sem.at[12 + dlt])
        for i in range(1, NY):
            left(own_s.at[i, 0], send_sem.at[20 + i])
            left(phi_s.at[i - 1], send_sem.at[24 + i])
        for i in range(NY):
            left(sout_s.at[i], send_sem.at[28 + i])
            left(c_s.at[i], send_sem.at[32 + i])
            left(d0_s.at[i], send_sem.at[36 + i])

    @pl.when(c == 0)
    def _():
        for h in near_first:
            left(s1_s.at[h], send_sem.at[28 + h])
        for h in near_first[1:]:
            left(cc_s.at[h], send_sem.at[32 + h])
        for dlt in range(1, NZ):
            @pl.when(z >= dlt)
            def _():
                left(crow_s, send_sem.at[4 + dlt])
        for i in range(NY):
            left(dsend_s.at[i], send_sem.at[12 + i])
    for copy in gsends:
        copy.wait_send()
    for d in range(1, NZ):
        gz_copy(d).wait_send()
    for d in range(1, 4):
        gx_copy(d).wait_send()


def local(queries, keys, values, betas, gain, out_grad):
    tok, heads, dim = queries.shape
    per = keys.shape[1]
    steps = tok * per
    f = lambda *s: pltpu.VMEM(s, F32)
    dma = pltpu.SemaphoreType.DMA
    vmem = pl.BlockSpec(memory_space=pltpu.VMEM)
    b16 = lambda *sh: pltpu.VMEM(sh, BF16)
    scratch = [
        b16(tok * heads, dim), b16(steps * heads, dim), b16(steps * heads, dim), f(per * heads, tok), f(1, dim),
        b16(tok * heads, dim), f(steps, heads), f(steps, heads), dma((6,)),
        f(steps * heads, dim), f(tok * heads, dim), f(steps * heads, dim), f(tok * heads, dim),
        f(steps * heads, 1), f(tok * heads, 1), f(heads, steps, steps), f(heads, steps, steps),
        f(heads, steps, steps), f(heads, steps, dim), f(heads, steps, 2 * dim), f(heads, steps, tok),
        f(heads, tok, dim), f(heads, dim, tok), f(heads, tok, dim), f(heads, steps, dim), f(heads, tok, dim),
        f(heads, steps, dim), f(heads, steps, dim), f(tok * heads, dim), f(tok * heads, dim),
        f(steps * heads, dim), f(steps * heads, dim), f(heads, steps, dim),
        f(heads, 2, dim, dim), f(2, 2, dim, dim), f(2, 2, dim, dim), f(NY, 2, dim, dim),
        f(NY, dim, dim), f(NY, dim, dim), f(NG, 2, dim, dim), f(NZ - 1, dim, dim),
        f(NY, dim, dim), f(heads, dim, dim), f(heads, dim, dim),
        f(NY, dim, dim), f(NY, dim, dim), f(NZ - 1, dim, dim), f(NY - 1, dim, dim), f(heads, dim, dim),
        f(heads, dim, dim), f(heads, dim, dim), f(NY, dim, dim), f(dim, dim), f(NZ - 1, dim, dim),
        f(NY - 1, dim, dim), f(NY, dim, dim), f(heads, dim, dim), f(heads, dim, dim),
        f(8, dim), f(NY * NC, 8, dim), f(NZ, 8, dim), f(4, 8, dim), f(2, 8, dim),
        f(NY * dim, dim), f(dim, dim), f(dim, dim), f(dim, dim), dma,
        dma((48,)), dma((2,)), dma((2 * NY,)), dma((2 * NG,)), dma((NZ - 1,)), dma((heads,)), dma((2 * NY,)),
        dma((heads,)), dma((NY,)), dma((NZ - 1,)), dma((heads,)),
        dma((24,)), dma((NY * NC - 1,)), dma((NZ - 1,)), dma((3,)),
    ]
    outs = pl.pallas_call(
        kernel,
        out_shape=(
            jax.ShapeDtypeStruct((tok * heads, dim), BF16),
            jax.ShapeDtypeStruct((tok * heads, dim), BF16),
            jax.ShapeDtypeStruct((steps * heads, dim), BF16),
            jax.ShapeDtypeStruct((steps * heads, dim), BF16),
            jax.ShapeDtypeStruct((per * heads, tok), F32),
            jax.ShapeDtypeStruct((1, dim), F32),
        ),
        in_specs=[pl.BlockSpec(memory_space=pltpu.HBM)] * 6,
        out_specs=(vmem,) * 6,
        scratch_shapes=scratch,
        compiler_params=pltpu.CompilerParams(
            collective_id=0, has_side_effects=True, vmem_limit_bytes=32 * 1024 * 1024
        ),
        name="delta_product",
    )(*[
        pltpu.with_memory_space_constraint(a, pltpu.HBM)
        for a in (
            queries.reshape(tok * heads, dim),
            keys.reshape(steps * heads, dim),
            values.reshape(steps * heads, dim),
            betas.transpose(1, 2, 0).reshape(per * heads, tok),
            gain.reshape(1, dim),
            out_grad.reshape(tok * heads, dim),
        )
    ])
    out, dq, dk, dv, db, dg = pl.pallas_call(
        store,
        out_shape=tuple(jax.ShapeDtypeStruct(a.shape, a.dtype) for a in outs),
        in_specs=[vmem] * 6,
        out_specs=(pl.BlockSpec(memory_space=pl.ANY),) * 6,
        scratch_shapes=[dma((6,))],
        compiler_params=pltpu.CompilerParams(vmem_limit_bytes=4 * 1024 * 1024),
        name="store",
    )(*outs)
    return (
        out.reshape(queries.shape), dq.reshape(queries.shape), dk.reshape(keys.shape), dv.reshape(values.shape),
        db.reshape(per, heads, tok).transpose(2, 0, 1), dg.reshape(dim),
    )


def store(*refs):
    sem = refs[-1]
    copies = [pltpu.make_async_copy(refs[n], refs[6 + n], sem.at[n]) for n in range(6)]
    for copy in copies:
        copy.start()
    for copy in copies:
        copy.wait()


def solution(mesh):
    return jax.shard_map(
        local,
        mesh=mesh,
        in_specs=(
            P("seq", "head", None),
            P("seq", None, "head", None),
            P("seq", None, "head", None),
            P("seq", None, "head"),
            P(),
            P("seq", "head", None),
        ),
        out_specs=(
            P("seq", "head", None),
            P("seq", "head", None),
            P("seq", None, "head", None),
            P("seq", None, "head", None),
            P("seq", None, "head"),
            P(),
        ),
        check_vma=False,
    )
```

```python
import functools

import jax
import jax.numpy as jnp
from jax import lax
from jax.experimental import pallas as pl
from jax.experimental.pallas import tpu as pltpu
from jax.sharding import PartitionSpec as P

EPS = 1e-06
F32 = jnp.float32
BF16 = jnp.bfloat16
MESH = pl.DeviceIdType.MESH
NY = 4
NZ = 8
NG = 4
NC = 2


def split(x):
    hi = x.astype(BF16)
    lo = (x - hi.astype(F32)).astype(BF16)
    return hi, lo


def dot(a, b, dims):
    return lax.dot_general(a, b, (dims, ((), ())), preferred_element_type=F32)


def mms(a, b, ca=1, cb=0):
    left = jnp.concatenate([a[0], a[1], a[0]], axis=ca)
    right = jnp.concatenate([b[0], b[0], b[1]], axis=cb)
    return dot(left, right, ((ca,), (cb,)))


def mm(a, b, ca=1, cb=0):
    return mms(split(a), split(b), ca, cb)


def iotas(rows, cols):
    return (
        lax.broadcasted_iota(jnp.int32, (rows, cols), 0),
        lax.broadcasted_iota(jnp.int32, (rows, cols), 1),
    )


def unit_pullback(d_unit, unit, inverse):
    return (d_unit - unit * jnp.sum(unit * d_unit, axis=-1, keepdims=True)) * inverse


def kernel(
    q_hbm, k_hbm, v_hbm, b_hbm, g_hbm, do_hbm,
    out_ref, dq_ref, dk_ref, dv_ref, db_ref, dg_ref,
    q_ref, k_ref, v_ref, bt_ref, g_ref, do_ref, b_ref, db_s, in_sem,
    ku_s, qu_s, vf_s, dof_s, rk_s, rq_s, low_s, n_s, nt_s, nk_s, wu_s, sct_s, r_s, rt_s, ol_s, p_s, adj_s,
    g0_s, dk1_s, of_s, dq_s, dk_s, dvf_s, dv_s,
    ab_s, pair_s, comp_s, own_s, phi_s, beta_s, zab_s, za_s, sout_s, sin_s, s1_s,
    aown_s, phi0_s, theta_s, psi_s, c_s, cpair_s, cc_s, cown_s, crow_s, zc_s, gam_s, dsend_s, dout_s, d0_s,
    gpart_s, grow_s, gz_s, gx_s, gsum_s, xa_s, xb_s, middle_s, mid_s, mid_sem, at_s, psit_s, phit_s, thetat_s,
    send_sem, pair_sem, own_sem, zab_sem, za_sem, sin_sem, aown_sem, cpair_sem, cown_sem, zc_sem, dout_sem,
    gsend_sem, grow_sem, gz_sem, gx_sem,
):
    steps, heads = b_ref.shape
    per = steps // (q_ref.shape[0] // heads)
    tok = q_ref.shape[0] // heads
    dim = q_ref.shape[1]
    seq = lax.axis_index("seq")
    xpos = lax.axis_index("head")
    z = seq // (NY * NC)
    y = (seq // NC) % NY
    c = seq % NC

    def dev(zz, yy, cc):
        return {"seq": zz * (NY * NC) + yy * NC + cc}

    barrier = pltpu.get_barrier_semaphore()
    count = 0
    for dy in range(NY):
        for dc in range(NC):
            if dy or dc:
                pl.semaphore_signal(
                    barrier, inc=1, device_id=dev(z, (y + dy) % NY, (c + dc) % NC), device_id_type=MESH
                )
                count += 1
    for dz in range(1, NZ):
        for dc in range(NC):
            pl.semaphore_signal(
                barrier, inc=1, device_id=dev((z + dz) % NZ, y, (c + dc) % NC), device_id_type=MESH
            )
            count += 1
    for dx in range(1, 4):
        pl.semaphore_signal(
            barrier, inc=1, device_id={"head": (xpos + dx) % 4}, device_id_type=MESH
        )
        count += 1

    loads = [
        pltpu.make_async_copy(src, dst, in_sem.at[n])
        for n, (src, dst) in enumerate([
            (k_hbm, k_ref), (b_hbm, bt_ref), (v_hbm, v_ref), (q_hbm, q_ref), (do_hbm, do_ref), (g_hbm, g_ref)
        ])
    ]
    for load in loads:
        load.start()

    def remote(src, dst, ssem, rsem, target):
        return pltpu.make_async_remote_copy(
            src_ref=src, dst_ref=dst, send_sem=ssem, recv_sem=rsem, device_id=target, device_id_type=MESH
        )

    def arrived(dst, rsem):
        pltpu.make_async_copy(dst, dst, rsem).wait()

    group = z // NG
    rank = z % NG

    near_first = [(y + d) % NY for d in (0, 1, 3, 2)]

    def own_copy(j, part):
        head = 2 * c + j
        return remote(
            comp_s.at[j, part], own_s.at[y, part], send_sem.at[2 + j if part == 0 else 45 + j],
            own_sem.at[part * NY + y], dev(z, head, 1),
        )

    def own_here(j):
        return (c == 1) & (y == 2 * c + j)

    def own_start(j, part):
        @pl.when(own_here(j))
        def _():
            pltpu.make_async_copy(
                comp_s.at[j, part], own_s.at[y, part], own_sem.at[part * NY + y]
            ).start()

        @pl.when(jnp.logical_not(own_here(j)))
        def _():
            own_copy(j, part).start()

    def zab_copy(dlt, part, back=False):
        src = (beta_s if part else phi_s).at[NY - 1]
        to = 0 if back else z + dlt
        sem = (8, 44)[part] if back else (4, 40)[part] + dlt
        return remote(
            src, zab_s.at[rank, part], send_sem.at[sem], zab_sem.at[part * NG + rank], dev(to, y, 1)
        )

    def zab_each(part, act):
        for dlt in range(NG - 1, 0, -1):
            @pl.when((rank + dlt < NG) & ((z > 0) | (part == 1)))
            def _():
                act(zab_copy(dlt, part))

        @pl.when((group == 0) & (rank > 0))
        def _():
            act(zab_copy(0, part, True))

    def middle_copy(n):
        to = jnp.where(rank == 0, NZ - 1 - n, NG + n)
        return remote(middle_s, mid_s, send_sem.at[9 + n], mid_sem, dev(to, y, 1))

    row_i, col_i = iotas(steps, steps)
    tok_i, step_i = iotas(tok, steps)
    visible = step_i <= 2 * tok_i + 1
    eye = (row_i == col_i).astype(F32)
    eye_dim = eye[:dim, :dim]

    for dlt in range(1, NZ):
        @pl.when(z + dlt >= NZ)
        def _():
            za_s[dlt - 1] = jnp.zeros((dim, dim), F32)
            zc_s[dlt - 1] = jnp.zeros((dim, dim), F32)

    for load in loads:
        load.wait()
    turned = bt_ref[...].T
    for j in range(per):
        b_ref[pl.ds(j, tok, stride=per), :] = turned[:, j * heads:(j + 1) * heads]
    k = k_ref[...].astype(F32)
    rk = lax.rsqrt(jnp.sum(k * k, axis=-1, keepdims=True) + EPS)
    rk_s[...] = rk
    ku_s[...] = k * rk
    vf_s[...] = v_ref[...].astype(F32)

    def of_head(ref, h, rows):
        return ref[pl.ds(h, rows, stride=heads), :]

    half = steps // 2
    base = 16
    blocks = half // base
    lane16 = lax.broadcasted_iota(jnp.int32, (base, half), 1) // base
    packed = []
    for h in range(heads):
        ku = of_head(ku_s, h, steps)
        b = b_ref[:, h:h + 1]
        low = jnp.where(col_i < row_i, mm(ku, ku, 1, 1) * b, 0.0)
        low_s[h] = low
        for part in range(2):
            tri = low[part * half:(part + 1) * half, part * half:(part + 1) * half]
            diag = jnp.zeros((base, half), F32)
            for i in range(blocks):
                diag = jnp.where(lane16 == i, tri[i * base:(i + 1) * base], diag)
            packed.append(diag)
    packed = jnp.concatenate(packed, axis=0)
    rows = packed.shape[0]
    lane = lax.broadcasted_iota(jnp.int32, (rows, half), 1)
    row = lax.broadcasted_iota(jnp.int32, (rows, half), 0)
    inv = jnp.where(row % base == lane % base, 1.0, 0.0)
    for step in range(base - 1):
        column = jnp.take_along_axis(packed, (lane // base) * base + step, axis=1)
        pivot = inv.reshape(rows // base, base, half)[:, step:step + 1, :]
        pivot = jnp.broadcast_to(pivot, (rows // base, base, half)).reshape(rows, half)
        inv = inv - column * pivot
    quads = [(h, part) for h in range(heads) for part in range(2)]
    for n, (h, part) in enumerate(quads):
        mine = inv[n * base:(n + 1) * base]
        n_s[h, part * half:(part + 1) * half, part * half:(part + 1) * half] = jnp.concatenate(
            [jnp.where(lane16 == i, mine, 0.0) for i in range(blocks)], axis=0
        )
        if part:
            n_s[h, 0:half, half:steps] = jnp.zeros((half, half), F32)
    sub_i, sub_j = row_i[:half, :half], col_i[:half, :half]
    size = base
    while size < half:
        band = (sub_i // (2 * size) == sub_j // (2 * size)) & (sub_i // size != sub_j // size)
        firsts = {}
        for h, part in quads:
            at = pl.ds(part * half, half)
            parts = split(n_s[h, at, at])
            firsts[h, part] = parts, mms(split(low_s[h, at, at]), parts)
        for h, part in quads:
            at = pl.ds(part * half, half)
            parts, first = firsts[h, part]
            n_s[h, at, at] = n_s[h, at, at] - jnp.where(band, mms(parts, split(first)), 0.0)
        size *= 2
    firsts = [mm(low_s[h, half:steps, 0:half], n_s[h, 0:half, 0:half]) for h in range(heads)]
    for h in range(heads):
        n_s[h, half:steps, 0:half] = -mm(n_s[h, half:steps, half:steps], firsts[h])
    for h in range(heads):
        ku = of_head(ku_s, h, steps)
        b = b_ref[:, h:h + 1]
        wu_s[h] = mm(n_s[h], jnp.concatenate([b * ku, b * of_head(vf_s, h, steps)], axis=1))
    for h in range(heads):
        ab = mm(of_head(ku_s, h, steps).T, wu_s[h])
        ab_s[h, 0] = eye_dim - ab[:, :dim]
        ab_s[h, 1] = ab[:, dim:]

    def fill_forward():
        q = q_ref[...].astype(F32)
        rq = lax.rsqrt(jnp.sum(q * q, axis=-1, keepdims=True) + EPS)
        rq_s[...] = rq
        qu_s[...] = q * rq
        dof_s[...] = do_ref[...].astype(F32)
        for h in range(heads):
            at_s[h] = ab_s[h, 0].T
            ku = of_head(ku_s, h, steps)
            qu = of_head(qu_s, h, tok)
            sc = jnp.where(visible, mm(qu, ku, 1, 1), 0.0)
            ro = mm(sc, wu_s[h])
            r = qu - ro[:, :dim]
            r_s[h] = r
            rt_s[h] = r.T
            ol_s[h] = ro[:, dim:]
            sct_s[h] = sc.T
            nt = n_s[h].T
            nt_s[h] = nt
            nk_s[h] = mm(nt, ku)

    def fill_backward():
        for h in range(heads):
            ku = of_head(ku_s, h, steps)
            adj = adj_s[h]
            m_do = jnp.where(visible, mm(adj, p_s[h], 1, 1), 0.0)
            dq = mm(adj, sin_s[h], 1, 1) + mm(m_do, ku)
            dq_s[pl.ds(h, tok, stride=heads), :] = dq
            dk1_s[h] = mm(m_do.T, of_head(qu_s, h, tok))
            g0_s[h] = mm(nt_s[h], mm(sct_s[h], adj))
        out_ref[...] = of_s[...].astype(BF16)
        dq_ref[...] = unit_pullback(dq_s[...], qu_s[...], rq_s[...]).astype(BF16)

    pl.semaphore_wait(barrier, count)

    other = 1 - c
    pair = dev(z, y, other)
    send = {}
    for j in range(2):
        send["pair", j] = remote(
            ab_s.at[2 * other + j], pair_s.at[j], send_sem.at[j], pair_sem.at[j], pair
        )
        send["pair", j].start()
    for j in range(2):
        arrived(pair_s.at[j], pair_sem.at[j])
        mine = ab_s[2 * c + j]
        theirs = pair_s[j]
        first = jnp.where(c == 0, mine, theirs)
        second = jnp.where(c == 0, theirs, mine)
        both = mm(second[0], jnp.concatenate([first[0], first[1]], axis=1))
        comp_s[j, 0] = both[:, :dim]
        comp_s[j, 1] = both[:, dim:] + second[1]
        own_start(j, 0)
    for j in range(2):
        own_start(j, 1)

    @pl.when(c == 1)
    def _():
        low_core = dev(z, y, 0)
        for i in range(NY):
            arrived(own_s.at[i, 0], own_sem.at[i])
            phi_s[i] = mm(own_s[i, 0], phi_s[i - 1]) if i else own_s[0, 0]
        zab_each(0, lambda copy: copy.start())
        for i in range(NY):
            arrived(own_s.at[i, 1], own_sem.at[NY + i])
            beta_s[i] = mm(own_s[i, 0], beta_s[i - 1]) + own_s[i, 1] if i else own_s[0, 1]
        zab_each(1, lambda copy: copy.start())

        for i in range(1, NY):
            remote(own_s.at[i, 0], aown_s.at[i], send_sem.at[20 + i], aown_sem.at[i], low_core).start()
            remote(phi_s.at[i - 1], phi0_s.at[i], send_sem.at[24 + i], aown_sem.at[NY + i], low_core).start()
        fill_forward()

        phis = jnp.concatenate([phi_s[i] for i in range(NY - 1)], axis=0)

        @pl.when(group == 1)
        def _():
            @pl.when(rank == 0)
            def _():
                xa_s[0:dim] = eye_dim

            for i in range(NG - 1):
                @pl.when(rank > i)
                def _():
                    arrived(zab_s.at[i, 0], zab_sem.at[i])
                    xa_s[0:dim] = mm(zab_s[i, 0], xa_s[0:dim]) if i else zab_s[0, 0]
            xa_s[dim:] = mm(phis, xa_s[0:dim])

        @pl.when(group == 0)
        def _():
            for i in range(1, NG):
                @pl.when((rank > i) | (rank == 0))
                def _():
                    arrived(zab_s.at[i, 0], zab_sem.at[i])

        @pl.when(rank == 0)
        def _():
            xb_s[...] = jnp.zeros((dim, dim), F32)

        for i in range(NG - 1):
            @pl.when(rank > i)
            def _():
                arrived(zab_s.at[i, 1], zab_sem.at[NG + i])
                xb_s[...] = mm(zab_s[i, 0], xb_s[...]) + zab_s[i, 1] if i else zab_s[0, 1]

        @pl.when((group == 0) & (rank == NG - 1))
        def _():
            middle_s[...] = mm(phi_s[NY - 1], xb_s[...]) + beta_s[NY - 1]
            for n in range(2):
                middle_copy(n).start()

        @pl.when((group == 0) & (rank == 0))
        def _():
            state = beta_s[NY - 1]
            for i in range(1, NG):
                arrived(zab_s.at[i, 1], zab_sem.at[NG + i])
                state = mm(zab_s[i, 0], state) + zab_s[i, 1]
            middle_s[...] = state
            for n in range(2):
                middle_copy(n).start()

        sout_s[0] = xb_s[...]
        later = mm(phis, xb_s[...])
        for i in range(1, NY):
            sout_s[i] = later[(i - 1) * dim:i * dim] + beta_s[i - 1]

        @pl.when(group == 1)
        def _():
            arrived(mid_s, mid_sem)
            more = mm(xa_s[...], mid_s[...])
            for i in range(NY):
                sout_s[i] = sout_s[i] + more[i * dim:(i + 1) * dim]

        for i in near_first[::-1]:
            remote(sout_s.at[i], sin_s.at[y], send_sem.at[28 + i], sin_sem.at[y], dev(z, i, 0)).start()
        for dlt in range(1, NZ):
            @pl.when(z >= dlt)
            def _():
                remote(
                    phi_s.at[NY - 1], za_s.at[dlt - 1], send_sem.at[12 + dlt], za_sem.at[dlt - 1],
                    dev(z - dlt, y, 0),
                ).start()
        for h in range(heads):
            arrived(sin_s.at[h], sin_sem.at[h])

    @pl.when(c == 0)
    def _():
        fill_forward()
        for i in range(1, NY):
            arrived(aown_s.at[i], aown_sem.at[i])
            arrived(phi0_s.at[i], aown_sem.at[NY + i])
        psi_s[NY - 2] = aown_s[NY - 1]
        for i in range(NY - 3, -1, -1):
            psi_s[i] = mm(psi_s[i + 1], aown_s[i + 1])
        for i in range(NY - 1):
            psit_s[i * dim:(i + 1) * dim] = psi_s[i].T
            phit_s[:, i * dim:(i + 1) * dim] = phi0_s[i + 1].T
        for h in near_first:
            arrived(sin_s.at[h], sin_sem.at[h])
            s1_s[h] = mm(ab_s[h, 0], sin_s[h]) + ab_s[h, 1]
            remote(s1_s.at[h], sin_s.at[h], send_sem.at[28 + h], sin_sem.at[h], pair).start()

    gain = g_ref[...]
    gain_part = jnp.zeros((1, dim), F32)
    for h in range(heads):
        both = mm(jnp.concatenate([r_s[h], wu_s[h, :, :dim]], axis=0), sin_s[h])
        ol_s[h] = ol_s[h] + both[:tok]
        p_s[h] = wu_s[h, :, dim:] - both[tok:]
    for h in range(heads):
        o = ol_s[h]
        inv_rms = lax.rsqrt(jnp.mean(o * o, axis=-1, keepdims=True) + EPS)
        normal = o * inv_rms
        grad = of_head(dof_s, h, tok)
        of_s[pl.ds(h, tok, stride=heads), :] = gain * normal
        gain_part = gain_part + jnp.sum(grad * normal, axis=0, keepdims=True)
        scaled = grad * gain
        adj_s[h] = inv_rms * (scaled - normal * jnp.mean(scaled * normal, axis=-1, keepdims=True))
    for h in range(heads):
        c_s[h] = mm(rt_s[h], adj_s[h])

    @pl.when(c == 1)
    def _():
        for h in near_first[::-1]:
            remote(c_s.at[h], cpair_s.at[h], send_sem.at[32 + h], cpair_sem.at[h], pair).start()

    gpart_s[...] = jnp.broadcast_to(gain_part, (8, dim))
    me8 = y * NC + c
    n_g = 0
    gsends = []
    for d in range(1, NY * NC):
        to = (me8 + d) % (NY * NC)
        gsends.append(remote(
            gpart_s, grow_s.at[me8], gsend_sem.at[n_g], grow_sem.at[d - 1], dev(z, to // NC, to % NC)))
        gsends[-1].start()
        n_g += 1
    grow_s[me8] = gpart_s[...]

    def gain_along_z():
        for d in range(1, NY * NC):
            fr = (me8 + NY * NC - d) % (NY * NC)
            arrived(grow_s.at[fr], grow_sem.at[d - 1])
        gsum_s[0] = jnp.sum(grow_s[...], axis=0)
        for d in range(1, NZ):
            gz_copy(d).start()
        gz_s[z] = gsum_s[0]

    def gain_along_x():
        for d in range(1, NZ):
            arrived(gz_s.at[(z + NZ - d) % NZ], gz_sem.at[d - 1])
        gsum_s[1] = jnp.sum(gz_s[...], axis=0)
        for d in range(1, 4):
            gx_copy(d).start()
        gx_s[xpos] = gsum_s[1]

    def gz_copy(d):
        return remote(
            gsum_s.at[0], gz_s.at[z], gsend_sem.at[6 + d], gz_sem.at[d - 1], dev((z + d) % NZ, y, c)
        )

    def gx_copy(d):
        return remote(
            gsum_s.at[1], gx_s.at[xpos], gsend_sem.at[13 + d], gx_sem.at[d - 1], {"head": (xpos + d) % 4}
        )

    @pl.when(c == 0)
    def _():
        for h in near_first[::-1]:
            arrived(cpair_s.at[h], cpair_sem.at[h])
            cc_s[h] = mm(at_s[h], cpair_s[h]) + c_s[h]
            if h is near_first[0]:
                pltpu.make_async_copy(cc_s.at[h], cown_s.at[h], cown_sem.at[h]).start()
            else:
                remote(cc_s.at[h], cown_s.at[y], send_sem.at[32 + h], cown_sem.at[y], dev(z, h, 0)).start()
        for i in range(NY):
            arrived(cown_s.at[i], cown_sem.at[i])
        right = jnp.concatenate([cown_s[i] for i in range(1, NY)], axis=0)
        crow_s[...] = cown_s[0] + mm(phit_s[...], right)
        for dlt in range(NZ - 1, 0, -1):
            @pl.when(z >= dlt)
            def _():
                remote(
                    crow_s, zc_s.at[dlt - 1], send_sem.at[4 + dlt], zc_sem.at[dlt - 1], dev(z - dlt, y, 0)
                ).start()
        gam_s[NY - 2] = cown_s[NY - 1]
        for i in range(NY - 3, -1, -1):
            gam_s[i] = mm(aown_s[i + 1], gam_s[i + 1], 0, 0) + cown_s[i + 1]
        gain_along_z()
        fill_backward()
        for dlt in range(1, NZ - 1):
            @pl.when(z + dlt < NZ)
            def _():
                arrived(za_s.at[dlt - 1], za_sem.at[dlt - 1])

            theta_s[dlt] = za_s[0] if dlt == 1 else mm(za_s[dlt - 1], theta_s[dlt - 1])
            thetat_s[:, (dlt - 1) * dim:dlt * dim] = theta_s[dlt].T

        @pl.when(z + NZ - 1 < NZ)
        def _():
            arrived(za_s.at[NZ - 2], za_sem.at[NZ - 2])

        gain_along_x()
        for dlt in range(NZ - 1, 0, -1):
            @pl.when(z + dlt < NZ)
            def _():
                arrived(zc_s.at[dlt - 1], zc_sem.at[dlt - 1])
        right = jnp.concatenate([zc_s[i] for i in range(1, NZ - 1)], axis=0)
        d_row = zc_s[0] + mm(thetat_s[...], right)
        dsend_s[NY - 1] = d_row
        more = mm(psit_s[...], d_row)
        for i in range(NY - 1):
            dsend_s[i] = more[i * dim:(i + 1) * dim] + gam_s[i]
        for i in near_first[::-1]:
            remote(dsend_s.at[i], dout_s.at[y], send_sem.at[12 + i], dout_sem.at[y], dev(z, i, 1)).start()
        for h in range(heads):
            arrived(dout_s.at[h], dout_sem.at[h])

    @pl.when(c == 1)
    def _():
        gain_along_z()
        fill_backward()
        gain_along_x()
        for h in near_first:
            arrived(dout_s.at[h], dout_sem.at[h])
            d0_s[h] = mm(at_s[h], dout_s[h]) + c_s[h]
            remote(d0_s.at[h], dout_s.at[h], send_sem.at[36 + h], dout_sem.at[h], pair).start()

    lane = lax.broadcasted_iota(jnp.int32, (steps, heads), 1)
    db_all = jnp.zeros((steps, heads), F32)
    for h in range(heads):
        gm = g0_s[h] + mm(nk_s[h], dout_s[h])
        b = b_ref[:, h:h + 1]
        dv = b * gm
        dv_s[h] = dv
        dvf_s[pl.ds(h, steps, stride=heads), :] = dv
        db = jnp.sum(gm * p_s[h], axis=-1, keepdims=True) / b
        db_all = db_all + jnp.where(lane == h, db, 0.0)
    db_s[...] = db_all
    for h in range(heads):
        hm = jnp.where(col_i < row_i, mm(dv_s[h], p_s[h], 1, 1), 0.0)
        low_s[h] = hm + hm.T
    for h in range(heads):
        dk = dk1_s[h] + mm(
            jnp.concatenate([p_s[h], dv_s[h]], axis=1), jnp.concatenate([dout_s[h], -sin_s[h]], axis=1), 1, 1
        ) - mm(low_s[h], of_head(ku_s, h, steps))
        dk_s[pl.ds(h, steps, stride=heads), :] = dk
    db_ref[...] = jnp.concatenate([db_s[pl.ds(j, tok, stride=per), :] for j in range(per)], axis=1).T
    dk_ref[...] = unit_pullback(dk_s[...], ku_s[...], rk_s[...]).astype(BF16)
    dv_ref[...] = dvf_s[...].astype(BF16)

    for d in range(1, 4):
        arrived(gx_s.at[(xpos + 4 - d) % 4], gx_sem.at[d - 1])
    dg_ref[...] = jnp.sum(gx_s[...], axis=0)[0:1]

    for j in range(2):
        send["pair", j].wait_send()

        @pl.when(jnp.logical_not(own_here(j)))
        def _():
            own_copy(j, 0).wait_send()
            own_copy(j, 1).wait_send()

    def left(src, sem):
        remote(src, src, sem, sem, pair).wait_send()

    @pl.when(c == 1)
    def _():
        for part in range(2):
            zab_each(part, lambda copy: copy.wait_send())

        @pl.when((z == 0) | (z == NG - 1))
        def _():
            for n in range(2):
                middle_copy(n).wait_send()

        for dlt in range(1, NZ):
            @pl.when(z >= dlt)
            def _():
                left(phi_s.at[NY - 1], send_sem.at[12 + dlt])
        for i in range(1, NY):
            left(own_s.at[i, 0], send_sem.at[20 + i])
            left(phi_s.at[i - 1], send_sem.at[24 + i])
        for i in range(NY):
            left(sout_s.at[i], send_sem.at[28 + i])
            left(c_s.at[i], send_sem.at[32 + i])
            left(d0_s.at[i], send_sem.at[36 + i])

    @pl.when(c == 0)
    def _():
        for h in near_first:
            left(s1_s.at[h], send_sem.at[28 + h])
        for h in near_first[1:]:
            left(cc_s.at[h], send_sem.at[32 + h])
        for dlt in range(1, NZ):
            @pl.when(z >= dlt)
            def _():
                left(crow_s, send_sem.at[4 + dlt])
        for i in range(NY):
            left(dsend_s.at[i], send_sem.at[12 + i])
    for copy in gsends:
        copy.wait_send()
    for d in range(1, NZ):
        gz_copy(d).wait_send()
    for d in range(1, 4):
        gx_copy(d).wait_send()


def local(queries, keys, values, betas, gain, out_grad):
    tok, heads, dim = queries.shape
    per = keys.shape[1]
    steps = tok * per
    f = lambda *s: pltpu.VMEM(s, F32)
    dma = pltpu.SemaphoreType.DMA
    vmem = pl.BlockSpec(memory_space=pltpu.VMEM)
    b16 = lambda *sh: pltpu.VMEM(sh, BF16)
    scratch = [
        b16(tok * heads, dim), b16(steps * heads, dim), b16(steps * heads, dim), f(per * heads, tok), f(1, dim),
        b16(tok * heads, dim), f(steps, heads), f(steps, heads), dma((6,)),
        f(steps * heads, dim), f(tok * heads, dim), f(steps * heads, dim), f(tok * heads, dim),
        f(steps * heads, 1), f(tok * heads, 1), f(heads, steps, steps), f(heads, steps, steps),
        f(heads, steps, steps), f(heads, steps, dim), f(heads, steps, 2 * dim), f(heads, steps, tok),
        f(heads, tok, dim), f(heads, dim, tok), f(heads, tok, dim), f(heads, steps, dim), f(heads, tok, dim),
        f(heads, steps, dim), f(heads, steps, dim), f(tok * heads, dim), f(tok * heads, dim),
        f(steps * heads, dim), f(steps * heads, dim), f(heads, steps, dim),
        f(heads, 2, dim, dim), f(2, 2, dim, dim), f(2, 2, dim, dim), f(NY, 2, dim, dim),
        f(NY, dim, dim), f(NY, dim, dim), f(NG, 2, dim, dim), f(NZ - 1, dim, dim),
        f(NY, dim, dim), f(heads, dim, dim), f(heads, dim, dim),
        f(NY, dim, dim), f(NY, dim, dim), f(NZ - 1, dim, dim), f(NY - 1, dim, dim), f(heads, dim, dim),
        f(heads, dim, dim), f(heads, dim, dim), f(NY, dim, dim), f(dim, dim), f(NZ - 1, dim, dim),
        f(NY - 1, dim, dim), f(NY, dim, dim), f(heads, dim, dim), f(heads, dim, dim),
        f(8, dim), f(NY * NC, 8, dim), f(NZ, 8, dim), f(4, 8, dim), f(2, 8, dim),
        f(NY * dim, dim), f(dim, dim), f(dim, dim), f(dim, dim), dma,
        f(heads, dim, dim), f((NY - 1) * dim, dim), f(dim, (NY - 1) * dim), f(dim, (NZ - 2) * dim),
        dma((48,)), dma((2,)), dma((2 * NY,)), dma((2 * NG,)), dma((NZ - 1,)), dma((heads,)), dma((2 * NY,)),
        dma((heads,)), dma((NY,)), dma((NZ - 1,)), dma((heads,)),
        dma((24,)), dma((NY * NC - 1,)), dma((NZ - 1,)), dma((3,)),
    ]
    outs = pl.pallas_call(
        kernel,
        out_shape=(
            jax.ShapeDtypeStruct((tok * heads, dim), BF16),
            jax.ShapeDtypeStruct((tok * heads, dim), BF16),
            jax.ShapeDtypeStruct((steps * heads, dim), BF16),
            jax.ShapeDtypeStruct((steps * heads, dim), BF16),
            jax.ShapeDtypeStruct((per * heads, tok), F32),
            jax.ShapeDtypeStruct((1, dim), F32),
        ),
        in_specs=[pl.BlockSpec(memory_space=pltpu.HBM)] * 6,
        out_specs=(vmem,) * 6,
        scratch_shapes=scratch,
        compiler_params=pltpu.CompilerParams(
            collective_id=0, has_side_effects=True, vmem_limit_bytes=32 * 1024 * 1024
        ),
        name="delta_product",
    )(*[
        pltpu.with_memory_space_constraint(a, pltpu.HBM)
        for a in (
            queries.reshape(tok * heads, dim),
            keys.reshape(steps * heads, dim),
            values.reshape(steps * heads, dim),
            betas.transpose(1, 2, 0).reshape(per * heads, tok),
            gain.reshape(1, dim),
            out_grad.reshape(tok * heads, dim),
        )
    ])
    out, dq, dk, dv, db, dg = pl.pallas_call(
        store,
        out_shape=tuple(jax.ShapeDtypeStruct(a.shape, a.dtype) for a in outs),
        in_specs=[vmem] * 6,
        out_specs=(pl.BlockSpec(memory_space=pl.ANY),) * 6,
        scratch_shapes=[dma((6,))],
        compiler_params=pltpu.CompilerParams(vmem_limit_bytes=4 * 1024 * 1024),
        name="store",
    )(*outs)
    return (
        out.reshape(queries.shape), dq.reshape(queries.shape), dk.reshape(keys.shape), dv.reshape(values.shape),
        db.reshape(per, heads, tok).transpose(2, 0, 1), dg.reshape(dim),
    )


def store(*refs):
    sem = refs[-1]
    copies = [pltpu.make_async_copy(refs[n], refs[6 + n], sem.at[n]) for n in range(6)]
    for copy in copies:
        copy.start()
    for copy in copies:
        copy.wait()


def solution(mesh):
    return jax.shard_map(
        local,
        mesh=mesh,
        in_specs=(
            P("seq", "head", None),
            P("seq", None, "head", None),
            P("seq", None, "head", None),
            P("seq", None, "head"),
            P(),
            P("seq", "head", None),
        ),
        out_specs=(
            P("seq", "head", None),
            P("seq", "head", None),
            P("seq", None, "head", None),
            P("seq", None, "head", None),
            P("seq", None, "head"),
            P(),
        ),
        check_vma=False,
    )
```

```python
import functools

import jax
import jax.numpy as jnp
from jax import lax
from jax.experimental import pallas as pl
from jax.experimental.pallas import tpu as pltpu
from jax.sharding import PartitionSpec as P

EPS = 1e-06
F32 = jnp.float32
BF16 = jnp.bfloat16
MESH = pl.DeviceIdType.MESH
NY = 4
NZ = 8
NG = 4
NC = 2


def split(x):
    hi = x.astype(BF16)
    lo = (x - hi.astype(F32)).astype(BF16)
    return hi, lo


def dot(a, b, dims):
    return lax.dot_general(a, b, (dims, ((), ())), preferred_element_type=F32)


def mms(a, b, ca=1, cb=0):
    left = jnp.concatenate([a[0], a[1], a[0]], axis=ca)
    right = jnp.concatenate([b[0], b[0], b[1]], axis=cb)
    return dot(left, right, ((ca,), (cb,)))


def mm(a, b, ca=1, cb=0):
    return mms(split(a), split(b), ca, cb)


def iotas(rows, cols):
    return (
        lax.broadcasted_iota(jnp.int32, (rows, cols), 0),
        lax.broadcasted_iota(jnp.int32, (rows, cols), 1),
    )


def unit_pullback(d_unit, unit, inverse):
    return (d_unit - unit * jnp.sum(unit * d_unit, axis=-1, keepdims=True)) * inverse


def kernel(
    q_hbm, k_hbm, v_hbm, b_hbm, g_hbm, do_hbm,
    out_ref, dq_ref, dk_ref, dv_ref, db_ref, dg_ref,
    q_ref, k_ref, v_ref, bt_ref, g_ref, do_ref, b_ref, db_s, in_sem,
    ku_s, qu_s, vf_s, dof_s, rk_s, rq_s, low_s, n_s, nt_s, nk_s, wu_s, sct_s, r_s, rt_s, ol_s, p_s, adj_s,
    g0_s, dk1_s, of_s, dq_s, dk_s, dvf_s, dv_s,
    ab_s, pair_s, comp_s, own_s, phi_s, beta_s, zab_s, za_s, sout_s, sin_s, s1_s,
    aown_s, phi0_s, theta_s, psi_s, c_s, cpair_s, cc_s, cown_s, crow_s, zc_s, gam_s, dsend_s, dout_s, d0_s,
    gpart_s, grow_s, gz_s, gx_s, gsum_s, xa_s, xb_s, middle_s, mid_s, mid_sem, at_s, psit_s, phit_s, thetat_s, normal_s,
    send_sem, pair_sem, own_sem, zab_sem, za_sem, sin_sem, aown_sem, cpair_sem, cown_sem, zc_sem, dout_sem,
    gsend_sem, grow_sem, gz_sem, gx_sem,
):
    steps, heads = b_ref.shape
    per = steps // (q_ref.shape[0] // heads)
    tok = q_ref.shape[0] // heads
    dim = q_ref.shape[1]
    seq = lax.axis_index("seq")
    xpos = lax.axis_index("head")
    z = seq // (NY * NC)
    y = (seq // NC) % NY
    c = seq % NC

    def dev(zz, yy, cc):
        return {"seq": zz * (NY * NC) + yy * NC + cc}

    barrier = pltpu.get_barrier_semaphore()
    count = 0
    for dy in range(NY):
        for dc in range(NC):
            if dy or dc:
                pl.semaphore_signal(
                    barrier, inc=1, device_id=dev(z, (y + dy) % NY, (c + dc) % NC), device_id_type=MESH
                )
                count += 1
    for dz in range(1, NZ):
        for dc in range(NC):
            pl.semaphore_signal(
                barrier, inc=1, device_id=dev((z + dz) % NZ, y, (c + dc) % NC), device_id_type=MESH
            )
            count += 1
    for dx in range(1, 4):
        pl.semaphore_signal(
            barrier, inc=1, device_id={"head": (xpos + dx) % 4}, device_id_type=MESH
        )
        count += 1

    loads = [
        pltpu.make_async_copy(src, dst, in_sem.at[n])
        for n, (src, dst) in enumerate([
            (k_hbm, k_ref), (b_hbm, bt_ref), (v_hbm, v_ref), (q_hbm, q_ref), (do_hbm, do_ref), (g_hbm, g_ref)
        ])
    ]
    for load in loads:
        load.start()

    def remote(src, dst, ssem, rsem, target):
        return pltpu.make_async_remote_copy(
            src_ref=src, dst_ref=dst, send_sem=ssem, recv_sem=rsem, device_id=target, device_id_type=MESH
        )

    def arrived(dst, rsem):
        pltpu.make_async_copy(dst, dst, rsem).wait()

    group = z // NG
    rank = z % NG

    near_first = [(y + d) % NY for d in (0, 1, 3, 2)]

    def own_copy(j, part):
        head = 2 * c + j
        return remote(
            comp_s.at[j, part], own_s.at[y, part], send_sem.at[2 + j if part == 0 else 45 + j],
            own_sem.at[part * NY + y], dev(z, head, 1),
        )

    def own_here(j):
        return (c == 1) & (y == 2 * c + j)

    def own_start(j, part):
        @pl.when(own_here(j))
        def _():
            pltpu.make_async_copy(
                comp_s.at[j, part], own_s.at[y, part], own_sem.at[part * NY + y]
            ).start()

        @pl.when(jnp.logical_not(own_here(j)))
        def _():
            own_copy(j, part).start()

    def zab_copy(dlt, part, back=False):
        src = (beta_s if part else phi_s).at[NY - 1]
        to = 0 if back else z + dlt
        sem = (8, 44)[part] if back else (4, 40)[part] + dlt
        return remote(
            src, zab_s.at[rank, part], send_sem.at[sem], zab_sem.at[part * NG + rank], dev(to, y, 1)
        )

    def zab_each(part, act):
        for dlt in range(NG - 1, 0, -1):
            @pl.when((rank + dlt < NG) & ((z > 0) | (part == 1)))
            def _():
                act(zab_copy(dlt, part))

        @pl.when((group == 0) & (rank > 0))
        def _():
            act(zab_copy(0, part, True))

    def middle_copy(n):
        to = jnp.where(rank == 0, NZ - 1 - n, NG + n)
        return remote(middle_s, mid_s, send_sem.at[9 + n], mid_sem, dev(to, y, 1))

    row_i, col_i = iotas(steps, steps)
    tok_i, step_i = iotas(tok, steps)
    visible = step_i <= 2 * tok_i + 1
    eye = (row_i == col_i).astype(F32)
    eye_dim = eye[:dim, :dim]

    for dlt in range(1, NZ):
        @pl.when(z + dlt >= NZ)
        def _():
            za_s[dlt - 1] = jnp.zeros((dim, dim), F32)
            zc_s[dlt - 1] = jnp.zeros((dim, dim), F32)

    for load in loads:
        load.wait()
    turned = bt_ref[...].T
    for j in range(per):
        b_ref[pl.ds(j, tok, stride=per), :] = turned[:, j * heads:(j + 1) * heads]
    k = k_ref[...].astype(F32)
    rk = lax.rsqrt(jnp.sum(k * k, axis=-1, keepdims=True) + EPS)
    rk_s[...] = rk
    ku_s[...] = k * rk
    vf_s[...] = v_ref[...].astype(F32)

    def of_head(ref, h, rows):
        return ref[pl.ds(h, rows, stride=heads), :]

    half = steps // 2
    base = 16
    blocks = half // base
    lane16 = lax.broadcasted_iota(jnp.int32, (base, half), 1) // base
    packed = []
    for h in range(heads):
        ku = of_head(ku_s, h, steps)
        b = b_ref[:, h:h + 1]
        low = jnp.where(col_i < row_i, mm(ku, ku, 1, 1) * b, 0.0)
        low_s[h] = low
        for part in range(2):
            tri = low[part * half:(part + 1) * half, part * half:(part + 1) * half]
            diag = jnp.zeros((base, half), F32)
            for i in range(blocks):
                diag = jnp.where(lane16 == i, tri[i * base:(i + 1) * base], diag)
            packed.append(diag)
    packed = jnp.concatenate(packed, axis=0)
    rows = packed.shape[0]
    lane = lax.broadcasted_iota(jnp.int32, (rows, half), 1)
    row = lax.broadcasted_iota(jnp.int32, (rows, half), 0)
    inv = jnp.where(row % base == lane % base, 1.0, 0.0)
    for step in range(base - 1):
        column = jnp.take_along_axis(packed, (lane // base) * base + step, axis=1)
        pivot = inv.reshape(rows // base, base, half)[:, step:step + 1, :]
        pivot = jnp.broadcast_to(pivot, (rows // base, base, half)).reshape(rows, half)
        inv = inv - column * pivot
    quads = [(h, part) for h in range(heads) for part in range(2)]
    for n, (h, part) in enumerate(quads):
        mine = inv[n * base:(n + 1) * base]
        n_s[h, part * half:(part + 1) * half, part * half:(part + 1) * half] = jnp.concatenate(
            [jnp.where(lane16 == i, mine, 0.0) for i in range(blocks)], axis=0
        )
        if part:
            n_s[h, 0:half, half:steps] = jnp.zeros((half, half), F32)
    sub_i, sub_j = row_i[:half, :half], col_i[:half, :half]
    size = base
    while size < half:
        band = (sub_i // (2 * size) == sub_j // (2 * size)) & (sub_i // size != sub_j // size)
        firsts = {}
        for h, part in quads:
            at = pl.ds(part * half, half)
            parts = split(n_s[h, at, at])
            firsts[h, part] = parts, mms(split(low_s[h, at, at]), parts)
        for h, part in quads:
            at = pl.ds(part * half, half)
            parts, first = firsts[h, part]
            n_s[h, at, at] = n_s[h, at, at] - jnp.where(band, mms(parts, split(first)), 0.0)
        size *= 2
    firsts = [mm(low_s[h, half:steps, 0:half], n_s[h, 0:half, 0:half]) for h in range(heads)]
    for h in range(heads):
        n_s[h, half:steps, 0:half] = -mm(n_s[h, half:steps, half:steps], firsts[h])
    for h in range(heads):
        ku = of_head(ku_s, h, steps)
        b = b_ref[:, h:h + 1]
        right = split(jnp.concatenate([b * ku, b * of_head(vf_s, h, steps)], axis=1))
        wu_s[h, :half] = mms(split(n_s[h, :half, :half]), (right[0][:half], right[1][:half]))
        wu_s[h, half:] = mms(split(n_s[h, half:]), right)
    for h in range(heads):
        ab = mm(of_head(ku_s, h, steps).T, wu_s[h])
        ab_s[h, 0] = eye_dim - ab[:, :dim]
        ab_s[h, 1] = ab[:, dim:]

    def fill_forward():
        q = q_ref[...].astype(F32)
        rq = lax.rsqrt(jnp.sum(q * q, axis=-1, keepdims=True) + EPS)
        rq_s[...] = rq
        qu_s[...] = q * rq
        dof_s[...] = do_ref[...].astype(F32)
        for h in range(heads):
            at_s[h] = ab_s[h, 0].T
            ku = of_head(ku_s, h, steps)
            qu = of_head(qu_s, h, tok)
            sc = jnp.where(visible, mm(qu, ku, 1, 1), 0.0)
            ro = mm(sc, wu_s[h])
            r = qu - ro[:, :dim]
            r_s[h] = r
            rt_s[h] = r.T
            ol_s[h] = ro[:, dim:]
            sct_s[h] = sc.T
            nt = n_s[h].T
            nt_s[h] = nt
            nk_s[h] = mm(nt, ku)

    def fill_backward():
        for h in range(heads):
            of_s[pl.ds(h, tok, stride=heads), :] = g_ref[...] * normal_s[h]
            p_s[h] = wu_s[h, :, dim:] - mm(wu_s[h, :, :dim], sin_s[h])
        for h in range(heads):
            ku = of_head(ku_s, h, steps)
            adj = adj_s[h]
            m_do = jnp.where(visible, mm(adj, p_s[h], 1, 1), 0.0)
            dq = mm(adj, sin_s[h], 1, 1) + mm(m_do, ku)
            dq_s[pl.ds(h, tok, stride=heads), :] = dq
            dk1_s[h] = mm(m_do.T, of_head(qu_s, h, tok))
            g0_s[h] = mm(nt_s[h], mm(sct_s[h], adj))
        out_ref[...] = of_s[...].astype(BF16)
        dq_ref[...] = unit_pullback(dq_s[...], qu_s[...], rq_s[...]).astype(BF16)

    pl.semaphore_wait(barrier, count)

    other = 1 - c
    pair = dev(z, y, other)
    send = {}
    for j in range(2):
        send["pair", j] = remote(
            ab_s.at[2 * other + j], pair_s.at[j], send_sem.at[j], pair_sem.at[j], pair
        )
        send["pair", j].start()
    for j in range(2):
        arrived(pair_s.at[j], pair_sem.at[j])
        mine = ab_s[2 * c + j]
        theirs = pair_s[j]
        first = jnp.where(c == 0, mine, theirs)
        second = jnp.where(c == 0, theirs, mine)
        both = mm(second[0], jnp.concatenate([first[0], first[1]], axis=1))
        comp_s[j, 0] = both[:, :dim]
        comp_s[j, 1] = both[:, dim:] + second[1]
        own_start(j, 0)
    for j in range(2):
        own_start(j, 1)

    @pl.when(c == 1)
    def _():
        low_core = dev(z, y, 0)
        for i in range(NY):
            arrived(own_s.at[i, 0], own_sem.at[i])
            phi_s[i] = mm(own_s[i, 0], phi_s[i - 1]) if i else own_s[0, 0]
        zab_each(0, lambda copy: copy.start())
        for i in range(NY):
            arrived(own_s.at[i, 1], own_sem.at[NY + i])
            beta_s[i] = mm(own_s[i, 0], beta_s[i - 1]) + own_s[i, 1] if i else own_s[0, 1]
        zab_each(1, lambda copy: copy.start())

        for i in range(1, NY):
            remote(own_s.at[i, 0], aown_s.at[i], send_sem.at[20 + i], aown_sem.at[i], low_core).start()
            remote(phi_s.at[i - 1], phi0_s.at[i], send_sem.at[24 + i], aown_sem.at[NY + i], low_core).start()
        fill_forward()

        phis = jnp.concatenate([phi_s[i] for i in range(NY - 1)], axis=0)

        @pl.when(group == 1)
        def _():
            @pl.when(rank == 0)
            def _():
                xa_s[0:dim] = eye_dim

            for i in range(NG - 1):
                @pl.when(rank > i)
                def _():
                    arrived(zab_s.at[i, 0], zab_sem.at[i])
                    xa_s[0:dim] = mm(zab_s[i, 0], xa_s[0:dim]) if i else zab_s[0, 0]
            xa_s[dim:] = mm(phis, xa_s[0:dim])

        @pl.when(group == 0)
        def _():
            for i in range(1, NG):
                @pl.when((rank > i) | (rank == 0))
                def _():
                    arrived(zab_s.at[i, 0], zab_sem.at[i])

        @pl.when(rank == 0)
        def _():
            xb_s[...] = jnp.zeros((dim, dim), F32)

        for i in range(NG - 1):
            @pl.when(rank > i)
            def _():
                arrived(zab_s.at[i, 1], zab_sem.at[NG + i])
                xb_s[...] = mm(zab_s[i, 0], xb_s[...]) + zab_s[i, 1] if i else zab_s[0, 1]

        @pl.when((group == 0) & (rank == NG - 1))
        def _():
            middle_s[...] = mm(phi_s[NY - 1], xb_s[...]) + beta_s[NY - 1]
            for n in range(2):
                middle_copy(n).start()

        @pl.when((group == 0) & (rank == 0))
        def _():
            state = beta_s[NY - 1]
            for i in range(1, NG):
                arrived(zab_s.at[i, 1], zab_sem.at[NG + i])
                state = mm(zab_s[i, 0], state) + zab_s[i, 1]
            middle_s[...] = state
            for n in range(2):
                middle_copy(n).start()

        sout_s[0] = xb_s[...]
        later = mm(phis, xb_s[...])
        for i in range(1, NY):
            sout_s[i] = later[(i - 1) * dim:i * dim] + beta_s[i - 1]

        @pl.when(group == 1)
        def _():
            arrived(mid_s, mid_sem)
            more = mm(xa_s[...], mid_s[...])
            for i in range(NY):
                sout_s[i] = sout_s[i] + more[i * dim:(i + 1) * dim]

        for i in near_first[::-1]:
            remote(sout_s.at[i], sin_s.at[y], send_sem.at[28 + i], sin_sem.at[y], dev(z, i, 0)).start()
        for dlt in range(1, NZ):
            @pl.when(z >= dlt)
            def _():
                remote(
                    phi_s.at[NY - 1], za_s.at[dlt - 1], send_sem.at[12 + dlt], za_sem.at[dlt - 1],
                    dev(z - dlt, y, 0),
                ).start()
        for h in range(heads):
            arrived(sin_s.at[h], sin_sem.at[h])

    @pl.when(c == 0)
    def _():
        fill_forward()
        for i in range(1, NY):
            arrived(aown_s.at[i], aown_sem.at[i])
            arrived(phi0_s.at[i], aown_sem.at[NY + i])
        psi_s[NY - 2] = aown_s[NY - 1]
        for i in range(NY - 3, -1, -1):
            psi_s[i] = mm(psi_s[i + 1], aown_s[i + 1])
        for i in range(NY - 1):
            psit_s[i * dim:(i + 1) * dim] = psi_s[i].T
            phit_s[:, i * dim:(i + 1) * dim] = phi0_s[i + 1].T
        for h in near_first:
            arrived(sin_s.at[h], sin_sem.at[h])
            s1_s[h] = mm(ab_s[h, 0], sin_s[h]) + ab_s[h, 1]
            remote(s1_s.at[h], sin_s.at[h], send_sem.at[28 + h], sin_sem.at[h], pair).start()

    gain = g_ref[...]
    gain_part = jnp.zeros((1, dim), F32)
    for h in range(heads):
        ol_s[h] = ol_s[h] + mm(r_s[h], sin_s[h])
    for h in range(heads):
        o = ol_s[h]
        inv_rms = lax.rsqrt(jnp.mean(o * o, axis=-1, keepdims=True) + EPS)
        normal = o * inv_rms
        grad = of_head(dof_s, h, tok)
        normal_s[h] = normal
        scaled = grad * gain
        adj_s[h] = inv_rms * (scaled - normal * jnp.mean(scaled * normal, axis=-1, keepdims=True))
    for h in range(heads):
        c_s[h] = mm(rt_s[h], adj_s[h])

    @pl.when(c == 1)
    def _():
        for h in near_first[::-1]:
            remote(c_s.at[h], cpair_s.at[h], send_sem.at[32 + h], cpair_sem.at[h], pair).start()

    for h in range(heads):
        gain_part = gain_part + jnp.sum(of_head(dof_s, h, tok) * normal_s[h], axis=0, keepdims=True)
    gpart_s[...] = jnp.broadcast_to(gain_part, (8, dim))
    me8 = y * NC + c
    n_g = 0
    gsends = []
    for d in range(1, NY * NC):
        to = (me8 + d) % (NY * NC)
        gsends.append(remote(
            gpart_s, grow_s.at[me8], gsend_sem.at[n_g], grow_sem.at[d - 1], dev(z, to // NC, to % NC)))
        gsends[-1].start()
        n_g += 1
    grow_s[me8] = gpart_s[...]

    def gain_along_z():
        for d in range(1, NY * NC):
            fr = (me8 + NY * NC - d) % (NY * NC)
            arrived(grow_s.at[fr], grow_sem.at[d - 1])
        gsum_s[0] = jnp.sum(grow_s[...], axis=0)
        for d in range(1, NZ):
            gz_copy(d).start()
        gz_s[z] = gsum_s[0]

    def gain_along_x():
        for d in range(1, NZ):
            arrived(gz_s.at[(z + NZ - d) % NZ], gz_sem.at[d - 1])
        gsum_s[1] = jnp.sum(gz_s[...], axis=0)
        for d in range(1, 4):
            gx_copy(d).start()
        gx_s[xpos] = gsum_s[1]

    def gz_copy(d):
        return remote(
            gsum_s.at[0], gz_s.at[z], gsend_sem.at[6 + d], gz_sem.at[d - 1], dev((z + d) % NZ, y, c)
        )

    def gx_copy(d):
        return remote(
            gsum_s.at[1], gx_s.at[xpos], gsend_sem.at[13 + d], gx_sem.at[d - 1], {"head": (xpos + d) % 4}
        )

    @pl.when(c == 0)
    def _():
        for h in near_first[::-1]:
            arrived(cpair_s.at[h], cpair_sem.at[h])
            cc_s[h] = mm(at_s[h], cpair_s[h]) + c_s[h]
            if h is near_first[0]:
                pltpu.make_async_copy(cc_s.at[h], cown_s.at[h], cown_sem.at[h]).start()
            else:
                remote(cc_s.at[h], cown_s.at[y], send_sem.at[32 + h], cown_sem.at[y], dev(z, h, 0)).start()
        for i in range(NY):
            arrived(cown_s.at[i], cown_sem.at[i])
        right = jnp.concatenate([cown_s[i] for i in range(1, NY)], axis=0)
        crow_s[...] = cown_s[0] + mm(phit_s[...], right)
        for dlt in range(NZ - 1, 0, -1):
            @pl.when(z >= dlt)
            def _():
                remote(
                    crow_s, zc_s.at[dlt - 1], send_sem.at[4 + dlt], zc_sem.at[dlt - 1], dev(z - dlt, y, 0)
                ).start()
        gam_s[NY - 2] = cown_s[NY - 1]
        for i in range(NY - 3, -1, -1):
            gam_s[i] = mm(aown_s[i + 1], gam_s[i + 1], 0, 0) + cown_s[i + 1]
        gain_along_z()
        fill_backward()
        for dlt in range(1, NZ - 1):
            @pl.when(z + dlt < NZ)
            def _():
                arrived(za_s.at[dlt - 1], za_sem.at[dlt - 1])

            theta_s[dlt] = za_s[0] if dlt == 1 else mm(za_s[dlt - 1], theta_s[dlt - 1])
            thetat_s[:, (dlt - 1) * dim:dlt * dim] = theta_s[dlt].T

        @pl.when(z + NZ - 1 < NZ)
        def _():
            arrived(za_s.at[NZ - 2], za_sem.at[NZ - 2])

        gain_along_x()
        for dlt in range(NZ - 1, 0, -1):
            @pl.when(z + dlt < NZ)
            def _():
                arrived(zc_s.at[dlt - 1], zc_sem.at[dlt - 1])
        right = jnp.concatenate([zc_s[i] for i in range(1, NZ - 1)], axis=0)
        d_row = zc_s[0] + mm(thetat_s[...], right)
        dsend_s[NY - 1] = d_row
        more = mm(psit_s[...], d_row)
        for i in range(NY - 1):
            dsend_s[i] = more[i * dim:(i + 1) * dim] + gam_s[i]
        for i in near_first[::-1]:
            remote(dsend_s.at[i], dout_s.at[y], send_sem.at[12 + i], dout_sem.at[y], dev(z, i, 1)).start()
        for h in range(heads):
            arrived(dout_s.at[h], dout_sem.at[h])

    @pl.when(c == 1)
    def _():
        gain_along_z()
        fill_backward()
        gain_along_x()
        for h in near_first:
            arrived(dout_s.at[h], dout_sem.at[h])
            d0_s[h] = mm(at_s[h], dout_s[h]) + c_s[h]
            remote(d0_s.at[h], dout_s.at[h], send_sem.at[36 + h], dout_sem.at[h], pair).start()

    lane = lax.broadcasted_iota(jnp.int32, (steps, heads), 1)
    db_all = jnp.zeros((steps, heads), F32)
    for h in range(heads):
        gm = g0_s[h] + mm(nk_s[h], dout_s[h])
        b = b_ref[:, h:h + 1]
        dv = b * gm
        dv_s[h] = dv
        dvf_s[pl.ds(h, steps, stride=heads), :] = dv
        db = jnp.sum(gm * p_s[h], axis=-1, keepdims=True) / b
        db_all = db_all + jnp.where(lane == h, db, 0.0)
    db_s[...] = db_all
    dv_ref[...] = dvf_s[...].astype(BF16)
    for h in range(heads):
        hm = jnp.where(col_i < row_i, mm(dv_s[h], p_s[h], 1, 1), 0.0)
        low_s[h] = hm + hm.T
    for h in range(heads):
        dk = dk1_s[h] + mm(
            jnp.concatenate([p_s[h], dv_s[h]], axis=1), jnp.concatenate([dout_s[h], -sin_s[h]], axis=1), 1, 1
        ) - mm(low_s[h], of_head(ku_s, h, steps))
        dk_s[pl.ds(h, steps, stride=heads), :] = dk
    db_ref[...] = jnp.concatenate([db_s[pl.ds(j, tok, stride=per), :] for j in range(per)], axis=1).T
    dk_ref[...] = unit_pullback(dk_s[...], ku_s[...], rk_s[...]).astype(BF16)

    for d in range(1, 4):
        arrived(gx_s.at[(xpos + 4 - d) % 4], gx_sem.at[d - 1])
    dg_ref[...] = jnp.sum(gx_s[...], axis=0)[0:1]

    for j in range(2):
        send["pair", j].wait_send()

        @pl.when(jnp.logical_not(own_here(j)))
        def _():
            own_copy(j, 0).wait_send()
            own_copy(j, 1).wait_send()

    def left(src, sem):
        remote(src, src, sem, sem, pair).wait_send()

    @pl.when(c == 1)
    def _():
        for part in range(2):
            zab_each(part, lambda copy: copy.wait_send())

        @pl.when((z == 0) | (z == NG - 1))
        def _():
            for n in range(2):
                middle_copy(n).wait_send()

        for dlt in range(1, NZ):
            @pl.when(z >= dlt)
            def _():
                left(phi_s.at[NY - 1], send_sem.at[12 + dlt])
        for i in range(1, NY):
            left(own_s.at[i, 0], send_sem.at[20 + i])
            left(phi_s.at[i - 1], send_sem.at[24 + i])
        for i in range(NY):
            left(sout_s.at[i], send_sem.at[28 + i])
            left(c_s.at[i], send_sem.at[32 + i])
            left(d0_s.at[i], send_sem.at[36 + i])

    @pl.when(c == 0)
    def _():
        for h in near_first:
            left(s1_s.at[h], send_sem.at[28 + h])
        for h in near_first[1:]:
            left(cc_s.at[h], send_sem.at[32 + h])
        for dlt in range(1, NZ):
            @pl.when(z >= dlt)
            def _():
                left(crow_s, send_sem.at[4 + dlt])
        for i in range(NY):
            left(dsend_s.at[i], send_sem.at[12 + i])
    for copy in gsends:
        copy.wait_send()
    for d in range(1, NZ):
        gz_copy(d).wait_send()
    for d in range(1, 4):
        gx_copy(d).wait_send()


def local(queries, keys, values, betas, gain, out_grad):
    tok, heads, dim = queries.shape
    per = keys.shape[1]
    steps = tok * per
    f = lambda *s: pltpu.VMEM(s, F32)
    dma = pltpu.SemaphoreType.DMA
    vmem = pl.BlockSpec(memory_space=pltpu.VMEM)
    b16 = lambda *sh: pltpu.VMEM(sh, BF16)
    scratch = [
        b16(tok * heads, dim), b16(steps * heads, dim), b16(steps * heads, dim), f(per * heads, tok), f(1, dim),
        b16(tok * heads, dim), f(steps, heads), f(steps, heads), dma((6,)),
        f(steps * heads, dim), f(tok * heads, dim), f(steps * heads, dim), f(tok * heads, dim),
        f(steps * heads, 1), f(tok * heads, 1), f(heads, steps, steps), f(heads, steps, steps),
        f(heads, steps, steps), f(heads, steps, dim), f(heads, steps, 2 * dim), f(heads, steps, tok),
        f(heads, tok, dim), f(heads, dim, tok), f(heads, tok, dim), f(heads, steps, dim), f(heads, tok, dim),
        f(heads, steps, dim), f(heads, steps, dim), f(tok * heads, dim), f(tok * heads, dim),
        f(steps * heads, dim), f(steps * heads, dim), f(heads, steps, dim),
        f(heads, 2, dim, dim), f(2, 2, dim, dim), f(2, 2, dim, dim), f(NY, 2, dim, dim),
        f(NY, dim, dim), f(NY, dim, dim), f(NG, 2, dim, dim), f(NZ - 1, dim, dim),
        f(NY, dim, dim), f(heads, dim, dim), f(heads, dim, dim),
        f(NY, dim, dim), f(NY, dim, dim), f(NZ - 1, dim, dim), f(NY - 1, dim, dim), f(heads, dim, dim),
        f(heads, dim, dim), f(heads, dim, dim), f(NY, dim, dim), f(dim, dim), f(NZ - 1, dim, dim),
        f(NY - 1, dim, dim), f(NY, dim, dim), f(heads, dim, dim), f(heads, dim, dim),
        f(8, dim), f(NY * NC, 8, dim), f(NZ, 8, dim), f(4, 8, dim), f(2, 8, dim),
        f(NY * dim, dim), f(dim, dim), f(dim, dim), f(dim, dim), dma,
        f(heads, dim, dim), f((NY - 1) * dim, dim), f(dim, (NY - 1) * dim), f(dim, (NZ - 2) * dim), f(heads, tok, dim),
        dma((48,)), dma((2,)), dma((2 * NY,)), dma((2 * NG,)), dma((NZ - 1,)), dma((heads,)), dma((2 * NY,)),
        dma((heads,)), dma((NY,)), dma((NZ - 1,)), dma((heads,)),
        dma((24,)), dma((NY * NC - 1,)), dma((NZ - 1,)), dma((3,)),
    ]
    outs = pl.pallas_call(
        kernel,
        out_shape=(
            jax.ShapeDtypeStruct((tok * heads, dim), BF16),
            jax.ShapeDtypeStruct((tok * heads, dim), BF16),
            jax.ShapeDtypeStruct((steps * heads, dim), BF16),
            jax.ShapeDtypeStruct((steps * heads, dim), BF16),
            jax.ShapeDtypeStruct((per * heads, tok), F32),
            jax.ShapeDtypeStruct((1, dim), F32),
        ),
        in_specs=[pl.BlockSpec(memory_space=pltpu.HBM)] * 6,
        out_specs=(vmem,) * 6,
        scratch_shapes=scratch,
        compiler_params=pltpu.CompilerParams(
            collective_id=0, has_side_effects=True, vmem_limit_bytes=32 * 1024 * 1024
        ),
        name="delta_product",
    )(*[
        pltpu.with_memory_space_constraint(a, pltpu.HBM)
        for a in (
            queries.reshape(tok * heads, dim),
            keys.reshape(steps * heads, dim),
            values.reshape(steps * heads, dim),
            betas.transpose(1, 2, 0).reshape(per * heads, tok),
            gain.reshape(1, dim),
            out_grad.reshape(tok * heads, dim),
        )
    ])
    out, dq, dk, dv, db, dg = pl.pallas_call(
        store,
        out_shape=tuple(jax.ShapeDtypeStruct(a.shape, a.dtype) for a in outs),
        in_specs=[vmem] * 6,
        out_specs=(pl.BlockSpec(memory_space=pl.ANY),) * 6,
        scratch_shapes=[dma((6,))],
        compiler_params=pltpu.CompilerParams(vmem_limit_bytes=4 * 1024 * 1024),
        name="store",
    )(*outs)
    return (
        out.reshape(queries.shape), dq.reshape(queries.shape), dk.reshape(keys.shape), dv.reshape(values.shape),
        db.reshape(per, heads, tok).transpose(2, 0, 1), dg.reshape(dim),
    )


def store(*refs):
    sem = refs[-1]
    copies = [pltpu.make_async_copy(refs[n], refs[6 + n], sem.at[n]) for n in range(6)]
    for copy in copies:
        copy.start()
    for copy in copies:
        copy.wait()


def solution(mesh):
    return jax.shard_map(
        local,
        mesh=mesh,
        in_specs=(
            P("seq", "head", None),
            P("seq", None, "head", None),
            P("seq", None, "head", None),
            P("seq", None, "head"),
            P(),
            P("seq", "head", None),
        ),
        out_specs=(
            P("seq", "head", None),
            P("seq", "head", None),
            P("seq", None, "head", None),
            P("seq", None, "head", None),
            P("seq", None, "head"),
            P(),
        ),
        check_vma=False,
    )
```
